32 devices in a mesh: dp: 4 (over y, core), fsdp: 8 (over z, x).
Axes of the slice: x: 2, y: 2, z: 4, core: 2. Of those that a mesh axis runs over, the one named last changes fastest.
Arguments:
- hidden_in: bfloat16 [20480, 768], P(('dp', 'fsdp')), may hold values from -7 to 7
- prev_logits: bfloat16 [32, 12, 640, 640], P(('dp', 'fsdp')), may hold values from -6 to 6
- segment_ids: int32 [32, 640], P(('dp', 'fsdp')), may hold values from 0 to 3, never falling along the last dimension, each value on 1 to 320 neighbouring positions
- d_hidden: bfloat16 [20480, 768], P(('dp', 'fsdp')), may hold values from -6 to 6
- d_logits: bfloat16 [32, 12, 640, 640], P(('dp', 'fsdp')), may hold values from -3 to 3
- weight_in: float32 [768, 5376], P(('dp', 'fsdp')), may hold values from -2.5 to 2.5
- weight_out: float32 [3840, 768], P(('dp', 'fsdp')), may hold values from -2 to 2
- vectors: float32 [12, 768], P(None, ('dp', 'fsdp')), may hold values from -0.6 to 1.45
- moment_in: float32 [768, 5376], P(('dp', 'fsdp')), may hold values from -0.55 to 0.55
- moment_out: float32 [3840, 768], P(('dp', 'fsdp')), may hold values from -0.55 to 0.55
- moment_vectors: float32 [12, 768], P(None, ('dp', 'fsdp')), may hold values from -1.5 to 1.5
- square_in: float32 [768, 5376], P(('dp', 'fsdp')), may hold values from 0.001 to 0.004
- square_out: float32 [3840, 768], P(('dp', 'fsdp')), may hold values from 0.001 to 0.004
- square_vectors: float32 [12, 768], P(None, ('dp', 'fsdp')), may hold values from 0.008 to 0.032
- step_count: int32 [1], replicated, may hold values from 1 to 20
Outputs:
- hidden_out: bfloat16 [20480, 768], P(('dp', 'fsdp'))
- logits: bfloat16 [32, 12, 640, 640], P(('dp', 'fsdp'))
- d_input: bfloat16 [20480, 768], P(('dp', 'fsdp'))
- d_prev: bfloat16 [32, 12, 640, 640], P(('dp', 'fsdp'))
- grad_weight_in: float32 [768, 5376], P(('dp', 'fsdp'))
- grad_weight_out: float32 [3840, 768], P(('dp', 'fsdp'))
- grad_vectors: float32 [12, 768], P(None, ('dp', 'fsdp'))
- new_moment_in: float32 [768, 5376], P(('dp', 'fsdp'))
- new_moment_out: float32 [3840, 768], P(('dp', 'fsdp'))
- new_moment_vectors: float32 [12, 768], P(None, ('dp', 'fsdp'))
- new_square_in: float32 [768, 5376], P(('dp', 'fsdp'))
- new_square_out: float32 [3840, 768], P(('dp', 'fsdp'))
- new_square_vectors: float32 [12, 768], P(None, ('dp', 'fsdp'))
- new_weight_in: float32 [768, 5376], P(('dp', 'fsdp'))
- new_weight_out: float32 [3840, 768], P(('dp', 'fsdp'))
- new_vectors: float32 [12, 768], P(None, ('dp', 'fsdp'))
- copy_weight_in: bfloat16 [768, 5376], P(('dp', 'fsdp'))
- copy_weight_out: bfloat16 [3840, 768], P(('dp', 'fsdp'))
- copy_vectors: bfloat16 [12, 768], P(None, ('dp', 'fsdp'))
- grad_norm: float32 [], replicated
The draws below stay inside these ranges and needn't reach their ends.
Inputs may be any that keep to these rules, and one draw needn't show every extreme that they name: `segment_ids`: along each row the segment numbers never fall; no segment holds more than 320 slots.
All inputs are finite; a program needn't handle non-finite values.
Results may differ from the reference program's by a relative error of at most 0.012.
Values may be sent and summed in bfloat16 or wider, within the bound.
A program may use at most 192 MiB of HBM per device.

```python
import math
import jax
import jax.numpy as jnp
import numpy as np
from jax import lax

D = 768
H = 12
HD = 64
FF = 3072
SEQ = 640
DOCS = 4
DOC_MOST = 320
SEQS = 32
TOKENS = 20480
VEC_ROWS = 12
PARAMS = 7087104


def draw_hidden_in(key, part):
    columns = jnp.arange(D, dtype=jnp.float32) / D
    spread = 3.0
    noise_part = jnp.clip(jax.random.normal(key, (TOKENS, D), jnp.float32), -4.0, 4.0)
    return (noise_part * jnp.power(spread, columns - 0.5)).astype(jnp.bfloat16)


def draw_weight_in(key, part):
    columns = jnp.arange(3 * D + FF)[None, :]
    value_columns = (columns >= 2 * D) & (columns < 3 * D)
    scaled = jnp.where(value_columns, 8.0 / math.sqrt(D), 1.0 / math.sqrt(D))
    noise_part = jnp.clip(jax.random.normal(key, (D, 3 * D + FF), jnp.float32), -4.0, 4.0)
    return noise_part * scaled


def draw_weight_out(key, part):
    upper_rows = jnp.arange(D + FF)[:, None] < D
    scaled = jnp.where(upper_rows, 1.0 / math.sqrt(D), 1.0 / math.sqrt(FF))
    noise_part = jnp.clip(jax.random.normal(key, (D + FF, D), jnp.float32), -4.0, 4.0)
    return noise_part * scaled


def draw_vectors(key, part):
    gain_rows = jnp.arange(VEC_ROWS)[:, None] < 2
    noise_part = jnp.clip(jax.random.normal(key, (VEC_ROWS, D), jnp.float32), -3.0, 3.0)
    return jnp.where(gain_rows, 1.0 + 0.15 * noise_part, 0.2 * noise_part)


def block_scale(own_key, shape, shards, low, top_value):
    level, own = 1.0, jax.random.fold_in(own_key, 6)
    for dim, blocks in shards:
        steps = jnp.exp(jax.random.uniform(jax.random.fold_in(own, dim), (blocks,), jnp.float32, low / len(shards), top_value / len(shards)))
        level = level * jnp.repeat(steps, shape[dim] // blocks).reshape([-1 if axis == dim else 1 for axis in range(len(shape))])
    return level


def length_profile(count, total, most, lean):
    loads = [(1 << 20) // math.isqrt(rank ** lean) + 1 for rank in range(2, count + 1)]
    rest, counts = total - most - (count - 1), [1] * (count - 1)
    while rest > 0:
        free = [i for i in range(count - 1) if counts[i] < most]
        mass, remaining = sum([loads[i] for i in free]), rest
        for i in free:
            more = min(most - counts[i], max(1, remaining * loads[i] // mass), rest)
            counts[i] = counts[i] + more
            rest = rest - more
    return np.array([most] + counts)


def uneven_parts(own_key, number_of, total, bound, skew):
    if number_of == 2:
        one = jax.random.randint(own_key, (), max(1, total - bound), min(bound, total - 1) + 1)
        return jnp.stack([one, total - one])
    sizes = jnp.asarray(length_profile(number_of, total, bound, skew), jnp.int32)
    couples = (number_of - 1) // 2
    donor, sink = sizes[1:1 + 2 * couples:2], sizes[2:2 + 2 * couples:2]
    room = jnp.minimum(donor - 1, bound - sink)
    passed = jax.random.randint(jax.random.fold_in(own_key, 1), (couples,), 0, 1 << 20) % (room + 1)
    sizes = sizes.at[1:1 + 2 * couples:2].set(donor - passed).at[2:2 + 2 * couples:2].set(sink + passed)
    return sizes[jax.random.permutation(jax.random.fold_in(own_key, 2), number_of)]


def scatter_about(key, extent, deviation, reach, pieces=(), kind=jnp.bfloat16):
    drawn = jax.random.normal(key, extent, jnp.float32) * deviation
    if len(pieces) > 0:
        drawn = block_scale(key, extent, pieces, -0.22, 0.18) * drawn
    return jnp.clip(drawn, min=-reach, max=reach).astype(kind)


def setup_inputs(seed: int = 0) -> dict:
    key_of = jax.random.split(jax.random.key(seed), 16)
    return {
        "hidden_in": draw_hidden_in(jax.random.fold_in(key_of[15], 71), 0),
        "prev_logits": scatter_about(key_of[1], (SEQS, H, SEQ, SEQ), 1.0, 6.0, ((0, 32),)),
        "segment_ids": jax.vmap(lambda own: jnp.searchsorted(jnp.cumsum(uneven_parts(own, DOCS, SEQ, DOC_MOST, 2)), jnp.arange(SEQ), side="right"))(jax.random.split(key_of[2], SEQS)).reshape((SEQS, SEQ)).astype(jnp.int32),
        "d_hidden": scatter_about(key_of[3], (TOKENS, D), 1.0, 6.0, ((0, 32),)),
        "d_logits": scatter_about(key_of[4], (SEQS, H, SEQ, SEQ), 0.5, 3.0, ((0, 32),)),
        "weight_in": draw_weight_in(jax.random.fold_in(key_of[15], 71), 0),
        "weight_out": draw_weight_out(jax.random.fold_in(key_of[15], 71), 0),
        "vectors": draw_vectors(jax.random.fold_in(key_of[15], 71), 0),
        "moment_in": scatter_about(key_of[8], (D, 3 * D + FF), 0.11, 0.55, ((0, 32),), jnp.float32),
        "moment_out": scatter_about(key_of[9], (D + FF, D), 0.11, 0.55, ((0, 32),), jnp.float32),
        "moment_vectors": scatter_about(key_of[10], (VEC_ROWS, D), 0.3, 1.5, ((1, 32),), jnp.float32),
        "square_in": jnp.clip(jnp.exp(math.log(0.004) - 1.3862944 * jax.random.uniform(key_of[11], (D, 3 * D + FF), jnp.float32) ** block_scale(key_of[11], (D, 3 * D + FF), ((0, 32),), -0.2, 0.2)), 0.001, 0.004),
        "square_out": jnp.clip(jnp.exp(math.log(0.004) - 1.3862944 * jax.random.uniform(key_of[12], (D + FF, D), jnp.float32) ** block_scale(key_of[12], (D + FF, D), ((0, 32),), -0.2, 0.2)), 0.001, 0.004),
        "square_vectors": jnp.clip(jnp.exp(math.log(0.032) - 1.3862944 * jax.random.uniform(key_of[13], (VEC_ROWS, D), jnp.float32) ** block_scale(key_of[13], (VEC_ROWS, D), ((1, 32),), -0.2, 0.2)), 0.008, 0.032),
        "step_count": jax.random.randint(key_of[14], (1,), 1, 21).astype(jnp.int32),
    }


norm_eps = 1e-12
clip_scale = 1.0
beta_one = 0.9
beta_two = 0.999
adam_eps = 1e-08
rate_matrix = 0.06
rate_vector = 0.25
decay_matrix = 0.01
masked_fill = -1e+30
highest = lax.Precision.HIGHEST

@jax.custom_vjp
def low(v):
    return lax.optimization_barrier(v.astype(jnp.bfloat16)).astype(jnp.float32)

@jax.custom_vjp
def low_back(v):
    return v

def low_keep(v):
    return (low(v), None)

def low_pass(kept, grad):
    return (grad,)

def back_keep(v):
    return (v, None)

def back_low(kept, grad):
    return (low(grad),)
low.defvjp(low_keep, low_pass)
low_back.defvjp(back_keep, back_low)

def norm_rows(residual, gain_row, shift_row):
    centered = residual - lax.optimization_barrier(jnp.mean(residual, axis=1, keepdims=True))
    scaling = lax.rsqrt(lax.optimization_barrier(jnp.mean(centered * centered, axis=1, keepdims=True)) + norm_eps)
    return centered * scaling * gain_row + shift_row

def layer(param_in, param_out, param_small, tokens, previous, same_doc):
    weight_in = low(param_in)
    weight_out = low(param_out)
    vector_rows = low(param_small)
    row_count = tokens.shape[0]
    projected = jnp.dot(tokens, weight_in[:, :3 * D], precision=highest)
    queries = low_back(low(projected[:, :D] + vector_rows[4]))
    keys_low = low_back(low(projected[:, D:2 * D]))
    values_low = low_back(low(projected[:, 2 * D:] + vector_rows[5]))
    head_queries = queries.reshape(row_count, H, HD)
    head_keys = keys_low.reshape(row_count, H, HD)
    head_values = values_low.reshape(row_count, H, HD)
    logits_raw = low_back(jnp.einsum('qhd,khd->hqk', head_queries, head_keys, precision=highest) * HD ** (-0.5) + previous)
    masked = jnp.where(same_doc[None], logits_raw, masked_fill)
    row_max = lax.optimization_barrier(jnp.max(masked, axis=2, keepdims=True))
    expo_terms = jnp.exp(masked - row_max)
    attn_probs = expo_terms / lax.optimization_barrier(jnp.sum(expo_terms, axis=2, keepdims=True))
    mixed_heads = jnp.einsum('hqk,khd->qhd', low(attn_probs), head_values, precision=highest)
    mixed_heads = low_back(low(mixed_heads.reshape(row_count, D)))
    first_sum = tokens + low_back(jnp.dot(mixed_heads, weight_out[:D], precision=highest) + vector_rows[6])
    hidden_one = norm_rows(first_sum, vector_rows[0], vector_rows[2])
    upward = low_back(jnp.dot(low(hidden_one), weight_in[:, 3 * D:], precision=highest) + vector_rows[8:].reshape(FF))
    activated = low(jax.nn.gelu(upward, approximate=False))
    second_sum = hidden_one + low_back(jnp.dot(activated, weight_out[D:], precision=highest) + vector_rows[7])
    output = norm_rows(second_sum, vector_rows[1], vector_rows[3])
    return (output, logits_raw)

def adam_update(master, moment, square, gradient, factor, step_value, step_rate, decay_rate):
    clipped = gradient * factor
    new_moment = beta_one * moment + (1.0 - beta_one) * clipped
    new_square = beta_two * square + (1.0 - beta_two) * clipped * clipped
    fixed_moment = new_moment / (1.0 - jnp.power(beta_one, step_value))
    fixed_square = new_square / (1.0 - jnp.power(beta_two, step_value))
    updated = master - step_rate * (fixed_moment / (jnp.sqrt(fixed_square) + adam_eps) + decay_rate * master)
    return (clipped, new_moment, new_square, updated)

def reference(hidden_in, prev_logits, segment_ids, d_hidden, d_logits, weight_in, weight_out, vectors, moment_in, moment_out, moment_vectors, square_in, square_out, square_vectors, step_count):
    token_rows = hidden_in.reshape(SEQS, SEQ, D)
    grad_rows = d_hidden.reshape(SEQS, SEQ, D)
    zero_sums = (jnp.zeros_like(weight_in), jnp.zeros_like(weight_out), jnp.zeros_like(vectors))

    def one_row(sums, items):
        row_tokens, row_prev, row_segments, row_grad, row_glogits = items
        same_doc = row_segments[:, None] == row_segments[None, :]

        def forward(param_in, param_out, param_small, tokens, previous):
            return layer(param_in, param_out, param_small, tokens, previous, same_doc)
        results, pull = jax.vjp(forward, weight_in, weight_out, vectors, row_tokens.astype(jnp.float32), row_prev.astype(jnp.float32))
        grad_in, grad_out, grad_small, grad_tokens, grad_prev = pull((row_grad.astype(jnp.float32), row_glogits.astype(jnp.float32)))
        new_sums = (sums[0] + grad_in, sums[1] + grad_out, sums[2] + grad_small)
        return (new_sums, (results[0].astype(jnp.bfloat16), results[1].astype(jnp.bfloat16), grad_tokens.astype(jnp.bfloat16), grad_prev.astype(jnp.bfloat16)))
    sums, rows_out = lax.scan(one_row, zero_sums, (token_rows, prev_logits, segment_ids, grad_rows, d_logits))
    raw_in, raw_out, raw_vectors = sums
    outputs, logits, grad_tokens, grad_prev = rows_out
    total_squares = jnp.sum(raw_in * raw_in) + jnp.sum(raw_out * raw_out) + jnp.sum(raw_vectors * raw_vectors)
    grad_norm = jnp.sqrt(total_squares)
    threshold = clip_scale * math.sqrt(PARAMS)
    factor = jnp.minimum(1.0, threshold / (grad_norm + 1e-06))
    step_value = step_count[0].astype(jnp.float32)
    clip_in, moment_one, square_one, updated_in = adam_update(weight_in, moment_in, square_in, raw_in, factor, step_value, rate_matrix, decay_matrix)
    clip_out, moment_two, square_two, updated_out = adam_update(weight_out, moment_out, square_out, raw_out, factor, step_value, rate_matrix, decay_matrix)
    clip_small, moment_three, square_three, updated_small = adam_update(vectors, moment_vectors, square_vectors, raw_vectors, factor, step_value, rate_vector, 0.0)
    return (outputs.reshape(TOKENS, D), logits, grad_tokens.reshape(TOKENS, D), grad_prev, clip_in, clip_out, clip_small, moment_one, moment_two, moment_three, square_one, square_two, square_three, updated_in, updated_out, updated_small, updated_in.astype(jnp.bfloat16), updated_out.astype(jnp.bfloat16), updated_small.astype(jnp.bfloat16), grad_norm)
```

```python
import functools
import math

import jax
import jax.numpy as jnp
from jax import lax
from jax.experimental import pallas as pl
from jax.experimental.pallas import tpu as pltpu
from jax.sharding import PartitionSpec as P

PARAMS = 7087104


norm_eps = 1e-12
clip_scale = 1.0
beta_one = 0.9
beta_two = 0.999
adam_eps = 1e-08
rate_matrix = 0.06
rate_vector = 0.25
decay_matrix = 0.01
NEG = -1e30
NT = (((1,), (1,)), ((), ()))
NN = (((1,), (0,)), ((), ()))
TN = (((0,), (0,)), ((), ()))
AXES = ("dp", "fsdp")


def gelu_exact(upward):
    return jax.nn.gelu(upward, approximate=False)


def norm_rows(residual, gain_row, shift_row):
    centered = residual - jnp.mean(residual, axis=1, keepdims=True)
    scaling = lax.rsqrt(jnp.mean(centered * centered, axis=1, keepdims=True) + norm_eps)
    normed = centered * scaling
    return (normed * gain_row + shift_row, normed, scaling)


def norm_back(grad_after, normed, scaling, gain_row):
    scaled_grad = grad_after * gain_row
    return scaling * (
        scaled_grad
        - jnp.mean(scaled_grad, axis=1, keepdims=True)
        - normed * jnp.mean(scaled_grad * normed, axis=1, keepdims=True)
    )


def dotf(a, b, dims):
    return lax.dot_general(a, b, dims, preferred_element_type=jnp.float32)

def half_masks(rows):
    lane = lax.broadcasted_iota(jnp.int32, (rows, 128), 1)
    return lane < 64

def attn_fwd_kernel(BR, q_ref, k_ref, v_ref, prev_ref, srow_ref, scol_ref, logits_ref, mixed_ref, lse_ref, mask_ref):
    g = pl.program_id(0)
    rows = q_ref.shape[0]
    @pl.when(g == 0)
    def _():
        mask_ref[...] = jnp.where(scol_ref[...] == srow_ref[...], 0.0, NEG)
        lse_ref[...] = jnp.zeros_like(lse_ref)
    k2 = k_ref[...]
    v2 = v_ref[...]
    left = half_masks(rows)
    zero = jnp.zeros_like(v2)
    va = jnp.where(left, v2, zero)
    vb = jnp.where(left, zero, v2)
    for rb in range(rows // BR):
        sl = pl.ds(rb * BR, BR)
        q2 = q_ref[sl, :] * jnp.bfloat16(0.125)
        lb = half_masks(BR)
        outs = []
        lses = []
        for h in range(2):
            qh = jnp.where(lb if h == 0 else ~lb, q2, jnp.zeros_like(q2))
            raw = dotf(qh, k2, NT) + prev_ref[h, sl, :].astype(jnp.float32)
            logits_ref[h, sl, :] = raw.astype(jnp.bfloat16)
            s = raw + mask_ref[sl, :]
            m = jnp.max(s, axis=1, keepdims=True)
            e = jnp.exp(s - m)
            tot = jnp.sum(e, axis=1, keepdims=True)
            o = dotf(e.astype(jnp.bfloat16), va if h == 0 else vb, NN)
            outs.append(o / tot)
            lses.append(m + jnp.log(tot))
        mixed_ref[sl, :] = (outs[0] + outs[1]).astype(jnp.bfloat16)
        lane = lax.broadcasted_iota(jnp.int32, (BR, 128), 1)
        cur = lse_ref[sl, :]
        cur = jnp.where(lane == 2 * g, lses[0], cur)
        cur = jnp.where(lane == 2 * g + 1, lses[1], cur)
        lse_ref[sl, :] = cur

def attn_fwd(qkv, prev, seg, BR=128):
    rows = qkv.shape[0]
    heads = prev.shape[0]
    G = heads // 2
    srow = seg.reshape(1, rows); scol = seg.reshape(rows, 1)
    return pl.pallas_call(
        functools.partial(attn_fwd_kernel, BR),
        grid=(G,),
        in_specs=[
            pl.BlockSpec((rows, 128), lambda g: (0, g)),
            pl.BlockSpec((rows, 128), lambda g: (0, G + g)),
            pl.BlockSpec((rows, 128), lambda g: (0, 2 * G + g)),
            pl.BlockSpec((2, rows, rows), lambda g: (g, 0, 0)),
            pl.BlockSpec((1, rows), lambda g: (0, 0)),
            pl.BlockSpec((rows, 1), lambda g: (0, 0)),
        ],
        out_specs=[
            pl.BlockSpec((2, rows, rows), lambda g: (g, 0, 0)),
            pl.BlockSpec((rows, 128), lambda g: (0, g)),
            pl.BlockSpec((rows, 128), lambda g: (0, 0)),
        ],
        out_shape=[
            jax.ShapeDtypeStruct((heads, rows, rows), jnp.bfloat16),
            jax.ShapeDtypeStruct((rows, heads * 64), jnp.bfloat16),
            jax.ShapeDtypeStruct((rows, 128), jnp.float32),
        ],
        scratch_shapes=[pltpu.VMEM((rows, rows), jnp.float32)],
        compiler_params=pltpu.CompilerParams(vmem_limit_bytes=60 * 2**20),
        name="attn_fwd",
    )(qkv, qkv, qkv, prev, srow, scol)

def attn_bwd_kernel(BR, q_ref, k_ref, v_ref, do_ref, prev_ref, dl_ref, lse_ref, srow_ref, scol_ref,
                    dprev_ref, dq_ref, dk_ref, dv_ref, mask_ref, p_ref, g_ref):
    g = pl.program_id(0)
    rows = q_ref.shape[0]
    @pl.when(g == 0)
    def _():
        mask_ref[...] = jnp.where(scol_ref[...] == srow_ref[...], 0.0, NEG)
    k2 = k_ref[...]
    v2 = v_ref[...]
    left = half_masks(rows)
    zero = jnp.zeros_like(v2)
    for h in range(2):
        lm = left if h == 0 else ~left
        kh = jnp.where(lm, k2, zero)
        for rb in range(rows // BR):
            sl = pl.ds(rb * BR, BR)
            lb = half_masks(BR)
            lb = lb if h == 0 else ~lb
            q2 = q_ref[sl, :] * jnp.bfloat16(0.125)
            qh = jnp.where(lb, q2, jnp.zeros_like(q2))
            doh = jnp.where(lb, do_ref[sl, :], jnp.zeros_like(q2))
            lane = lax.broadcasted_iota(jnp.int32, (BR, 128), 1)
            lse = jnp.sum(jnp.where(lane == 2 * g + h, lse_ref[sl, :], 0.0), axis=1, keepdims=True)
            s = dotf(qh, k2, NT) + prev_ref[h, sl, :].astype(jnp.float32) + mask_ref[sl, :]
            p = jnp.exp(s - lse)
            dp = dotf(doh, v2, NT)
            delta = jnp.sum(p * dp, axis=1, keepdims=True)
            ds = p * (dp - delta)
            gt = (ds + dl_ref[h, sl, :].astype(jnp.float32)).astype(jnp.bfloat16)
            dprev_ref[h, sl, :] = gt
            p_ref[sl, :] = p.astype(jnp.bfloat16)
            dq = dotf(gt, kh, NN) * 0.125
            if h == 0:
                dq_ref[sl, :] = dq.astype(jnp.bfloat16)
            else:
                dq_ref[sl, :] = dq_ref[sl, :] + dq.astype(jnp.bfloat16)
        qh = jnp.where(lm, q_ref[...], zero)
        doh = jnp.where(lm, do_ref[...], zero)
        dk = (dotf(dprev_ref[h], qh, TN) * 0.125).astype(jnp.bfloat16)
        dv = dotf(p_ref[...], doh, TN).astype(jnp.bfloat16)
        if h == 0:
            dk_ref[...] = dk
            dv_ref[...] = dv
        else:
            dk_ref[...] = dk_ref[...] + dk
            dv_ref[...] = dv_ref[...] + dv

def attn_bwd(qkv, do, prev, dl, lse, seg, BR=128):
    rows = qkv.shape[0]
    heads = prev.shape[0]
    G = heads // 2
    srow = seg.reshape(1, rows); scol = seg.reshape(rows, 1)
    col = lambda off: pl.BlockSpec((rows, 128), lambda g: (0, off + g))
    return pl.pallas_call(
        functools.partial(attn_bwd_kernel, BR),
        grid=(G,),
        in_specs=[
            col(0), col(G), col(2 * G), col(0),
            pl.BlockSpec((2, rows, rows), lambda g: (g, 0, 0)),
            pl.BlockSpec((2, rows, rows), lambda g: (g, 0, 0)),
            pl.BlockSpec((rows, 128), lambda g: (0, 0)),
            pl.BlockSpec((1, rows), lambda g: (0, 0)),
            pl.BlockSpec((rows, 1), lambda g: (0, 0)),
        ],
        out_specs=[
            pl.BlockSpec((2, rows, rows), lambda g: (g, 0, 0)),
            col(0), col(0), col(0),
        ],
        out_shape=[
            jax.ShapeDtypeStruct((heads, rows, rows), jnp.bfloat16),
        ] + [jax.ShapeDtypeStruct((rows, heads * 64), jnp.bfloat16)] * 3,
        scratch_shapes=[pltpu.VMEM((rows, rows), jnp.float32), pltpu.VMEM((rows, rows), jnp.bfloat16), pltpu.VMEM((8, 128), jnp.float32)],
        compiler_params=pltpu.CompilerParams(vmem_limit_bytes=60 * 2**20),
        name="attn_bwd",
    )(qkv, qkv, qkv, do, prev, dl, lse, srow, scol)


MESH = pl.DeviceIdType.MESH

def coords():
    dp = lax.axis_index("dp"); fs = lax.axis_index("fsdp")
    y = dp // 2; c = lax.rem(dp, 2)
    z = fs // 2; x = lax.rem(fs, 2)
    return y, c, z, x

def dev(y, c, z, x):
    return (y * 2 + c, z * 2 + x)

def ag_kernel(chunks, *refs):
    n_arr = max(a for a, _, _ in chunks) + 1
    ins = refs[:n_arr]
    outs = refs[n_arr:2 * n_arr]
    rest = refs[2 * n_arr:]
    bufs = rest[:n_arr]
    send_sem, recv_sem, loc_sem = rest[n_arr:]
    y, c, z, x = coords()
    peers = [dev(y, c, lax.rem(z + d, 4), x) for d in (1, 2, 3)] + [dev(y, c, z, 1 - x), dev(1 - y, c, z, x), dev(y, 1 - c, z, x)]
    barrier = pltpu.get_barrier_semaphore()
    for p in peers:
        pl.semaphore_signal(barrier, inc=1, device_id=p, device_id_type=MESH)
    load = [pltpu.make_async_copy(ins[a], bufs[a], loc_sem.at[0, a]) for a in range(n_arr)]
    for l in load: l.start()
    for l in load: l.wait()
    store = [pltpu.make_async_copy(bufs[a], outs[a].at[y, c, z, x], loc_sem.at[1, a]) for a in range(n_arr)]
    for s in store: s.start()
    pl.semaphore_wait(barrier, len(peers))

    def remote(src, dst, k, slot, who):
        return pltpu.make_async_remote_copy(src_ref=src, dst_ref=dst, send_sem=send_sem.at[k, slot], recv_sem=recv_sem.at[k, slot], device_id=who, device_id_type=MESH)
    zc, ac, b2, cc = [], [], [], []
    for k, (a, s, n) in enumerate(chunks):
        cols = pl.ds(s, n)
        zc.append([remote(bufs[a].at[:, cols], outs[a].at[y, c, z, x, :, cols], k, d, peers[d]) for d in range(3)])
        mine = outs[a].at[y, c, :, x, :, cols]
        ac.append([remote(mine, mine, k, 3 + i, peers[3 + i]) for i in range(2)])
    for k in range(len(chunks)):
        for d in zc[k]: d.start()
    for s in store: s.wait()
    nc = len(chunks)
    for t in range(nc + 2):
        if t < nc:
            for d in zc[t]: d.wait_recv()
            for d in ac[t]: d.start()
        k = t - 1
        if 0 <= k < nc:
            a, s, n = chunks[k]
            cols = pl.ds(s, n)
            ry = jnp.where(c == 0, y, 1 - y); rx = jnp.where(c == 0, 1 - x, x)
            blk = outs[a].at[ry, c, :, rx, :, cols]
            got = remote(blk, blk, k, 3 + c, peers[3])
            got.wait_recv()
            td = jnp.where(c == 0, (1 - y) * 2 + c, y * 2 + c); tf = jnp.where(c == 0, z * 2 + x, z * 2 + 1 - x)
            r = remote(blk, blk, k, 5, (td, tf))
            r.start()
            b2.append(r)
        k = t - 2
        if 0 <= k < nc:
            a, s, n = chunks[k]
            cols = pl.ds(s, n)
            b2[k].wait_recv()
            blk = outs[a].at[y, c, :, x, :, cols]
            remote(blk, blk, k, 4 - c, peers[3]).wait_recv()
            pln = outs[a].at[:, c, :, :, :, cols]
            r = remote(pln, pln, k, 6, peers[5])
            r.start()
            cc.append(r)
    for k in range(nc):
        cc[k].wait_recv()
    for k in range(nc):
        for d in zc[k] + ac[k] + [b2[k], cc[k]]: d.wait_send()

def gather(arrs, chunks):
    na = len(arrs)
    return pl.pallas_call(
        functools.partial(ag_kernel, chunks),
        in_specs=[pl.BlockSpec(memory_space=pl.ANY)] * na,
        out_specs=[pl.BlockSpec(memory_space=pl.ANY)] * na,
        out_shape=[jax.ShapeDtypeStruct((2, 2, 4, 2) + a.shape, a.dtype) for a in arrs],
        scratch_shapes=[pltpu.VMEM(a.shape, a.dtype) for a in arrs] + [
            pltpu.SemaphoreType.DMA((len(chunks), 7)), pltpu.SemaphoreType.DMA((len(chunks), 7)), pltpu.SemaphoreType.DMA((2, na))],
        compiler_params=pltpu.CompilerParams(collective_id=1, has_side_effects=True, vmem_limit_bytes=40 * 2**20),
        name="gather",
    )(*arrs)


def rs_kernel(chunks, n_arr, n_out, *refs):
    ins = refs[:n_arr]; vec_in = refs[n_arr]
    outs = refs[n_arr + 1:n_arr + 1 + n_out]
    vec_out, norm_out = refs[n_arr + 1 + n_out:n_arr + 3 + n_out]
    rest = refs[n_arr + 3 + n_out:]
    nc = len(chunks)
    own, r1, r2, r3, rz = [rest[i * nc:(i + 1) * nc] for i in range(5)]
    vrecv, nmine, nrecv, send_sem, recv_sem, loc_sem, vs_sem, vr_sem, ns_sem, nr_sem = rest[5 * nc:]
    y, c, z, x = coords()
    px, py, pc = dev(y, c, z, 1 - x), dev(1 - y, c, z, x), dev(y, 1 - c, z, x)
    pz = [dev(y, c, lax.rem(z + d, 4), x) for d in (1, 2, 3)]
    peers = pz + [px, py, pc]
    barrier = pltpu.get_barrier_semaphore()
    for p in peers:
        pl.semaphore_signal(barrier, inc=1, device_id=p, device_id_type=MESH)
    n1 = (jnp.where(c == 0, (1 - y) * 2 + c, y * 2 + c), jnp.where(c == 0, z * 2 + x, z * 2 + 1 - x))
    n2 = (jnp.where(c == 0, y * 2 + c, (1 - y) * 2 + c), jnp.where(c == 0, z * 2 + 1 - x, z * 2 + x))
    b1 = (jnp.where(c == 0, 1 - y, y), jnp.where(c == 0, x, 1 - x))
    b2 = (jnp.where(c == 0, y, 1 - y), jnp.where(c == 0, 1 - x, x))
    bd = (1 - y, 1 - x)
    me = (y, x)

    def remote(src, dst, k, slot, who):
        return pltpu.make_async_remote_copy(src_ref=src, dst_ref=dst, send_sem=send_sem.at[k, slot], recv_sem=recv_sem.at[k, slot], device_id=who, device_id_type=MESH)
    loads = []
    for k, (a, s, n, oa, os) in enumerate(chunks):
        l = pltpu.make_async_copy(ins[a].at[:, c, :, :, :, :, pl.ds(s, n)], own[k], loc_sem.at[k])
        l.start(); loads.append(l)
    pl.semaphore_wait(barrier, len(peers))
    pend = []
    cs = []
    for k, (a, s, n, oa, os) in enumerate(chunks):
        d = remote(ins[a].at[:, 1 - c, :, :, :, :, pl.ds(s, n)], r1[k], k, 0, pc)
        d.start(); cs.append(d)
    acc = vec_in[...]
    vsend = vrecv
    for i, who in enumerate((pc, py, px)):
        vrecv[6 + i] = acc
        d = pltpu.make_async_remote_copy(src_ref=vrecv.at[6 + i], dst_ref=vrecv.at[i], send_sem=vs_sem.at[i], recv_sem=vr_sem.at[i], device_id=who, device_id_type=MESH)
        d.start(); d.wait_recv(); pend.append(d)
        acc = acc + vrecv[i]
    vrecv[9] = acc
    vz = []
    for i in range(3):
        d = pltpu.make_async_remote_copy(src_ref=vrecv.at[9], dst_ref=vrecv.at[3 + i], send_sem=vs_sem.at[3 + i], recv_sem=vr_sem.at[3 + i], device_id=pz[i], device_id_type=MESH)
        d.start(); vz.append(d); pend.append(d)

    s1, s2, sz = {}, {}, {}
    fl = lambda ref, b: ref.at[b[0], :, b[1]]
    for t in range(nc + 3):
        k = t
        if k < nc:
            loads[k].wait(); cs[k].wait_recv()
            for yy in range(2):
                for zz in range(4):
                    for xx in range(2):
                        own[k][yy, zz, xx] = (own[k][yy, zz, xx].astype(jnp.float32) + r1[k][yy, zz, xx].astype(jnp.float32)).astype(jnp.bfloat16)
            d1 = remote(own[k].at[bd[0], :, bd[1]], r2[k].at[0], k, 1, n1)
            d2 = remote(own[k].at[b1[0], :, b1[1]], r2[k].at[1], k, 2, n1)
            d1.start(); d2.start(); s1[k] = (d1, d2)
        k = t - 1
        if 0 <= k < nc:
            for d in s1[k]: d.wait_recv()
            for zz in range(4):
                own[k][b2[0], zz, b2[1]] = (own[k][b2[0], zz, b2[1]].astype(jnp.float32) + r2[k][0, zz].astype(jnp.float32)).astype(jnp.bfloat16)
            d = remote(own[k].at[b2[0], :, b2[1]], r3[k], k, 3, n2)
            d.start(); s2[k] = d
        k = t - 2
        if 0 <= k < nc:
            s2[k].wait_recv()
            for zz in range(4):
                own[k][y, zz, x] = (own[k][y, zz, x].astype(jnp.float32) + r2[k][1, zz].astype(jnp.float32) + r3[k][zz].astype(jnp.float32)).astype(jnp.bfloat16)
            sz[k] = []
            for i in range(3):
                zt = lax.rem(z + i + 1, 4)
                d = remote(own[k].at[y, zt, x], rz[k].at[i], k, 4 + i, pz[i])
                d.start(); sz[k].append(d)
        k = t - 3
        if 0 <= k < nc:
            a, s, n, oa, os = chunks[k]
            for d in sz[k]: d.wait_recv()
            tot = own[k][y, z, x].astype(jnp.float32)
            for i in range(3): tot = tot + rz[k][i].astype(jnp.float32)
            outs[oa][:, :, pl.ds(os, n)] = tot
    for d in vz: d.wait_recv()
    vals = [acc] + [vrecv[3 + i] for i in range(3)]
    tot = jnp.zeros_like(acc)
    for zz in range(4):
        pick = vals[0]
        for i in range(1, 4):
            pick = jnp.where(lax.rem(z - i + 4, 4) == zz, vals[i], pick)
        tot = tot + pick
    vec_out[...] = tot
    sq = jnp.zeros((8, 128), jnp.float32)
    for a in range(n_out):
        v = outs[a][...]
        v = v * v
        p = jnp.sum(v, axis=(0))
        for j in range(p.shape[1] // 128):
            sq = sq + p[:, j * 128:(j + 1) * 128]
    part = jnp.sum(sq, keepdims=True) + jnp.zeros((8, 128), jnp.float32)
    for i, who in enumerate((pc, py, px)):
        nmine[i] = part
        d = pltpu.make_async_remote_copy(src_ref=nmine.at[i], dst_ref=nrecv.at[i], send_sem=ns_sem.at[i], recv_sem=nr_sem.at[i], device_id=who, device_id_type=MESH)
        d.start(); d.wait_recv(); pend.append(d)
        part = part + nrecv[i]
    nmine[3] = part
    nz = []
    for i in range(3):
        d = pltpu.make_async_remote_copy(src_ref=nmine.at[3], dst_ref=nrecv.at[3 + i], send_sem=ns_sem.at[3 + i], recv_sem=nr_sem.at[3 + i], device_id=pz[i], device_id_type=MESH)
        d.start(); nz.append(d); pend.append(d)
    for d in nz: d.wait_recv()
    vals = [part] + [nrecv[3 + i] for i in range(3)]
    tot = jnp.sum(vec_out[...] * vec_out[...]) + jnp.zeros((8, 128), jnp.float32)
    for zz in range(4):
        pick = vals[0]
        for i in range(1, 4):
            pick = jnp.where(lax.rem(z - i + 4, 4) == zz, vals[i], pick)
        tot = tot + pick
    norm_out[...] = jnp.sqrt(tot)
    for k in range(nc):
        for d in [cs[k]] + list(s1[k]) + [s2[k]] + sz[k]: d.wait_send()
    for d in pend: d.wait_send()

def scatter(arrs, vec, chunks, out_shapes):
    na = len(arrs)
    bufs = []
    for lead in ((2, 4, 2), (2, 4, 2), (2, 4), (4,), (3,)):
        for a, s, n, oa, os in chunks:
            bufs.append(pltpu.VMEM(lead + (arrs[a].shape[4], 8, n), jnp.bfloat16))
    nc = len(chunks)
    return pl.pallas_call(
        functools.partial(rs_kernel, chunks, na, len(out_shapes)),
        in_specs=[pl.BlockSpec(memory_space=pl.ANY)] * na + [pl.BlockSpec(memory_space=pltpu.VMEM)],
        out_specs=[pl.BlockSpec(memory_space=pltpu.VMEM)] * (len(out_shapes) + 2),
        out_shape=[jax.ShapeDtypeStruct(s, jnp.float32) for s in out_shapes] + [jax.ShapeDtypeStruct(vec.shape, jnp.float32), jax.ShapeDtypeStruct((8, 128), jnp.float32)],
        scratch_shapes=bufs + [
            pltpu.VMEM((10,) + vec.shape, jnp.float32), pltpu.VMEM((4, 8, 128), jnp.float32), pltpu.VMEM((6, 8, 128), jnp.float32),
            pltpu.SemaphoreType.DMA((nc, 7)), pltpu.SemaphoreType.DMA((nc, 7)), pltpu.SemaphoreType.DMA((nc,)),
            pltpu.SemaphoreType.DMA((6,)), pltpu.SemaphoreType.DMA((6,)), pltpu.SemaphoreType.DMA((6,)), pltpu.SemaphoreType.DMA((6,))],
        compiler_params=pltpu.CompilerParams(collective_id=2, has_side_effects=True, vmem_limit_bytes=60 * 2**20),
        name="scatter_sum",
    )(*arrs, vec)


def adam_update(master, moment, square, gradient, factor, step_value, step_rate, decay_rate):
    clipped = gradient * factor
    new_moment = beta_one * moment + (1.0 - beta_one) * clipped
    new_square = beta_two * square + (1.0 - beta_two) * clipped * clipped
    fixed_moment = new_moment / (1.0 - jnp.power(beta_one, step_value))
    fixed_square = new_square / (1.0 - jnp.power(beta_two, step_value))
    updated = master - step_rate * (
        fixed_moment / (jnp.sqrt(fixed_square) + adam_eps) + decay_rate * master
    )
    return (clipped, new_moment, new_square, updated)


def rounded(v):
    return lax.reduce_precision(v, 8, 7)


def gather_all(remote, weight_in, weight_out, vectors, width):
    low_qkv = weight_in[:, : 3 * width].astype(jnp.bfloat16)
    low_up = weight_in[:, 3 * width :].astype(jnp.bfloat16)
    low_out = weight_out.astype(jnp.bfloat16)
    low_small = rounded(vectors)
    if not remote:
        whole = lambda v: lax.all_gather(v, AXES, axis=0, tiled=True)
        return whole(low_qkv), whole(low_up), whole(low_out), lax.all_gather(low_small, AXES, axis=1, tiled=True)
    rows, cols = vectors.shape
    padded = jnp.pad(low_small, ((0, 16 - rows), (0, 128 - cols)))
    chunks = [(3, 0, 128)] + [(0, 768 * i, 768) for i in range(3)] + [(1, 768 * i, 768) for i in range(4)] + [(2, 256 * i, 256) for i in range(3)]
    full_qkv, full_up, full_out, small = gather([low_qkv, low_up, low_out, padded], chunks)
    small = small.reshape(-1, 16, 128)[:, :rows, :cols].transpose(1, 0, 2).reshape(rows, -1)
    return full_qkv.reshape(-1, 3 * width), full_up.reshape(width, -1), full_out.reshape(-1, width), small


def reduce_all(remote, grad_qkv, grad_up, grad_out, small, shards):
    rows_in, rows_out = grad_qkv.shape[0] // shards, grad_out.shape[0] // shards
    if not remote:
        part = lambda v: lax.psum_scatter(v, AXES, scatter_dimension=0, tiled=True).astype(jnp.float32)
        owned_in = jnp.concatenate([part(grad_qkv), part(grad_up)], axis=1)
        owned_out = part(grad_out)
        owned_small = lax.psum_scatter(small, AXES, scatter_dimension=1, tiled=True)
        total = lax.psum(jnp.sum(owned_in**2) + jnp.sum(owned_out**2) + jnp.sum(owned_small**2), AXES)
        return owned_in, owned_out, owned_small, jnp.sqrt(total)
    q, u = grad_qkv.shape[1], grad_up.shape[1]
    chunks = [(2, 256 * i, 256, 1, 256 * i) for i in range(3)] + [(1, 768 * i, 768, 0, q + 768 * i) for i in range(4)] + [(0, 768 * i, 768, 0, 768 * i) for i in range(3)]
    split = lambda v, r: v.reshape(2, 2, 4, 2, r // 8, 8, v.shape[1])
    padded = jnp.pad(small, ((0, 16 - small.shape[0]), (0, 0)))
    owned_in, owned_out, total_small, norm = scatter(
        [split(grad_qkv, rows_in), split(grad_up, rows_in), split(grad_out, rows_out)], padded, chunks,
        [(rows_in // 8, 8, q + u), (rows_out // 8, 8, grad_out.shape[1])])
    me = lax.axis_index("dp") * lax.axis_size("fsdp") + lax.axis_index("fsdp")
    columns = small.shape[1] // shards
    owned_small = lax.dynamic_slice(total_small[: small.shape[0]], (0, me * columns), (small.shape[0], columns))
    return owned_in.reshape(rows_in, -1), owned_out.reshape(rows_out, -1), owned_small, norm[0, 0]


def body(remote, hidden_in, prev_logits, segment_ids, d_hidden, d_logits, weight_in, weight_out, vectors,
         moment_in, moment_out, moment_vectors, square_in, square_out, square_vectors, step_count):
    width = weight_out.shape[1]
    shards = lax.axis_size("dp") * lax.axis_size("fsdp")
    full_qkv, full_up, full_out, small = gather_all(remote, weight_in, weight_out, vectors, width)
    w_attn, w_down = full_out[:width], full_out[width:]
    dot = lambda spec, a, b: jnp.einsum(spec, a, b, preferred_element_type=jnp.float32)
    sums = lambda v: jnp.sum(v, axis=0, dtype=jnp.float32)

    offsets = jnp.concatenate([small[4], jnp.zeros_like(small[4]), small[5]])
    qkv = (dot("td,dc->tc", hidden_in, full_qkv) + offsets).astype(jnp.bfloat16)
    segments = segment_ids[0]
    logits, mixed, log_sums = attn_fwd(qkv, prev_logits[0], segments, 640)
    first = hidden_in.astype(jnp.float32) + (dot("tc,cd->td", mixed, w_attn) + small[6])
    hidden_one, normed_one, scale_one = norm_rows(first, small[0], small[2])
    hidden_low = hidden_one.astype(jnp.bfloat16)
    upward = dot("td,df->tf", hidden_low, full_up) + small[8:].reshape(-1)
    activated, gelu_pull = jax.vjp(gelu_exact, upward)
    activated = activated.astype(jnp.bfloat16)
    second = hidden_one + (dot("tf,fd->td", activated, w_down) + small[7])
    output, normed_two, scale_two = norm_rows(second, small[1], small[3])

    grad_output = d_hidden.astype(jnp.float32)
    grad_second = norm_back(grad_output, normed_two, scale_two, small[1])
    grad_down = grad_second.astype(jnp.bfloat16)
    down_grad = dot("tf,td->fd", activated, grad_down).astype(jnp.bfloat16)
    grad_up = gelu_pull(dot("td,fd->tf", grad_down, w_down))[0].astype(jnp.bfloat16)
    up_grad = dot("td,tf->df", hidden_low, grad_up).astype(jnp.bfloat16)
    grad_one = grad_second + dot("tf,df->td", grad_up, full_up)
    grad_first = norm_back(grad_one, normed_one, scale_one, small[0])
    grad_attn = grad_first.astype(jnp.bfloat16)
    attn_grad = dot("tc,td->cd", mixed, grad_attn).astype(jnp.bfloat16)
    grad_mixed = dot("td,cd->tc", grad_attn, w_attn).astype(jnp.bfloat16)
    grad_prev, grad_q, grad_k, grad_v = attn_bwd(qkv, grad_mixed, prev_logits[0], d_logits[0], log_sums, segments, 640)
    grad_qkv = jnp.concatenate([grad_q, grad_k, grad_v], axis=1)
    qkv_grad = dot("td,tc->dc", hidden_in, grad_qkv).astype(jnp.bfloat16)
    grad_tokens = grad_first + dot("tc,dc->td", grad_qkv, full_qkv)
    small_grad = jnp.concatenate([
        jnp.stack([sums(grad_one * normed_one), sums(grad_output * normed_two), sums(grad_one), sums(grad_output),
                   sums(grad_q), sums(grad_v), sums(grad_attn), sums(grad_down)]),
        sums(grad_up).reshape(-1, width)], axis=0)

    owned_in, owned_out, owned_small, grad_norm = reduce_all(
        remote, qkv_grad, up_grad, jnp.concatenate([attn_grad, down_grad], axis=0), small_grad, shards)
    factor = jnp.minimum(1.0, clip_scale * math.sqrt(PARAMS) / (grad_norm + 1e-06))
    step_value = step_count[0].astype(jnp.float32)
    new = [
        adam_update(weight_in, moment_in, square_in, owned_in, factor, step_value, rate_matrix, decay_matrix),
        adam_update(weight_out, moment_out, square_out, owned_out, factor, step_value, rate_matrix, decay_matrix),
        adam_update(vectors, moment_vectors, square_vectors, owned_small, factor, step_value, rate_vector, 0.0),
    ]
    clipped, moments, squares, updated = zip(*new)
    return (output.astype(jnp.bfloat16), logits[None], grad_tokens.astype(jnp.bfloat16), grad_prev[None],
            *clipped, *moments, *squares, *updated, *[u.astype(jnp.bfloat16) for u in updated], grad_norm)


def solution(mesh):
    remote = (mesh.shape["dp"], mesh.shape["fsdp"]) == (4, 8)
    rows = P(AXES, None)
    heads = P(AXES, None, None, None)
    cols = P(None, AXES)
    trio = (rows, rows, cols)
    return jax.shard_map(
        functools.partial(body, remote),
        mesh=mesh,
        in_specs=(rows, heads, rows, rows, heads, *trio, *trio, *trio, P()),
        out_specs=(rows, heads, rows, heads, *trio, *trio, *trio, *trio, *trio, P()),
        check_vma=False,
    )
```

```python
import functools
import math

import jax
import jax.numpy as jnp
from jax import lax
from jax.experimental import pallas as pl
from jax.experimental.pallas import tpu as pltpu
from jax.sharding import PartitionSpec as P

PARAMS = 7087104


norm_eps = 1e-12
clip_scale = 1.0
beta_one = 0.9
beta_two = 0.999
adam_eps = 1e-08
rate_matrix = 0.06
rate_vector = 0.25
decay_matrix = 0.01
NEG = -1e30
NT = (((1,), (1,)), ((), ()))
NN = (((1,), (0,)), ((), ()))
TN = (((0,), (0,)), ((), ()))
AXES = ("dp", "fsdp")


def gelu_exact(upward):
    return jax.nn.gelu(upward, approximate=False)


def norm_rows(residual, gain_row, shift_row):
    centered = residual - jnp.mean(residual, axis=1, keepdims=True)
    scaling = lax.rsqrt(jnp.mean(centered * centered, axis=1, keepdims=True) + norm_eps)
    normed = centered * scaling
    return (normed * gain_row + shift_row, normed, scaling)


def norm_back(grad_after, normed, scaling, gain_row):
    scaled_grad = grad_after * gain_row
    return scaling * (
        scaled_grad
        - jnp.mean(scaled_grad, axis=1, keepdims=True)
        - normed * jnp.mean(scaled_grad * normed, axis=1, keepdims=True)
    )


def dotf(a, b, dims):
    return lax.dot_general(a, b, dims, preferred_element_type=jnp.float32)

def half_masks(rows):
    lane = lax.broadcasted_iota(jnp.int32, (rows, 128), 1)
    return lane < 64

def attn_fwd_kernel(BR, q_ref, k_ref, v_ref, prev_ref, srow_ref, scol_ref, logits_ref, mixed_ref, lse_ref, mask_ref):
    g = pl.program_id(0)
    rows = q_ref.shape[0]
    @pl.when(g == 0)
    def _():
        mask_ref[...] = jnp.where(scol_ref[...] == srow_ref[...], 0.0, NEG)
        lse_ref[...] = jnp.zeros_like(lse_ref)
    k2 = k_ref[...]
    v2 = v_ref[...]
    left = half_masks(rows)
    zero = jnp.zeros_like(v2)
    va = jnp.where(left, v2, zero)
    vb = jnp.where(left, zero, v2)
    for rb in range(rows // BR):
        sl = pl.ds(rb * BR, BR)
        q2 = q_ref[sl, :] * jnp.bfloat16(0.125)
        lb = half_masks(BR)
        outs = []
        lses = []
        for h in range(2):
            qh = jnp.where(lb if h == 0 else ~lb, q2, jnp.zeros_like(q2))
            raw = dotf(qh, k2, NT) + prev_ref[h, sl, :].astype(jnp.float32)
            logits_ref[h, sl, :] = raw.astype(jnp.bfloat16)
            s = raw + mask_ref[sl, :]
            m = jnp.max(s, axis=1, keepdims=True)
            e = jnp.exp(s - m)
            tot = jnp.sum(e, axis=1, keepdims=True)
            o = dotf(e.astype(jnp.bfloat16), va if h == 0 else vb, NN)
            outs.append(o / tot)
            lses.append(m + jnp.log(tot))
        mixed_ref[sl, :] = (outs[0] + outs[1]).astype(jnp.bfloat16)
        lane = lax.broadcasted_iota(jnp.int32, (BR, 128), 1)
        cur = lse_ref[sl, :]
        cur = jnp.where(lane == 2 * g, lses[0], cur)
        cur = jnp.where(lane == 2 * g + 1, lses[1], cur)
        lse_ref[sl, :] = cur

def attn_fwd(qkv, prev, seg, BR=128):
    rows = qkv.shape[0]
    heads = prev.shape[0]
    G = heads // 2
    srow = seg.reshape(1, rows); scol = seg.reshape(rows, 1)
    return pl.pallas_call(
        functools.partial(attn_fwd_kernel, BR),
        grid=(G,),
        in_specs=[
            pl.BlockSpec((rows, 128), lambda g: (0, g)),
            pl.BlockSpec((rows, 128), lambda g: (0, G + g)),
            pl.BlockSpec((rows, 128), lambda g: (0, 2 * G + g)),
            pl.BlockSpec((2, rows, rows), lambda g: (g, 0, 0)),
            pl.BlockSpec((1, rows), lambda g: (0, 0)),
            pl.BlockSpec((rows, 1), lambda g: (0, 0)),
        ],
        out_specs=[
            pl.BlockSpec((2, rows, rows), lambda g: (g, 0, 0)),
            pl.BlockSpec((rows, 128), lambda g: (0, g)),
            pl.BlockSpec((rows, 128), lambda g: (0, 0)),
        ],
        out_shape=[
            jax.ShapeDtypeStruct((heads, rows, rows), jnp.bfloat16),
            jax.ShapeDtypeStruct((rows, heads * 64), jnp.bfloat16),
            jax.ShapeDtypeStruct((rows, 128), jnp.float32),
        ],
        scratch_shapes=[pltpu.VMEM((rows, rows), jnp.float32)],
        compiler_params=pltpu.CompilerParams(vmem_limit_bytes=60 * 2**20),
        name="attn_fwd",
    )(qkv, qkv, qkv, prev, srow, scol)

def attn_bwd_kernel(BR, q_ref, k_ref, v_ref, do_ref, prev_ref, dl_ref, lse_ref, srow_ref, scol_ref,
                    dprev_ref, dq_ref, dk_ref, dv_ref, mask_ref, p_ref, g_ref):
    g = pl.program_id(0)
    rows = q_ref.shape[0]
    @pl.when(g == 0)
    def _():
        mask_ref[...] = jnp.where(scol_ref[...] == srow_ref[...], 0.0, NEG)
    k2 = k_ref[...]
    v2 = v_ref[...]
    left = half_masks(rows)
    zero = jnp.zeros_like(v2)
    for h in range(2):
        lm = left if h == 0 else ~left
        kh = jnp.where(lm, k2, zero)
        for rb in range(rows // BR):
            sl = pl.ds(rb * BR, BR)
            lb = half_masks(BR)
            lb = lb if h == 0 else ~lb
            q2 = q_ref[sl, :] * jnp.bfloat16(0.125)
            qh = jnp.where(lb, q2, jnp.zeros_like(q2))
            doh = jnp.where(lb, do_ref[sl, :], jnp.zeros_like(q2))
            lane = lax.broadcasted_iota(jnp.int32, (BR, 128), 1)
            lse = jnp.sum(jnp.where(lane == 2 * g + h, lse_ref[sl, :], 0.0), axis=1, keepdims=True)
            s = dotf(qh, k2, NT) + prev_ref[h, sl, :].astype(jnp.float32) + mask_ref[sl, :]
            p = jnp.exp(s - lse)
            dp = dotf(doh, v2, NT)
            delta = jnp.sum(p * dp, axis=1, keepdims=True)
            ds = p * (dp - delta)
            gt = (ds + dl_ref[h, sl, :].astype(jnp.float32)).astype(jnp.bfloat16)
            dprev_ref[h, sl, :] = gt
            p_ref[sl, :] = p.astype(jnp.bfloat16)
            dq = dotf(gt, kh, NN) * 0.125
            if h == 0:
                dq_ref[sl, :] = dq.astype(jnp.bfloat16)
            else:
                dq_ref[sl, :] = dq_ref[sl, :] + dq.astype(jnp.bfloat16)
        qh = jnp.where(lm, q_ref[...], zero)
        doh = jnp.where(lm, do_ref[...], zero)
        dk = (dotf(dprev_ref[h], qh, TN) * 0.125).astype(jnp.bfloat16)
        dv = dotf(p_ref[...], doh, TN).astype(jnp.bfloat16)
        if h == 0:
            dk_ref[...] = dk
            dv_ref[...] = dv
        else:
            dk_ref[...] = dk_ref[...] + dk
            dv_ref[...] = dv_ref[...] + dv

def attn_bwd(qkv, do, prev, dl, lse, seg, BR=128):
    rows = qkv.shape[0]
    heads = prev.shape[0]
    G = heads // 2
    srow = seg.reshape(1, rows); scol = seg.reshape(rows, 1)
    col = lambda off: pl.BlockSpec((rows, 128), lambda g: (0, off + g))
    return pl.pallas_call(
        functools.partial(attn_bwd_kernel, BR),
        grid=(G,),
        in_specs=[
            col(0), col(G), col(2 * G), col(0),
            pl.BlockSpec((2, rows, rows), lambda g: (g, 0, 0)),
            pl.BlockSpec((2, rows, rows), lambda g: (g, 0, 0)),
            pl.BlockSpec((rows, 128), lambda g: (0, 0)),
            pl.BlockSpec((1, rows), lambda g: (0, 0)),
            pl.BlockSpec((rows, 1), lambda g: (0, 0)),
        ],
        out_specs=[
            pl.BlockSpec((2, rows, rows), lambda g: (g, 0, 0)),
            col(0), col(0), col(0),
        ],
        out_shape=[
            jax.ShapeDtypeStruct((heads, rows, rows), jnp.bfloat16),
        ] + [jax.ShapeDtypeStruct((rows, heads * 64), jnp.bfloat16)] * 3,
        scratch_shapes=[pltpu.VMEM((rows, rows), jnp.float32), pltpu.VMEM((rows, rows), jnp.bfloat16), pltpu.VMEM((8, 128), jnp.float32)],
        compiler_params=pltpu.CompilerParams(vmem_limit_bytes=60 * 2**20),
        name="attn_bwd",
    )(qkv, qkv, qkv, do, prev, dl, lse, srow, scol)


MESH = pl.DeviceIdType.MESH


def coords():
    dp = lax.axis_index("dp"); fs = lax.axis_index("fsdp")
    y = dp // 2; c = lax.rem(dp, 2)
    z = fs // 2; x = lax.rem(fs, 2)
    return y, c, z, x

def dev(y, c, z, x):
    return (y * 2 + c, z * 2 + x)


class Gather:
    def __init__(self, chunks, sources, wholes, send_sem, recv_sem):
        self.chunks, self.sources, self.wholes = chunks, sources, wholes
        self.send_sem, self.recv_sem = send_sem, recv_sem
        self.y, self.c, self.z, self.x = coords()

    def part(self, k):
        array, start, size, origin = self.chunks[k]
        return self.wholes[array], pl.ds(start, size), self.sources[array].at[:, pl.ds(origin, size)]

    def rows_of(self, k, x):
        size = self.sources[self.chunks[k][0]].shape[0]
        return pl.ds(pl.multiple_of(size * x, 8), size)

    def copy(self, src, dst, k, slot, who):
        return pltpu.make_async_remote_copy(
            src_ref=src, dst_ref=dst, send_sem=self.send_sem.at[k, slot], recv_sem=self.recv_sem.at[k, slot],
            device_id=who, device_id_type=MESH)

    def along_z(self, k):
        whole, cols, mine = self.part(k)
        spot = whole.at[self.y, self.c, self.z, self.rows_of(k, self.x), cols]
        return [self.copy(mine, spot, k, d, dev(self.y, self.c, lax.rem(self.z + d + 1, 4), self.x)) for d in range(3)]

    def to_neighbours(self, k):
        whole, cols, _ = self.part(k)
        block = whole.at[self.y, self.c, :, self.rows_of(k, self.x), cols]
        return [self.copy(block, block, k, 3, dev(self.y, self.c, self.z, 1 - self.x)),
                self.copy(block, block, k, 4, dev(1 - self.y, self.c, self.z, self.x))]

    def handed_on(self, k):
        whole, cols, _ = self.part(k)
        y, c, z, x = self.y, self.c, self.z, self.x
        block = whole.at[jnp.where(c == 0, y, 1 - y), c, :, self.rows_of(k, jnp.where(c == 0, 1 - x, x)), cols]
        who = (jnp.where(c == 0, 1 - y, y) * 2 + c, z * 2 + jnp.where(c == 0, x, 1 - x))
        return self.copy(block, block, k, 3 + c, who), self.copy(block, block, k, 5, who), self.copy(block, block, k, 4 - c, who)

    def to_core(self, k):
        whole, cols, _ = self.part(k)
        plane = whole.at[:, self.c, :, :, cols]
        return self.copy(plane, plane, k, 6, dev(self.y, 1 - self.c, self.z, self.x))

    def start(self, k):
        for d in self.along_z(k):
            d.start()

    def s1(self, k):
        for d in self.along_z(k):
            d.wait_recv()
        for d in self.to_neighbours(k):
            d.start()

    def s2(self, k):
        got, on, _ = self.handed_on(k)
        got.wait_recv()
        on.start()

    def s3(self, k):
        _, on, other = self.handed_on(k)
        other.wait_recv()
        on.wait_recv()
        self.to_core(k).start()

    def s4(self, k):
        self.to_core(k).wait_recv()

    def finish(self, k):
        for d in self.along_z(k) + self.to_neighbours(k) + [self.handed_on(k)[1], self.to_core(k)]:
            d.wait_send()


def peers_of(y, c, z, x):
    return [dev(y, c, lax.rem(z + d, 4), x) for d in (1, 2, 3)] + [dev(y, c, z, 1 - x), dev(1 - y, c, z, x), dev(y, 1 - c, z, x)]


class SmallSum:
    def __init__(self, mine, got, send_sem, recv_sem):
        self.mine, self.got, self.send_sem, self.recv_sem = mine, got, send_sem, recv_sem
        self.y, self.c, self.z, self.x = coords()
        self.peers = peers_of(self.y, self.c, self.z, self.x)

    def copy(self, i):
        return pltpu.make_async_remote_copy(
            src_ref=self.mine.at[max(i - 2, 0)], dst_ref=self.got.at[i], send_sem=self.send_sem.at[i], recv_sem=self.recv_sem.at[i],
            device_id=self.peers[i], device_id_type=MESH)

    def start(self, value):
        self.mine[0] = value
        for i in range(3):
            self.copy(i).start()

    def add_z(self):
        for i in range(3):
            self.copy(i).wait_recv()
        total = None
        for at in range(4):
            pick = self.mine[0]
            for i in range(3):
                pick = jnp.where(lax.rem(self.z - i + 3, 4) == at, self.got[i], pick)
            total = pick if total is None else total + pick
        self.mine[1] = total
        self.copy(3).start()

    def add(self, i):
        self.copy(i).wait_recv()
        total = self.mine[i - 2] + self.got[i]
        if i < 5:
            self.mine[i - 1] = total
            self.copy(i + 1).start()
        return total

    def finish(self):
        for i in range(6):
            self.copy(i).wait_send()


def normalise(v):
    centered = v - jnp.mean(v, axis=1, keepdims=True)
    scaling = lax.rsqrt(jnp.mean(centered * centered, axis=1, keepdims=True) + norm_eps)
    return centered * scaling, scaling


def fetch(src, dst, sem):
    copy = pltpu.make_async_copy(src, dst, sem)
    copy.start()
    copy.wait()


def forward_kernel(heads, x_ref, dout_ref, win_ref, wout_ref, vec_ref, prev_ref, srow_ref, scol_ref,
                   logits_ref, gq_ref, gu_ref, go_ref, small_ref, qkv_ref, mixed_ref, lse_ref, hlow_ref, none_ref, sone_ref,
                   act_ref, gp_ref, out_ref, dsec_ref, ddown_ref, sums_ref,
                   mask_ref, cin_ref, cout_ref, wq_ref, wo_ref, hid_ref, sec_ref, vmine, vgot,
                   send_sem, recv_sem, loc_sem, vs_sem, vr_sem):
    g = pl.program_id(0)
    rows, width = x_ref.shape
    hidden = act_ref.shape[1]
    last = heads // 2 - 1
    tile = 256
    y, c, z, x = coords()
    q_chunks = [(0, 768 * i, 768, 768 * i) for i in range(3)]
    o_chunks = [(2, 256 * i, 256, 256 * i) for i in range(3)]
    u_chunks = [(1, 768 * i, 768, 3 * width + 768 * i) for i in range(4)]
    chunks = q_chunks + o_chunks + u_chunks
    O, U = 3, 6
    ga = Gather(chunks, [cin_ref, cin_ref, cout_ref], [gq_ref, gu_ref, go_ref], send_sem, recv_sem)
    small = SmallSum(vmine, vgot, vs_sem, vr_sem)
    stores = lambda: [
        pltpu.make_async_copy(cin_ref.at[:, pl.ds(0, 3 * width)], gq_ref.at[y, c, z, ga.rows_of(0, x)], loc_sem.at[0]),
        pltpu.make_async_copy(cin_ref.at[:, pl.ds(3 * width, hidden)], gu_ref.at[y, c, z, ga.rows_of(U, x)], loc_sem.at[1]),
        pltpu.make_async_copy(cout_ref, go_ref.at[y, c, z, ga.rows_of(O, x)], loc_sem.at[2])]

    @pl.when(g == 0)
    def _():
        barrier = pltpu.get_barrier_semaphore()
        for p in small.peers:
            pl.semaphore_signal(barrier, inc=1, device_id=p, device_id_type=MESH)
        cin_ref[...] = win_ref[...].astype(jnp.bfloat16)
        cout_ref[...] = wout_ref[...].astype(jnp.bfloat16)
        for s in stores():
            s.start()
        lane = lax.broadcasted_iota(jnp.int32, (vec_ref.shape[1], width), 1)
        row = lax.broadcasted_iota(jnp.int32, (vec_ref.shape[1], width), 0)
        me = (y * 2 + c) * 8 + z * 2 + x
        place = jnp.where(lane == row + me * vec_ref.shape[1], 1.0, 0.0).astype(jnp.bfloat16)
        spread = dotf(vec_ref[...].astype(jnp.bfloat16), place, NN)
        pl.semaphore_wait(barrier, len(small.peers))
        small.start(spread)
        for k in range(len(chunks)):
            ga.start(k)
        mask_ref[...] = jnp.where(scol_ref[...] == srow_ref[...], 0.0, NEG)
        lse_ref[...] = jnp.zeros_like(lse_ref)
        for s in stores():
            s.wait()
        small.add_z()
        ga.s1(0)
        small.add(3)
        ga.s1(1)
        ga.s2(0)
        small.add(4)
        ga.s1(2)
        ga.s2(1)
        ga.s3(0)
        small_ref[...] = small.add(5)
        ga.s2(2)
        ga.s3(1)

        def project(k):
            fetch(gq_ref.reshape(width, 3 * width).at[:, pl.ds(768 * k, 768)], wq_ref, loc_sem.at[3])
            bias = {0: small_ref[4:5, :], 1: None, 2: small_ref[5:6, :]}[k]
            for j in range(768 // tile):
                v = dotf(x_ref[...], wq_ref[:, j * tile:(j + 1) * tile], NN)
                if bias is not None:
                    v = v + bias[:, j * tile:(j + 1) * tile]
                qkv_ref[:, 768 * k + j * tile:768 * k + (j + 1) * tile] = v.astype(jnp.bfloat16)

        ga.s4(0)
        project(0)
        ga.s3(2)
        ga.s1(O)
        ga.s4(1)
        project(1)
        ga.s4(2)
        project(2)

    plan = {0: [(1, O + 1)], 1: [(2, O), (1, O + 2)], 2: [(1, U), (3, O)], 3: [(2, O + 1), (1, U + 1)],
            4: [(1, U + 2), (3, O + 1)], 5: [(2, O + 2), (1, U + 3)]}
    for at, todo in plan.items():
        @pl.when(g == at)
        def _():
            for stage, k in todo:
                {1: ga.s1, 2: ga.s2, 3: ga.s3}[stage](k)

    at = lambda off: pl.ds(pl.multiple_of(off * width + g * 128, 128), 128)
    left = half_masks(rows)
    q2 = qkv_ref[:, at(0)] * jnp.bfloat16(0.125)
    k2 = qkv_ref[:, at(1)]
    v2 = qkv_ref[:, at(2)]
    zero = jnp.zeros_like(v2)
    outs, logs = [], []
    for h in range(2):
        pick = (lambda v: jnp.where(left, v, zero)) if h == 0 else (lambda v: jnp.where(left, zero, v))
        raw = dotf(pick(q2), k2, NT) + prev_ref[h].astype(jnp.float32)
        logits_ref[h] = raw.astype(jnp.bfloat16)
        s = raw + mask_ref[...]
        m = jnp.max(s, axis=1, keepdims=True)
        e = jnp.exp(s - m)
        tot = jnp.sum(e, axis=1, keepdims=True)
        outs.append(dotf(e.astype(jnp.bfloat16), pick(v2), NN) / tot)
        logs.append(m + jnp.log(tot))
    mixed_ref[:, pl.ds(pl.multiple_of(g * 128, 128), 128)] = (outs[0] + outs[1]).astype(jnp.bfloat16)
    lane = lax.broadcasted_iota(jnp.int32, (rows, 128), 1)
    lse_ref[...] = jnp.where(lane == 2 * g, logs[0], jnp.where(lane == 2 * g + 1, logs[1], lse_ref[...]))

    @pl.when(g == last)
    def _():
        ga.s3(O + 2)
        ga.s2(U)
        for k in range(3):
            ga.s4(O + k)
        whole = go_ref.reshape(width + hidden, width)
        fetch(whole.at[pl.ds(0, width), :], wq_ref, loc_sem.at[3])
        down = pltpu.make_async_copy(whole.at[pl.ds(width, hidden), :], wo_ref, loc_sem.at[4])
        down.start()
        for j in range(width // tile):
            sl = slice(j * tile, (j + 1) * tile)
            hid_ref[:, sl] = x_ref[:, sl].astype(jnp.float32) + (dotf(mixed_ref[...], wq_ref[:, sl], NN) + small_ref[6:7, sl])
        ga.s3(U)
        ga.s2(U + 1)

        @pl.loop(0, rows // 128)
        def _(i):
            sl = pl.ds(pl.multiple_of(i * 128, 128), 128)
            normed, scaling = normalise(hid_ref[sl, :])
            none_ref[sl, :] = normed
            sone_ref[sl, :] = jnp.broadcast_to(scaling, (128, 128))
            hid = normed * small_ref[0:1, :] + small_ref[2:3, :]
            hid_ref[sl, :] = hid
            hlow_ref[sl, :] = hid.astype(jnp.bfloat16)

        for k in range(4):
            ga.s4(U + k)
            fetch(gu_ref.reshape(width, hidden).at[:, pl.ds(768 * k, 768)], wq_ref, loc_sem.at[3])
            if k + 1 < 4:
                ga.s3(U + k + 1)
            if k + 2 < 4:
                ga.s2(U + k + 2)

            @pl.loop(0, 768 // tile)
            def _(j):
                sl = pl.ds(pl.multiple_of(j * tile, tile), tile)
                to = pl.ds(pl.multiple_of(768 * k + j * tile, tile), tile)
                u = dotf(hlow_ref[...], wq_ref[:, sl], NN) + small_ref[8 + k:9 + k, sl]
                cdf = 0.5 * (1.0 + lax.erf(u * math.sqrt(0.5)))
                act_ref[:, to] = (u * cdf).astype(jnp.bfloat16)
                gp_ref[:, to] = (cdf + u * (jnp.exp(-0.5 * (u * u)) * (1.0 / math.sqrt(2.0 * math.pi)))).astype(jnp.bfloat16)
        down.wait()
        for j in range(width // tile):
            sl = slice(j * tile, (j + 1) * tile)
            sec_ref[:, sl] = hid_ref[:, sl] + (dotf(act_ref[...], wo_ref[:, sl], NN) + small_ref[7:8, sl])
        sums_ref[...] = jnp.zeros_like(sums_ref)

        @pl.loop(0, rows // 128)
        def _(i):
            sl = pl.ds(pl.multiple_of(i * 128, 128), 128)
            normed, scaling = normalise(sec_ref[sl, :])
            out_ref[sl, :] = (normed * small_ref[1:2, :] + small_ref[3:4, :]).astype(jnp.bfloat16)
            dy = dout_ref[sl, :].astype(jnp.float32)
            back = norm_back(dy, normed, scaling, small_ref[1:2, :])
            low = back.astype(jnp.bfloat16)
            dsec_ref[sl, :] = back
            ddown_ref[sl, :] = low
            sums_ref[0:1, :] += jnp.sum(dy * normed, axis=0, keepdims=True)
            sums_ref[1:2, :] += jnp.sum(dy, axis=0, keepdims=True)
            sums_ref[2:3, :] += jnp.sum(low.astype(jnp.float32), axis=0, keepdims=True)
        small.finish()
        for k in range(len(chunks)):
            ga.finish(k)


def forward_all(tokens, grad_out, weight_in, weight_out, vectors, prev, seg):
    rows, width = tokens.shape
    heads = prev.shape[0]
    hidden = weight_in.shape[1] - 3 * width
    f32, bf16 = jnp.float32, jnp.bfloat16
    fixed = lambda shape: pl.BlockSpec(shape, lambda g: (0,) * len(shape), pipeline_mode=pl.Buffered(1))
    pair = pl.BlockSpec((2, rows, rows), lambda g: (g, 0, 0))
    hbm = pl.BlockSpec(memory_space=pl.ANY)
    grid4 = (2, 2, 4)
    flat = [((vectors.shape[0], width), f32), ((rows, 3 * width), bf16), ((rows, width), bf16), ((rows, 128), f32), ((rows, width), bf16),
            ((rows, width), f32), ((rows, 128), f32), ((rows, hidden), bf16), ((rows, hidden), bf16), ((rows, width), bf16),
            ((rows, width), f32), ((rows, width), bf16), ((8, width), f32)]
    whole = [grid4 + (2 * weight_in.shape[0], 3 * width), grid4 + (2 * weight_in.shape[0], hidden), grid4 + (2 * weight_out.shape[0], width)]
    return pl.pallas_call(
        functools.partial(forward_kernel, heads),
        grid=(heads // 2,),
        in_specs=[fixed((rows, width)), fixed((rows, width)), fixed(weight_in.shape), fixed(weight_out.shape), fixed(vectors.shape), pair,
                  fixed((1, rows)), fixed((rows, 1))],
        out_specs=[pair, hbm, hbm, hbm] + [fixed(s) for s, _ in flat],
        out_shape=[jax.ShapeDtypeStruct(prev.shape, bf16)] + [jax.ShapeDtypeStruct(s, bf16) for s in whole]
        + [jax.ShapeDtypeStruct(s, t) for s, t in flat],
        scratch_shapes=[
            pltpu.VMEM((rows, rows), f32), pltpu.VMEM(weight_in.shape, bf16), pltpu.VMEM(weight_out.shape, bf16),
            pltpu.VMEM((width, 768), bf16), pltpu.VMEM((hidden, width), bf16), pltpu.VMEM((rows, width), f32), pltpu.VMEM((rows, width), f32),
            pltpu.VMEM((4, vectors.shape[0], width), f32), pltpu.VMEM((6, vectors.shape[0], width), f32),
            pltpu.SemaphoreType.DMA((10, 7)), pltpu.SemaphoreType.DMA((10, 7)), pltpu.SemaphoreType.DMA((5,)),
            pltpu.SemaphoreType.DMA((6,)), pltpu.SemaphoreType.DMA((6,))],
        compiler_params=pltpu.CompilerParams(collective_id=1, has_side_effects=True, vmem_limit_bytes=64 * 2**20 - 65536),
        name="forward",
    )(tokens, grad_out, weight_in, weight_out, vectors, prev, seg.reshape(1, rows), seg.reshape(rows, 1))


class Scatter:
    def __init__(self, full, got, send_sem, recv_sem):
        self.full, self.got = full, got
        self.send_sem, self.recv_sem = send_sem, recv_sem
        y, c, z, x = self.y, self.c, self.z, self.x = coords()
        first, second = (1 - y) * 2 + c, z * 2 + 1 - x
        self.core = dev(y, 1 - c, z, x)
        self.one = (jnp.where(c == 0, first, y * 2 + c), jnp.where(c == 0, z * 2 + x, second))
        self.two = (jnp.where(c == 0, y * 2 + c, first), jnp.where(c == 0, second, z * 2 + x))
        self.at_one = (jnp.where(c == 0, 1 - y, y), jnp.where(c == 0, x, 1 - x))
        self.at_two = (jnp.where(c == 0, y, 1 - y), jnp.where(c == 0, 1 - x, x))

    def copy(self, src, dst, k, slot, who):
        return pltpu.make_async_remote_copy(
            src_ref=src, dst_ref=dst, send_sem=self.send_sem.at[k, slot], recv_sem=self.recv_sem.at[k, slot],
            device_id=who, device_id_type=MESH)

    def to_core(self, k):
        return self.copy(self.full[k]().at[:, 1 - self.c], self.got[k][0], k, 0, self.core)

    def to_one(self, k):
        full = self.full[k]()
        return [self.copy(full.at[1 - self.y, self.c, :, 1 - self.x], self.got[k][1].at[0], k, 1, self.one),
                self.copy(full.at[self.at_one[0], self.c, :, self.at_one[1]], self.got[k][1].at[1], k, 2, self.one)]

    def to_two(self, k):
        return self.copy(self.full[k]().at[self.at_two[0], self.c, :, self.at_two[1]], self.got[k][2], k, 3, self.two)

    def along_z(self, k):
        full = self.full[k]()
        out = []
        for i in range(3):
            z = lax.rem(self.z + i + 1, 4)
            out.append(self.copy(full.at[self.y, self.c, z, self.x], self.got[k][3].at[i], k, 4 + i, dev(self.y, self.c, z, self.x)))
        return out

    def r1(self, k):
        self.to_core(k).start()

    def r2(self, k):
        full, got = self.full[k](), self.got[k][0]
        self.to_core(k).wait_recv()

        @pl.loop(0, 8)
        def _(i):
            for y in range(2):
                z, x = i // 2, lax.rem(i, 2)
                total = full[y, self.c, z, x].astype(jnp.float32) + got[y, z, x].astype(jnp.float32)
                full[y, self.c, z, x] = total.astype(jnp.bfloat16)
        for d in self.to_one(k):
            d.start()

    def r3(self, k):
        full, got = self.full[k](), self.got[k][1]
        for d in self.to_one(k):
            d.wait_recv()
        y, x = self.at_two

        @pl.loop(0, 4)
        def _(z):
            total = full[y, self.c, z, x].astype(jnp.float32) + got[0, z].astype(jnp.float32)
            full[y, self.c, z, x] = total.astype(jnp.bfloat16)
        self.to_two(k).start()

    def r4(self, k):
        full = self.full[k]()
        self.to_two(k).wait_recv()

        @pl.loop(0, 4)
        def _(z):
            total = full[self.y, self.c, z, self.x].astype(jnp.float32) + self.got[k][1][1, z].astype(jnp.float32)
            total = total + self.got[k][2][z].astype(jnp.float32)
            full[self.y, self.c, z, self.x] = total.astype(jnp.bfloat16)
        for d in self.along_z(k):
            d.start()

    def r5(self, k):
        for d in self.along_z(k):
            d.wait_recv()
        total = self.full[k]()[self.y, self.c, self.z, self.x].astype(jnp.float32)
        for i in range(3):
            total = total + self.got[k][3][i].astype(jnp.float32)
        return total

    def finish(self, k):
        for d in [self.to_core(k), *self.to_one(k), self.to_two(k), *self.along_z(k)]:
            d.wait_send()


def put_rows(ref, start, value, columns):
    size, count = ref.shape[4], value.shape[0]
    for d in range(start // size, (start + count - 1) // size + 1):
        low, high = max(start, d * size), min(start + count, (d + 1) * size)
        ref[d // 16, d // 8 % 2, d // 2 % 4, d % 2, low - d * size:high - d * size, :, columns] = value[low - start:high - start]


def backward_kernel(heads, plan, *refs):
    (ddown_ref, hlow_ref, small_ref, two_ref, lse_ref, sone_ref, srow_ref, scol_ref, prev_ref, dl_ref,
     act_hbm, gp_hbm, go_hbm, gu_hbm, gq_hbm, dsec_hbm, none_hbm, mixed_hbm, x_hbm, qkv_hbm,
     dprev_ref, dx_ref, gin_ref, gout_ref, sumsmall_ref, norm_ref) = refs[:26]
    (mask_ref, p_ref, qkv_ref, do_ref, x_ref, mixed_ref, act_ref, gp_ref, dup_ref, w0_ref, w1_ref, w2_ref, acc_ref, none_ref,
     part_ref) = refs[26:41]
    ups, outs = refs[41:45], refs[45:48]
    got_flat = refs[48:100]
    (vmine, vgot, nmine, ngot, send_sem, recv_sem, loc_sem, vs_sem, vr_sem, ns_sem, nr_sem) = refs[100:]
    g = pl.program_id(0)
    rows, width = ddown_ref.shape
    hidden = act_hbm.shape[1]
    tile = 256
    U, O, Q = 0, 4, 7
    got = [got_flat[4 * k:4 * k + 4] for k in range(13)]
    full = [lambda r=r: r for r in ups] + [lambda r=r: r for r in outs]
    full += [lambda r=ups[p // 2], at=384 * (p % 2): r.at[:, :, :, :, :, :, pl.ds(at, 384)] for p in range(6)]
    sc = Scatter(full, got, send_sem, recv_sem)
    small = SmallSum(vmine, vgot, vs_sem, vr_sem)
    norm = SmallSum(nmine, ngot, ns_sem, nr_sem)
    stages = {1: sc.r1, 2: sc.r2, 3: sc.r3, 4: sc.r4}

    def run(place):
        for stage, k in plan.get(place, ()):
            if stage == 5:
                finish(k)
            else:
                stages[stage](k)

    def finish(k):
        total = sc.r5(k)
        if k < O:
            gin_ref[:, :, 3 * width + 768 * k:3 * width + 768 * (k + 1)] = total
        elif k < Q:
            gout_ref[:, :, 256 * (k - O):256 * (k - O + 1)] = total
        else:
            for i in range(3):
                gin_ref[:, :, width * i + 128 * (k - Q):width * i + 128 * (k - Q + 1)] = total[:, :, 128 * i:128 * (i + 1)]

    def load(src, dst, i):
        return pltpu.make_async_copy(src, dst, loc_sem.at[i])

    w_out, w_up, w_qkv = go_hbm.reshape(width + hidden, width), gu_hbm.reshape(width, hidden), gq_hbm.reshape(width, 3 * width)
    late = lambda: [load(dsec_hbm, acc_ref, 0), load(none_hbm, none_ref, 1), load(mixed_hbm, mixed_ref, 2), load(x_hbm, x_ref, 3), load(qkv_hbm, qkv_ref, 4)]
    last_w = lambda: [load(w_qkv.at[:, pl.ds(768 * i, 768)], w, 5 + i) for i, w in enumerate((w0_ref, w1_ref, w2_ref))]

    @pl.when(g == 0)
    def _():
        barrier = pltpu.get_barrier_semaphore()
        for p in small.peers:
            pl.semaphore_signal(barrier, inc=1, device_id=p, device_id_type=MESH)

        def piece(k):
            cols = pl.ds(768 * k, 768)
            return [load(w_out.at[pl.ds(width + 768 * k, 768), :], w0_ref, 5), load(gp_hbm.at[:, cols], gp_ref, 6),
                    load(w_up.at[:, cols], w1_ref, 7), load(act_hbm.at[:, cols], act_ref, 8)]
        for d in piece(0) + late():
            d.start()
        part_ref[...] = jnp.zeros_like(part_ref)
        mask_ref[...] = jnp.where(scol_ref[...] == srow_ref[...], 0.0, NEG)
        part_ref[1:2, :] = two_ref[0:1, :]
        part_ref[3:4, :] = two_ref[1:2, :]
        part_ref[7:8, :] = two_ref[2:3, :]
        pl.semaphore_wait(barrier, len(small.peers))
        for k in range(4):
            for d in piece(k):
                d.wait()

            @pl.loop(0, 768 // tile)
            def _(j):
                sl = pl.ds(pl.multiple_of(j * tile, tile), tile)
                grad = dotf(ddown_ref[...], w0_ref[sl, :], NT) * gp_ref[:, sl].astype(jnp.float32)
                low = grad.astype(jnp.bfloat16)
                dup_ref[:, sl] = low
                part_ref[8 + k:9 + k, sl] = jnp.sum(low.astype(jnp.float32), axis=0, keepdims=True)
                ups[k][:, :, :, :, :, :, sl] = dotf(hlow_ref[...], low, TN).reshape(ups[k].shape[:6] + (tile,)).astype(jnp.bfloat16)
            sc.r1(U + k)
            run(("down", k))
            if k == 0:
                late()[0].wait()
            for j in range(3):
                sl = slice(j * tile, (j + 1) * tile)
                acc_ref[:, sl] += dotf(dup_ref[...], w1_ref[sl, :], NT)
                put_rows(outs[j], (width + 768 * k) // 8, dotf(act_ref[...], ddown_ref[:, sl], TN).reshape(96, 8, tile).astype(jnp.bfloat16), slice(None))
            if k < 3:
                for d in piece(k + 1):
                    d.start()
            run(("up", k))
        wo = load(w_out.at[pl.ds(0, width), :], w0_ref, 5)
        wo.start()
        late()[1].wait()

        @pl.loop(0, rows // 128)
        def _(i):
            sl = pl.ds(pl.multiple_of(i * 128, 128), 128)
            one, normed = acc_ref[sl, :], none_ref[sl, :]
            part_ref[0:1, :] += jnp.sum(one * normed, axis=0, keepdims=True)
            part_ref[2:3, :] += jnp.sum(one, axis=0, keepdims=True)
            back = norm_back(one, normed, sone_ref[sl, 0:1], small_ref[0:1, :])
            low = back.astype(jnp.bfloat16)
            acc_ref[sl, :] = back
            dup_ref[sl, :] = low
            part_ref[6:7, :] += jnp.sum(low.astype(jnp.float32), axis=0, keepdims=True)
        run("norm")
        late()[2].wait()
        for j in range(3):
            sl = slice(j * tile, (j + 1) * tile)
            put_rows(outs[j], 0, dotf(mixed_ref[...], dup_ref[:, sl], TN).reshape(96, 8, tile).astype(jnp.bfloat16), slice(None))
            sc.r1(O + j)
        wo.wait()
        for j in range(3):
            sl = slice(j * tile, (j + 1) * tile)
            do_ref[:, sl] = dotf(dup_ref[...], w0_ref[sl, :], NT).astype(jnp.bfloat16)
        late()[3].wait()
        late()[4].wait()
        for d in last_w():
            d.start()

    for i in range(heads):
        if plan.get(("head", i)):
            @pl.when(g == i)
            def _():
                run(("head", i))

    pair, half = g // 2, lax.rem(g, 2)
    at = lambda off: pl.ds(pl.multiple_of(off * width + pair * 128, 128), 128)
    lane = lax.broadcasted_iota(jnp.int32, (rows, 128), 1)
    pick = lambda v: jnp.where(lane // 64 == half, v, jnp.zeros_like(v))
    q2, k2, v2, do2 = qkv_ref[:, at(0)], qkv_ref[:, at(1)], qkv_ref[:, at(2)], do_ref[:, at(0)]
    lse = jnp.sum(jnp.where(lane == g, lse_ref[...], 0.0), axis=1, keepdims=True)
    s = dotf(pick(q2) * jnp.bfloat16(0.125), k2, NT) + prev_ref[0].astype(jnp.float32) + mask_ref[...]
    p = jnp.exp(s - lse)
    dp = dotf(pick(do2), v2, NT)
    ds = p * (dp - jnp.sum(p * dp, axis=1, keepdims=True))
    grad = (ds + dl_ref[0].astype(jnp.float32)).astype(jnp.bfloat16)
    dprev_ref[0] = grad
    p_ref[...] = p.astype(jnp.bfloat16)
    dq = (dotf(grad, pick(k2), NN) * 0.125).astype(jnp.bfloat16)
    dk = (dotf(dprev_ref[0], pick(q2), TN) * 0.125).astype(jnp.bfloat16)
    dv = dotf(p_ref[...], pick(do2), TN).astype(jnp.bfloat16)

    @pl.when(half == 0)
    def _():
        for i, v in enumerate((dq, dk, dv)):
            gp_ref[:, 128 * i:128 * (i + 1)] = v

    @pl.when(half == 1)
    def _():
        for i, v in enumerate((dq, dk, dv)):
            v = gp_ref[:, 128 * i:128 * (i + 1)] + v
            gp_ref[:, 128 * i:128 * (i + 1)] = v
            qkv_ref[:, at(i)] = v
            if i != 1:
                part_ref[4 + i // 2:5 + i // 2, at(0)] = jnp.sum(v.astype(jnp.float32), axis=0, keepdims=True)
        for p in range(heads // 2):
            @pl.when(pair == p)
            def _():
                if p % 2 == 0:
                    sc.finish(U + p // 2)
                for i in range(3):
                    dst = ups[p // 2]
                    to = 384 * (p % 2) + 128 * i
                    v = dotf(x_ref[...], gp_ref[:, 128 * i:128 * (i + 1)], TN)
                    dst[:, :, :, :, :, :, to:to + 128] = v.reshape(dst.shape[:6] + (128,)).astype(jnp.bfloat16)
                sc.r1(Q + p)

    @pl.when(g == heads - 1)
    def _():
        small.start(part_ref[...])
        run("end0")
        for d in last_w():
            d.wait()
        ws = (w0_ref, w1_ref, w2_ref)
        for j in range(3):
            sl = slice(j * tile, (j + 1) * tile)
            total = acc_ref[:, sl]
            for i in range(3):
                total = total + dotf(qkv_ref[:, 768 * i:768 * (i + 1)], ws[i][sl, :], NT)
            dx_ref[:, sl] = total.astype(jnp.bfloat16)
            run(("end1", j))
            if j == 0:
                small.add_z()
            elif j == 1:
                small.add(3)
            else:
                small.add(4)
        run("end2")
        total_small = small.add(5)
        sumsmall_ref[...] = total_small
        run("end3")
        squares = jnp.zeros((8, 128), jnp.float32)
        for ref in (gin_ref, gout_ref):
            v = ref[...]
            v = jnp.sum(v * v, axis=0)
            for j in range(v.shape[1] // 128):
                squares = squares + v[:, 128 * j:128 * (j + 1)]
        norm.start(jnp.sum(squares, keepdims=True) + jnp.zeros((8, 128), jnp.float32))
        norm.add_z()
        norm.add(3)
        norm.add(4)
        total = norm.add(5) + jnp.sum(total_small * total_small, keepdims=True)
        norm_ref[...] = jnp.sqrt(total)
        small.finish()
        norm.finish()
        for k in range(13):
            if k not in (0, 1, 2):
                sc.finish(k)


def backward_all(plan, grad_down, hidden_low, small, two_sums, log_sums, scale_one, seg, prev, grad_logits,
                 activated, slope, full_out, full_up, full_qkv, grad_second, normed_one, mixed, tokens, qkv):
    rows, width = tokens.shape
    heads = prev.shape[0]
    hidden = activated.shape[1]
    f32, bf16 = jnp.float32, jnp.bfloat16
    fixed = lambda shape: pl.BlockSpec(shape, lambda g: (0,) * len(shape), pipeline_mode=pl.Buffered(1))
    head = pl.BlockSpec((1, rows, rows), lambda g: (g, 0, 0))
    hbm = pl.BlockSpec(memory_space=pl.ANY)
    r_in, r_out = full_qkv.shape[3] // 2, full_out.shape[3] // 2
    landing = []
    for r, n in [(r_in, 768)] * 4 + [(r_out, 256)] * 3 + [(r_in, 384)] * 6:
        landing += [pltpu.VMEM(lead + (r // 8, 8, n), bf16) for lead in ((2, 4, 2), (2, 4), (4,), (3,))]
    lead = (2, 2, 4, 2)
    v = lambda *shape: pltpu.VMEM(shape, bf16)
    vf = lambda *shape: pltpu.VMEM(shape, f32)
    shapes = [((r_in // 8, 8, 3 * width + hidden), f32), ((r_out // 8, 8, width), f32), (small.shape, f32), ((8, 128), f32)]
    dma = pltpu.SemaphoreType.DMA
    return pl.pallas_call(
        functools.partial(backward_kernel, heads, plan),
        grid=(heads,),
        in_specs=[fixed((rows, width)), fixed((rows, width)), fixed(small.shape), fixed(two_sums.shape), fixed(log_sums.shape),
                  fixed(scale_one.shape), fixed((1, rows)), fixed((rows, 1)), head, head] + [hbm] * 10,
        out_specs=[head, fixed((rows, width))] + [fixed(s) for s, _ in shapes],
        out_shape=[jax.ShapeDtypeStruct(prev.shape, bf16), jax.ShapeDtypeStruct((rows, width), bf16)]
        + [jax.ShapeDtypeStruct(s, t) for s, t in shapes],
        scratch_shapes=[vf(rows, rows), v(rows, rows), v(rows, 3 * width), v(rows, width), v(rows, width), v(rows, width), v(rows, 768),
                        v(rows, 768), v(rows, 768), v(768, width), v(768, width), v(768, width), vf(rows, width), vf(rows, width),
                        vf(*small.shape)]
        + [v(*lead, r_in // 8, 8, 768)] * 4 + [v(*lead, r_out // 8, 8, 256)] * 3 + landing
        + [vf(4, *small.shape), vf(6, *small.shape), vf(4, 8, 128), vf(6, 8, 128), dma((13, 7)), dma((13, 7)), dma((9,)),
           dma((6,)), dma((6,)), dma((6,)), dma((6,))],
        compiler_params=pltpu.CompilerParams(collective_id=2, has_side_effects=True, vmem_limit_bytes=64 * 2**20 - 65536),
        name="backward",
    )(grad_down, hidden_low, small, two_sums, log_sums, scale_one, seg.reshape(1, rows), seg.reshape(rows, 1), prev, grad_logits,
      activated, slope, full_out, full_up, full_qkv, grad_second, normed_one, mixed, tokens, qkv)


PLAN = {
    ("down", 1): [(2, 0)],
    ("down", 2): [(3, 0), (2, 1)],
    ("up", 2): [],
    ("down", 3): [(3, 1), (2, 2), (4, 0)],
    ("up", 3): [],
    "norm": [(4, 1), (3, 2), (2, 3)],
    ("head", 0): [(5, 0), (2, 4), (3, 3), (4, 2)],
    ("head", 1): [(2, 5), (2, 6)],
    ("head", 2): [(5, 1), (4, 3)],
    ("head", 3): [(3, 4), (5, 2)],
    ("head", 4): [(2, 7)],
    ("head", 5): [(3, 5), (4, 4), (5, 3)],
    ("head", 6): [(2, 8)],
    ("head", 7): [(3, 6), (4, 5), (3, 7)],
    ("head", 8): [(2, 9), (5, 4)],
    ("head", 9): [(4, 6), (3, 8), (4, 7)],
    ("head", 10): [(2, 10), (5, 5), (3, 9), (4, 8)],
    ("head", 11): [(5, 6), (3, 10), (4, 9)],
    "end0": [(2, 11), (2, 12), (5, 7)],
    ("end1", 0): [(4, 10), (3, 11)],
    ("end1", 1): [(3, 12), (5, 8)],
    ("end1", 2): [(4, 11), (5, 9), (4, 12)],
    "end2": [(5, 10), (5, 11), (5, 12)],
    "end3": [],
}


def adam_update(master, moment, square, gradient, factor, step_value, step_rate, decay_rate):
    clipped = gradient * factor
    new_moment = beta_one * moment + (1.0 - beta_one) * clipped
    new_square = beta_two * square + (1.0 - beta_two) * clipped * clipped
    fixed_moment = new_moment / (1.0 - jnp.power(beta_one, step_value))
    fixed_square = new_square / (1.0 - jnp.power(beta_two, step_value))
    updated = master - step_rate * (
        fixed_moment / (jnp.sqrt(fixed_square) + adam_eps) + decay_rate * master
    )
    return (clipped, new_moment, new_square, updated)


def rounded(v):
    return lax.reduce_precision(v, 8, 7)


def gather_all(weight_in, weight_out, vectors, width):
    whole = lambda v: lax.all_gather(v, AXES, axis=0, tiled=True)
    low_in = weight_in.astype(jnp.bfloat16)
    small = lax.all_gather(rounded(vectors), AXES, axis=1, tiled=True)
    return whole(low_in[:, : 3 * width]), whole(low_in[:, 3 * width :]), whole(weight_out.astype(jnp.bfloat16)), small


def forward_plain(tokens, grad_out, full_qkv, full_up, full_out, small, prev, segments):
    width = tokens.shape[1]
    dot = lambda a, b: jnp.dot(a, b, preferred_element_type=jnp.float32)
    sums = lambda v: jnp.sum(v, axis=0, dtype=jnp.float32)
    offsets = jnp.concatenate([small[4], jnp.zeros_like(small[4]), small[5]])
    qkv = (dot(tokens, full_qkv) + offsets).astype(jnp.bfloat16)
    logits, mixed, log_sums = attn_fwd(qkv, prev, segments, 640)
    first = tokens.astype(jnp.float32) + (dot(mixed, full_out[:width]) + small[6])
    hidden_one, normed_one, scale_one = norm_rows(first, small[0], small[2])
    hidden_low = hidden_one.astype(jnp.bfloat16)
    upward = dot(hidden_low, full_up) + small[8:].reshape(-1)
    activated, gelu_pull = jax.vjp(gelu_exact, upward)
    activated, slope = activated.astype(jnp.bfloat16), gelu_pull(jnp.ones_like(upward))[0]
    second = hidden_one + (dot(activated, full_out[width:]) + small[7])
    output, normed_two, scale_two = norm_rows(second, small[1], small[3])
    grad_output = grad_out.astype(jnp.float32)
    grad_second = norm_back(grad_output, normed_two, scale_two, small[1])
    grad_down = grad_second.astype(jnp.bfloat16)
    two_sums = jnp.stack([sums(grad_output * normed_two), sums(grad_output), sums(grad_down)])
    return (logits, qkv, mixed, log_sums, hidden_low, normed_one, scale_one, activated, slope, output.astype(jnp.bfloat16),
            grad_second, grad_down, two_sums)


def reduce_all(grad_qkv, grad_up, grad_out, small, shards):
    part = lambda v: lax.psum_scatter(v, AXES, scatter_dimension=0, tiled=True).astype(jnp.float32)
    owned_in = jnp.concatenate([part(grad_qkv), part(grad_up)], axis=1)
    owned_out = part(grad_out)
    owned_small = lax.psum_scatter(small, AXES, scatter_dimension=1, tiled=True)
    total = lax.psum(jnp.sum(owned_in**2) + jnp.sum(owned_out**2) + jnp.sum(owned_small**2), AXES)
    return owned_in, owned_out, owned_small, jnp.sqrt(total)


def body(remote, hidden_in, prev_logits, segment_ids, d_hidden, d_logits, weight_in, weight_out, vectors,
         moment_in, moment_out, moment_vectors, square_in, square_out, square_vectors, step_count):
    width = weight_out.shape[1]
    shards = lax.axis_size("dp") * lax.axis_size("fsdp")
    dot = lambda spec, a, b: jnp.einsum(spec, a, b, preferred_element_type=jnp.float32)
    sums = lambda v: jnp.sum(v, axis=0, dtype=jnp.float32)
    segments = segment_ids[0]
    if remote:
        (logits, full_qkv, full_up, full_out, small, qkv, mixed, log_sums, hidden_low, normed_one, scale_one, activated, slope, output,
         grad_second, grad_down, two_sums) = forward_all(hidden_in, d_hidden, weight_in, weight_out, vectors, prev_logits[0], segments)
        grad_prev, grad_tokens, owned_in, owned_out, total_small, norm = backward_all(
            PLAN, grad_down, hidden_low, small, two_sums, log_sums, scale_one, segments, prev_logits[0], d_logits[0],
            activated, slope, full_out, full_up, full_qkv, grad_second, normed_one, mixed, hidden_in, qkv)
        me = lax.axis_index("dp") * lax.axis_size("fsdp") + lax.axis_index("fsdp")
        owned_small = lax.dynamic_slice(total_small, (0, me * vectors.shape[1]), vectors.shape)
        owned_in, owned_out, grad_norm = owned_in.reshape(weight_in.shape), owned_out.reshape(weight_out.shape), norm[0, 0]
    else:
        (full_qkv, full_up, full_out, small) = gather_all(weight_in, weight_out, vectors, width)
        (logits, qkv, mixed, log_sums, hidden_low, normed_one, scale_one, activated, slope, output,
         grad_second, grad_down, two_sums) = forward_plain(hidden_in, d_hidden, full_qkv, full_up, full_out, small, prev_logits[0], segments)
        w_attn, w_down = full_out[:width], full_out[width:]
        down_grad = dot("tf,td->fd", activated, grad_down).astype(jnp.bfloat16)
        grad_up = (dot("td,fd->tf", grad_down, w_down) * slope).astype(jnp.bfloat16)
        up_grad = dot("td,tf->df", hidden_low, grad_up).astype(jnp.bfloat16)
        grad_one = grad_second + dot("tf,df->td", grad_up, full_up)
        grad_first = norm_back(grad_one, normed_one, scale_one, small[0])
        grad_attn = grad_first.astype(jnp.bfloat16)
        attn_grad = dot("tc,td->cd", mixed, grad_attn).astype(jnp.bfloat16)
        grad_mixed = dot("td,cd->tc", grad_attn, w_attn).astype(jnp.bfloat16)
        grad_prev, grad_q, grad_k, grad_v = attn_bwd(qkv, grad_mixed, prev_logits[0], d_logits[0], log_sums, segments, 640)
        grad_qkv = jnp.concatenate([grad_q, grad_k, grad_v], axis=1)
        qkv_grad = dot("td,tc->dc", hidden_in, grad_qkv).astype(jnp.bfloat16)
        grad_tokens = (grad_first + dot("tc,dc->td", grad_qkv, full_qkv)).astype(jnp.bfloat16)
        small_grad = jnp.concatenate([
            jnp.stack([sums(grad_one * normed_one), two_sums[0], sums(grad_one), two_sums[1],
                       sums(grad_q), sums(grad_v), sums(grad_attn), two_sums[2]]),
            sums(grad_up).reshape(-1, width)], axis=0)

        owned_in, owned_out, owned_small, grad_norm = reduce_all(
            qkv_grad, up_grad, jnp.concatenate([attn_grad, down_grad], axis=0), small_grad, shards)
    factor = jnp.minimum(1.0, clip_scale * math.sqrt(PARAMS) / (grad_norm + 1e-06))
    step_value = step_count[0].astype(jnp.float32)
    new = [
        adam_update(weight_in, moment_in, square_in, owned_in, factor, step_value, rate_matrix, decay_matrix),
        adam_update(weight_out, moment_out, square_out, owned_out, factor, step_value, rate_matrix, decay_matrix),
        adam_update(vectors, moment_vectors, square_vectors, owned_small, factor, step_value, rate_vector, 0.0),
    ]
    clipped, moments, squares, updated = zip(*new)
    return (output.astype(jnp.bfloat16), logits[None], grad_tokens, grad_prev[None],
            *clipped, *moments, *squares, *updated, *[u.astype(jnp.bfloat16) for u in updated], grad_norm)


def solution(mesh):
    remote = (mesh.shape["dp"], mesh.shape["fsdp"]) == (4, 8)
    rows = P(AXES, None)
    heads = P(AXES, None, None, None)
    cols = P(None, AXES)
    trio = (rows, rows, cols)
    return jax.shard_map(
        functools.partial(body, remote),
        mesh=mesh,
        in_specs=(rows, heads, rows, rows, heads, *trio, *trio, *trio, P()),
        out_specs=(rows, heads, rows, heads, *trio, *trio, *trio, *trio, *trio, P()),
        check_vma=False,
    )
```

```python
import functools
import math

import jax
import jax.numpy as jnp
from jax import lax
from jax.experimental import pallas as pl
from jax.experimental.pallas import tpu as pltpu
from jax.sharding import PartitionSpec as P

PARAMS = 7087104


norm_eps = 1e-12
clip_scale = 1.0
beta_one = 0.9
beta_two = 0.999
adam_eps = 1e-08
rate_matrix = 0.06
rate_vector = 0.25
decay_matrix = 0.01
NEG = -1e30
NT = (((1,), (1,)), ((), ()))
NN = (((1,), (0,)), ((), ()))
TN = (((0,), (0,)), ((), ()))
AXES = ("dp", "fsdp")


def gelu_exact(upward):
    return jax.nn.gelu(upward, approximate=False)


def norm_rows(residual, gain_row, shift_row):
    centered = residual - jnp.mean(residual, axis=1, keepdims=True)
    scaling = lax.rsqrt(jnp.mean(centered * centered, axis=1, keepdims=True) + norm_eps)
    normed = centered * scaling
    return (normed * gain_row + shift_row, normed, scaling)


def norm_back(grad_after, normed, scaling, gain_row):
    scaled_grad = grad_after * gain_row
    return scaling * (
        scaled_grad
        - jnp.mean(scaled_grad, axis=1, keepdims=True)
        - normed * jnp.mean(scaled_grad * normed, axis=1, keepdims=True)
    )


def dotf(a, b, dims):
    return lax.dot_general(a, b, dims, preferred_element_type=jnp.float32)

def half_masks(rows):
    lane = lax.broadcasted_iota(jnp.int32, (rows, 128), 1)
    return lane < 64

def attn_fwd_kernel(BR, q_ref, k_ref, v_ref, prev_ref, srow_ref, scol_ref, logits_ref, mixed_ref, lse_ref, mask_ref):
    g = pl.program_id(0)
    rows = q_ref.shape[0]
    @pl.when(g == 0)
    def _():
        mask_ref[...] = jnp.where(scol_ref[...] == srow_ref[...], 0.0, NEG)
        lse_ref[...] = jnp.zeros_like(lse_ref)
    k2 = k_ref[...]
    v2 = v_ref[...]
    left = half_masks(rows)
    zero = jnp.zeros_like(v2)
    va = jnp.where(left, v2, zero)
    vb = jnp.where(left, zero, v2)
    for rb in range(rows // BR):
        sl = pl.ds(rb * BR, BR)
        q2 = q_ref[sl, :] * jnp.bfloat16(0.125)
        lb = half_masks(BR)
        outs = []
        lses = []
        for h in range(2):
            qh = jnp.where(lb if h == 0 else ~lb, q2, jnp.zeros_like(q2))
            raw = dotf(qh, k2, NT) + prev_ref[h, sl, :].astype(jnp.float32)
            logits_ref[h, sl, :] = raw.astype(jnp.bfloat16)
            s = raw + mask_ref[sl, :]
            m = jnp.max(s, axis=1, keepdims=True)
            e = jnp.exp(s - m)
            tot = jnp.sum(e, axis=1, keepdims=True)
            o = dotf(e.astype(jnp.bfloat16), va if h == 0 else vb, NN)
            outs.append(o / tot)
            lses.append(m + jnp.log(tot))
        mixed_ref[sl, :] = (outs[0] + outs[1]).astype(jnp.bfloat16)
        lane = lax.broadcasted_iota(jnp.int32, (BR, 128), 1)
        cur = lse_ref[sl, :]
        cur = jnp.where(lane == 2 * g, lses[0], cur)
        cur = jnp.where(lane == 2 * g + 1, lses[1], cur)
        lse_ref[sl, :] = cur

def attn_fwd(qkv, prev, seg, BR=128):
    rows = qkv.shape[0]
    heads = prev.shape[0]
    G = heads // 2
    srow = seg.reshape(1, rows); scol = seg.reshape(rows, 1)
    return pl.pallas_call(
        functools.partial(attn_fwd_kernel, BR),
        grid=(G,),
        in_specs=[
            pl.BlockSpec((rows, 128), lambda g: (0, g)),
            pl.BlockSpec((rows, 128), lambda g: (0, G + g)),
            pl.BlockSpec((rows, 128), lambda g: (0, 2 * G + g)),
            pl.BlockSpec((2, rows, rows), lambda g: (g, 0, 0)),
            pl.BlockSpec((1, rows), lambda g: (0, 0)),
            pl.BlockSpec((rows, 1), lambda g: (0, 0)),
        ],
        out_specs=[
            pl.BlockSpec((2, rows, rows), lambda g: (g, 0, 0)),
            pl.BlockSpec((rows, 128), lambda g: (0, g)),
            pl.BlockSpec((rows, 128), lambda g: (0, 0)),
        ],
        out_shape=[
            jax.ShapeDtypeStruct((heads, rows, rows), jnp.bfloat16),
            jax.ShapeDtypeStruct((rows, heads * 64), jnp.bfloat16),
            jax.ShapeDtypeStruct((rows, 128), jnp.float32),
        ],
        scratch_shapes=[pltpu.VMEM((rows, rows), jnp.float32)],
        compiler_params=pltpu.CompilerParams(vmem_limit_bytes=60 * 2**20),
        name="attn_fwd",
    )(qkv, qkv, qkv, prev, srow, scol)

def attn_bwd_kernel(BR, q_ref, k_ref, v_ref, do_ref, prev_ref, dl_ref, lse_ref, srow_ref, scol_ref,
                    dprev_ref, dq_ref, dk_ref, dv_ref, mask_ref, p_ref, g_ref):
    g = pl.program_id(0)
    rows = q_ref.shape[0]
    @pl.when(g == 0)
    def _():
        mask_ref[...] = jnp.where(scol_ref[...] == srow_ref[...], 0.0, NEG)
    k2 = k_ref[...]
    v2 = v_ref[...]
    left = half_masks(rows)
    zero = jnp.zeros_like(v2)
    for h in range(2):
        lm = left if h == 0 else ~left
        kh = jnp.where(lm, k2, zero)
        for rb in range(rows // BR):
            sl = pl.ds(rb * BR, BR)
            lb = half_masks(BR)
            lb = lb if h == 0 else ~lb
            q2 = q_ref[sl, :] * jnp.bfloat16(0.125)
            qh = jnp.where(lb, q2, jnp.zeros_like(q2))
            doh = jnp.where(lb, do_ref[sl, :], jnp.zeros_like(q2))
            lane = lax.broadcasted_iota(jnp.int32, (BR, 128), 1)
            lse = jnp.sum(jnp.where(lane == 2 * g + h, lse_ref[sl, :], 0.0), axis=1, keepdims=True)
            s = dotf(qh, k2, NT) + prev_ref[h, sl, :].astype(jnp.float32) + mask_ref[sl, :]
            p = jnp.exp(s - lse)
            dp = dotf(doh, v2, NT)
            delta = jnp.sum(p * dp, axis=1, keepdims=True)
            ds = p * (dp - delta)
            gt = (ds + dl_ref[h, sl, :].astype(jnp.float32)).astype(jnp.bfloat16)
            dprev_ref[h, sl, :] = gt
            p_ref[sl, :] = p.astype(jnp.bfloat16)
            dq = dotf(gt, kh, NN) * 0.125
            if h == 0:
                dq_ref[sl, :] = dq.astype(jnp.bfloat16)
            else:
                dq_ref[sl, :] = dq_ref[sl, :] + dq.astype(jnp.bfloat16)
        qh = jnp.where(lm, q_ref[...], zero)
        doh = jnp.where(lm, do_ref[...], zero)
        dk = (dotf(dprev_ref[h], qh, TN) * 0.125).astype(jnp.bfloat16)
        dv = dotf(p_ref[...], doh, TN).astype(jnp.bfloat16)
        if h == 0:
            dk_ref[...] = dk
            dv_ref[...] = dv
        else:
            dk_ref[...] = dk_ref[...] + dk
            dv_ref[...] = dv_ref[...] + dv

def attn_bwd(qkv, do, prev, dl, lse, seg, BR=128):
    rows = qkv.shape[0]
    heads = prev.shape[0]
    G = heads // 2
    srow = seg.reshape(1, rows); scol = seg.reshape(rows, 1)
    col = lambda off: pl.BlockSpec((rows, 128), lambda g: (0, off + g))
    return pl.pallas_call(
        functools.partial(attn_bwd_kernel, BR),
        grid=(G,),
        in_specs=[
            col(0), col(G), col(2 * G), col(0),
            pl.BlockSpec((2, rows, rows), lambda g: (g, 0, 0)),
            pl.BlockSpec((2, rows, rows), lambda g: (g, 0, 0)),
            pl.BlockSpec((rows, 128), lambda g: (0, 0)),
            pl.BlockSpec((1, rows), lambda g: (0, 0)),
            pl.BlockSpec((rows, 1), lambda g: (0, 0)),
        ],
        out_specs=[
            pl.BlockSpec((2, rows, rows), lambda g: (g, 0, 0)),
            col(0), col(0), col(0),
        ],
        out_shape=[
            jax.ShapeDtypeStruct((heads, rows, rows), jnp.bfloat16),
        ] + [jax.ShapeDtypeStruct((rows, heads * 64), jnp.bfloat16)] * 3,
        scratch_shapes=[pltpu.VMEM((rows, rows), jnp.float32), pltpu.VMEM((rows, rows), jnp.bfloat16), pltpu.VMEM((8, 128), jnp.float32)],
        compiler_params=pltpu.CompilerParams(vmem_limit_bytes=60 * 2**20),
        name="attn_bwd",
    )(qkv, qkv, qkv, do, prev, dl, lse, srow, scol)


MESH = pl.DeviceIdType.MESH


def coords():
    dp = lax.axis_index("dp"); fs = lax.axis_index("fsdp")
    y = dp // 2; c = lax.rem(dp, 2)
    z = fs // 2; x = lax.rem(fs, 2)
    return y, c, z, x

def dev(y, c, z, x):
    return (y * 2 + c, z * 2 + x)


ROUTES = "zzzzzzznnnn"
FORWARD_PLAN = {
    "start": [(1, 7), (1, 8), (1, 9), (1, 10), (1, 0), (2, 0), (1, 1), (3, 0)],
    ("q", 0): [(1, 2), (2, 1), (1, 3), (2, 2), (3, 1)],
    ("q", 1): [(2, 3), (1, 4), (3, 2)],
    ("q", 2): [(3, 3), (1, 5)],
    ("pair", 0): [(2, 4), (1, 6)],
    ("pair", 2): [(2, 5)],
    ("pair", 3): [(3, 4)],
    ("pair", 5): [(2, 6)],
    "out": [(3, 5), (2, 7), (3, 6), (2, 8)],
    "norm": [(3, 7), (2, 9)],
    ("up", 0): [(3, 8), (2, 10)],
    ("up", 1): [(3, 9)],
    ("up", 2): [(3, 10)],
}
BACKWARD_PLAN = {
    ("down", 1): [(2, 0)],
    ("down", 2): [(2, 1)],
    ("up", 2): [(3, 0)],
    ("down", 3): [(2, 2)],
    ("up", 3): [(3, 1)],
    "norm": [(4, 0), (2, 3)],
    ("out", 0): [(3, 2), (4, 1)],
    ("out", 2): [(3, 3), (2, 4), (4, 2), (5, 0)],
    ("head", 0): [(2, 5), (5, 1)],
    ("head", 1): [(4, 3), (2, 6)],
    ("head", 2): [(3, 4), (5, 2)],
    ("head", 4): [(3, 5), (2, 7), (5, 3)],
    ("head", 5): [(2, 8)],
    ("head", 6): [(4, 4), (3, 6)],
    ("head", 7): [(4, 5), (2, 9), (3, 7)],
    ("head", 8): [(3, 8)],
    ("head", 9): [(4, 6), (3, 9), (4, 7), (2, 10), (4, 8), (5, 4)],
    ("head", 10): [(4, 9), (5, 5), (3, 10)],
    ("head", 11): [(2, 11)],
    "end": [(4, 10), (5, 6), (5, 7)],
    ("dx", 0): [(3, 11), (5, 8)],
    ("dx", 1): [(2, 12), (2, 13), (5, 9)],
    "last": [(4, 11), (5, 10), (3, 12), (3, 13), (4, 12), (4, 13), (5, 11), (5, 12), (5, 13)],
}


class Gather:
    def __init__(self, chunks, routes, sources, wholes, send_sem, recv_sem):
        self.chunks, self.routes, self.sources, self.wholes = chunks, routes, sources, wholes
        self.send_sem, self.recv_sem = send_sem, recv_sem
        self.y, self.c, self.z, self.x = coords()

    def part(self, k):
        array, start, size, origin = self.chunks[k]
        return self.wholes[array], pl.ds(start, size), self.sources[array].at[:, pl.ds(origin, size)]

    def rows_of(self, k, x):
        size = self.sources[self.chunks[k][0]].shape[0]
        return pl.ds(pl.multiple_of(size * x, 8), size)

    def copy(self, src, dst, k, slot, who):
        return pltpu.make_async_remote_copy(
            src_ref=src, dst_ref=dst, send_sem=self.send_sem.at[k, slot], recv_sem=self.recv_sem.at[k, slot],
            device_id=who, device_id_type=MESH)

    def along_z(self, k):
        whole, cols, mine = self.part(k)
        spot = whole.at[self.y, self.c, self.z, self.rows_of(k, self.x), cols]
        return [self.copy(mine, spot, k, d, dev(self.y, self.c, lax.rem(self.z + d + 1, 4), self.x)) for d in range(3)]

    def across(self):
        return jnp.where(self.c == 0, self.y, 1 - self.y), jnp.where(self.c == 0, 1 - self.x, self.x)

    def other(self):
        return (jnp.where(self.c == 0, 1 - self.y, self.y) * 2 + self.c, self.z * 2 + jnp.where(self.c == 0, self.x, 1 - self.x))

    def block(self, k, y, x):
        whole, cols, _ = self.part(k)
        return whole.at[y, self.c, :, self.rows_of(k, x), cols]

    def to_neighbours(self, k):
        block = self.block(k, self.y, self.x)
        return [self.copy(block, block, k, 3, dev(self.y, self.c, self.z, 1 - self.x)),
                self.copy(block, block, k, 4, dev(1 - self.y, self.c, self.z, self.x))]

    def handed_on(self, k):
        block = self.block(k, *self.across())
        return self.copy(block, block, k, 3 + self.c, self.other()), self.copy(block, block, k, 5, self.other()), self.copy(block, block, k, 4 - self.c, self.other())

    def early(self, k):
        whole, cols, mine = self.part(k)
        y, x = self.across()
        return self.copy(mine, whole.at[self.y, self.c, self.z, self.rows_of(k, self.x), cols], k, 3, dev(y, self.c, self.z, x))

    def relayed(self, k):
        whole, cols, _ = self.part(k)
        y, x = self.across()
        spot = whole.at[y, self.c, self.z, self.rows_of(k, x), cols]
        return [self.copy(spot, spot, k, 4 + d, dev(self.y, self.c, lax.rem(self.z + d + 1, 4), self.x)) for d in range(3)]

    def halves(self, k):
        own, far = self.block(k, self.y, self.x), self.block(k, *self.across())
        return [self.copy(own, own, k, 7, self.other()), self.copy(far, far, k, 8, self.other())]

    def to_core(self, k):
        whole, cols, _ = self.part(k)
        plane = whole.at[:, self.c, :, :, cols]
        return self.copy(plane, plane, k, 9, dev(self.y, 1 - self.c, self.z, self.x))

    def start(self, k):
        if self.routes[k] == "n":
            self.early(k).start()
        for d in self.along_z(k):
            d.start()

    def s1(self, k):
        if self.routes[k] == "n":
            self.early(k).wait_recv()
            for d in self.relayed(k):
                d.start()
            return
        for d in self.along_z(k):
            d.wait_recv()
        for d in self.to_neighbours(k):
            d.start()

    def s2(self, k):
        if self.routes[k] == "n":
            for d in self.along_z(k) + self.relayed(k):
                d.wait_recv()
            for d in self.halves(k):
                d.start()
            return
        got, on, _ = self.handed_on(k)
        got.wait_recv()
        on.start()

    def s3(self, k):
        if self.routes[k] == "n":
            for d in self.halves(k):
                d.wait_recv()
        else:
            _, on, other = self.handed_on(k)
            other.wait_recv()
            on.wait_recv()
        self.to_core(k).start()

    def s4(self, k):
        self.to_core(k).wait_recv()

    def finish(self, k):
        if self.routes[k] == "n":
            sent = [self.early(k), *self.relayed(k), *self.halves(k)]
        else:
            sent = self.to_neighbours(k) + [self.handed_on(k)[1]]
        for d in self.along_z(k) + sent + [self.to_core(k)]:
            d.wait_send()


def peers_of(y, c, z, x):
    return [dev(y, c, lax.rem(z + d, 4), x) for d in (1, 2, 3)] + [dev(y, c, z, 1 - x), dev(1 - y, c, z, x), dev(y, 1 - c, z, x)]


def normalise(v):
    centered = v - jnp.mean(v, axis=1, keepdims=True)
    scaling = lax.rsqrt(jnp.mean(centered * centered, axis=1, keepdims=True) + norm_eps)
    return centered * scaling, scaling


def spread_columns(ref, shards, columns, rows, width):
    lane = lax.broadcasted_iota(jnp.int32, (rows, 128), 1)
    blocks = [jnp.zeros((rows, 128), jnp.float32) for _ in range(width // 128)]
    for d in range(shards):
        at, off = columns * d // 128, columns * d % 128
        tile = ref[d // 16, d // 8 % 2, d // 2 % 4, 16 * (d % 2):16 * (d % 2) + 16, :][:rows]
        tile = pltpu.roll(tile, off, 1) if off else tile
        if off + columns > 128:
            blocks[at + 1] = blocks[at + 1] + jnp.where(lane < off, tile, 0.0)
            tile = jnp.where(lane < off, 0.0, tile)
        blocks[at] = blocks[at] + tile
    return blocks


def forward_kernel(plan, routes, win_ref, wout_ref, vec_ref, srow_ref, prev_ref, x_hbm, dout_hbm,
                   logits_ref, gq_ref, gu_ref, go_ref, qkv_hbm, mixed_hbm, hlow_hbm, none_hbm, act_hbm, gp_hbm, mask_hbm,
                   small_ref, lse_ref, sone_ref, out_ref, dsec_ref, ddown_ref, sums_ref,
                   gv_ref, mask_ref, cin_ref, cout_ref, cvec_ref, w_ref, wo_ref, x_ref, dout_ref, qkv_ref, mixed_ref, hlow_ref, none_ref,
                   act_ref, gp_ref, hid_ref, sec_ref, send_sem, recv_sem, loc_sem, out_sem):
    g = pl.program_id(0)
    rows, width = x_hbm.shape
    hidden = act_hbm.shape[1]
    last = pl.num_programs(0) - 1
    tile = 256
    y, c, z, x = coords()
    V, Q, O, U = 0, 1, 4, 7
    chunks = [(3, 0, 128, 0)] + [(0, 768 * i, 768, 768 * i) for i in range(3)] + [(2, 256 * i, 256, 256 * i) for i in range(3)]
    chunks += [(1, 768 * i, 768, 3 * width + 768 * i) for i in range(4)]
    ga = Gather(chunks, routes, [cin_ref, cin_ref, cout_ref, cvec_ref], [gq_ref, gu_ref, go_ref, gv_ref], send_sem, recv_sem)

    def run(place):
        for stage, k in plan.get(place, ()):
            (ga.s1, ga.s2, ga.s3)[stage - 1](k)

    def load(src, dst, i):
        return pltpu.make_async_copy(src, dst, loc_sem.at[i])

    def save(src, dst, i):
        return pltpu.make_async_copy(src, dst, out_sem.at[i])

    stores = lambda: [load(cin_ref.at[:, pl.ds(0, 3 * width)], gq_ref.at[y, c, z, ga.rows_of(Q, x)], 0),
                      load(cin_ref.at[:, pl.ds(3 * width, hidden)], gu_ref.at[y, c, z, ga.rows_of(U, x)], 1),
                      load(cout_ref, go_ref.at[y, c, z, ga.rows_of(O, x)], 2)]
    x_in, dout_in = lambda: load(x_hbm, x_ref, 3), lambda: load(dout_hbm, dout_ref, 4)
    w_out, w_up, w_qkv = go_ref.reshape(width + hidden, width), gu_ref.reshape(width, hidden), gq_ref.reshape(width, 3 * width)
    w_q = lambda k: load(w_qkv.at[:, pl.ds(768 * k, 768)], w_ref.at[k % 2], 5 + k % 2)
    w_u = lambda k: load(w_up.at[:, pl.ds(768 * k, 768)], w_ref.at[(k + 1) % 2], 5 + (k + 1) % 2)
    w_o = lambda: load(w_out.at[pl.ds(0, width), :], w_ref.at[0], 5)
    w_down = lambda: load(w_out.at[pl.ds(width, hidden), :], wo_ref, 7)
    saves = {"mask": lambda: save(mask_ref, mask_hbm, 0), "mixed": lambda: save(mixed_ref, mixed_hbm, 1), "hlow": lambda: save(hlow_ref, hlow_hbm, 2),
             "none": lambda: save(none_ref, none_hbm, 3), "qkv": lambda: save(qkv_ref, qkv_hbm, 4)}
    save_act = lambda k: save(act_ref.at[:, pl.ds(768 * k, 768)], act_hbm.at[:, pl.ds(768 * k, 768)], 5 + k)
    save_gp = lambda k: save(gp_ref.at[k % 2], gp_hbm.at[:, pl.ds(768 * k, 768)], 9 + k)

    @pl.when(g == 0)
    def _():
        barrier = pltpu.get_barrier_semaphore()
        peers = peers_of(y, c, z, x)
        for p in peers:
            pl.semaphore_signal(barrier, inc=1, device_id=p, device_id_type=MESH)
        cvec_ref[...] = jnp.zeros_like(cvec_ref)
        vec = vec_ref[...].astype(jnp.bfloat16).astype(jnp.float32)
        cvec_ref[0:vec.shape[0], 0:vec.shape[1]] = vec
        gv_ref[y, c, z, ga.rows_of(V, x), :] = cvec_ref[...]
        cin_ref[...] = win_ref[...].astype(jnp.bfloat16)
        cout_ref[...] = wout_ref[...].astype(jnp.bfloat16)
        pl.semaphore_wait(barrier, len(peers))
        for k in range(len(chunks)):
            ga.start(k)
        for s in stores():
            s.start()
        x_in().start()
        lse_ref[...] = jnp.zeros_like(lse_ref)
        seg = jnp.broadcast_to(srow_ref[...].astype(jnp.float32), (rows, rows))
        mask_ref[...] = jnp.where(seg == seg.T, 0.0, NEG)
        for s in stores():
            s.wait()
        saves["mask"]().start()
        dout_in().start()
        run("start")
        ga.s4(V)
        run("small")
        spread = spread_columns(gv_ref, 32, vec_ref.shape[1], vec_ref.shape[0], width)
        for i, v in enumerate(spread):
            small_ref[:, 128 * i:128 * (i + 1)] = v
        x_in().wait()
        for k in range(3):
            run(("q", k))
            ga.s4(Q + k)
            w_q(k).start()
            run(("qw", k))
            w_q(k).wait()
            for j in range(768 // tile):
                v = dotf(x_ref[...], w_ref[k % 2, :, j * tile:(j + 1) * tile], NN)
                if k != 1:
                    row = 4 if k == 0 else 5
                    v = v + small_ref[row:row + 1, j * tile:(j + 1) * tile]
                qkv_ref[:, 768 * k + j * tile:768 * k + (j + 1) * tile] = v.astype(jnp.bfloat16)
        saves["qkv"]().start()

    for i in range(6):
        if plan.get(("pair", i)):
            @pl.when(g == i)
            def _():
                run(("pair", i))

    at = lambda off: pl.ds(pl.multiple_of(off * width + g * 128, 128), 128)
    left = half_masks(rows)
    q2 = qkv_ref[:, at(0)] * jnp.bfloat16(0.125)
    k2 = qkv_ref[:, at(1)]
    v2 = qkv_ref[:, at(2)]
    zero = jnp.zeros_like(v2)
    outs, logs = [], []
    for h in range(2):
        pick = (lambda v: jnp.where(left, v, zero)) if h == 0 else (lambda v: jnp.where(left, zero, v))
        raw = dotf(pick(q2), k2, NT) + prev_ref[h].astype(jnp.float32)
        logits_ref[h] = raw.astype(jnp.bfloat16)
        s = raw + mask_ref[...]
        m = jnp.max(s, axis=1, keepdims=True)
        e = jnp.exp(s - m)
        tot = jnp.sum(e, axis=1, keepdims=True)
        outs.append(dotf(e.astype(jnp.bfloat16), pick(v2), NN) / tot)
        logs.append(m + jnp.log(tot))
    mixed_ref[:, pl.ds(pl.multiple_of(g * 128, 128), 128)] = (outs[0] + outs[1]).astype(jnp.bfloat16)
    lane = lax.broadcasted_iota(jnp.int32, (rows, 128), 1)
    lse_ref[...] = jnp.where(lane == 2 * g, logs[0], jnp.where(lane == 2 * g + 1, logs[1], lse_ref[...]))

    @pl.when(g == last)
    def _():
        saves["mixed"]().start()
        run("out")
        for k in range(3):
            ga.s4(O + k)
        w_o().start()
        w_down().start()
        run("outw")
        w_o().wait()
        for j in range(width // tile):
            sl = slice(j * tile, (j + 1) * tile)
            hid_ref[:, sl] = x_ref[:, sl].astype(jnp.float32) + (dotf(mixed_ref[...], w_ref[0, :, sl], NN) + small_ref[6:7, sl])
        run("norm")

        @pl.loop(0, rows // 128)
        def _(i):
            sl = pl.ds(pl.multiple_of(i * 128, 128), 128)
            normed, scaling = normalise(hid_ref[sl, :])
            none_ref[sl, :] = normed
            sone_ref[sl, :] = jnp.broadcast_to(scaling, (128, 128))
            hid = normed * small_ref[0:1, :] + small_ref[2:3, :]
            hid_ref[sl, :] = hid
            hlow_ref[sl, :] = hid.astype(jnp.bfloat16)

        saves["none"]().start()
        saves["hlow"]().start()
        for k in range(4):
            run(("up", k))
            ga.s4(U + k)
            w_u(k).start()
            run(("upw", k))
            w_u(k).wait()
            if k >= 2:
                save_gp(k - 2).wait()

            @pl.loop(0, 768 // tile)
            def _(j):
                sl = pl.ds(pl.multiple_of(j * tile, tile), tile)
                to = pl.ds(pl.multiple_of(768 * k + j * tile, tile), tile)
                u = dotf(hlow_ref[...], w_ref[(k + 1) % 2, :, sl], NN) + small_ref[8 + k:9 + k, sl]
                cdf = 0.5 * (1.0 + lax.erf(u * math.sqrt(0.5)))
                act_ref[:, to] = (u * cdf).astype(jnp.bfloat16)
                gp_ref[k % 2, :, sl] = (cdf + u * (jnp.exp(-0.5 * (u * u)) * (1.0 / math.sqrt(2.0 * math.pi)))).astype(jnp.bfloat16)
            save_act(k).start()
            save_gp(k).start()
        w_down().wait()
        for j in range(width // tile):
            sl = slice(j * tile, (j + 1) * tile)
            sec_ref[:, sl] = hid_ref[:, sl] + (dotf(act_ref[...], wo_ref[:, sl], NN) + small_ref[7:8, sl])
        sums_ref[...] = jnp.zeros_like(sums_ref)
        dout_in().wait()

        @pl.loop(0, rows // 128)
        def _(i):
            sl = pl.ds(pl.multiple_of(i * 128, 128), 128)
            normed, scaling = normalise(sec_ref[sl, :])
            out_ref[sl, :] = (normed * small_ref[1:2, :] + small_ref[3:4, :]).astype(jnp.bfloat16)
            dy = dout_ref[sl, :].astype(jnp.float32)
            back = norm_back(dy, normed, scaling, small_ref[1:2, :])
            low = back.astype(jnp.bfloat16)
            dsec_ref[sl, :] = back
            ddown_ref[sl, :] = low
            sums_ref[0:1, :] += jnp.sum(dy * normed, axis=0, keepdims=True)
            sums_ref[1:2, :] += jnp.sum(dy, axis=0, keepdims=True)
            sums_ref[2:3, :] += jnp.sum(low.astype(jnp.float32), axis=0, keepdims=True)
        for k in range(len(chunks)):
            ga.finish(k)
        for s in saves.values():
            s().wait()
        for k in range(4):
            save_act(k).wait()
        for k in (2, 3):
            save_gp(k).wait()


def forward_all(plan, routes, tokens, grad_out, weight_in, weight_out, vectors, prev, seg):
    rows, width = tokens.shape
    heads = prev.shape[0]
    hidden = weight_in.shape[1] - 3 * width
    f32, bf16 = jnp.float32, jnp.bfloat16
    fixed = lambda shape: pl.BlockSpec(shape, lambda g: (0,) * len(shape), pipeline_mode=pl.Buffered(1))
    pair = pl.BlockSpec((2, rows, rows), lambda g: (g, 0, 0))
    hbm = pl.BlockSpec(memory_space=pl.ANY)
    far = [((2, 2, 4, 2 * weight_in.shape[0], 3 * width), bf16), ((2, 2, 4, 2 * weight_in.shape[0], hidden), bf16),
           ((2, 2, 4, 2 * weight_out.shape[0], width), bf16), ((rows, 3 * width), bf16), ((rows, width), bf16), ((rows, width), bf16),
           ((rows, width), f32), ((rows, hidden), bf16), ((rows, hidden), bf16), ((rows, rows), f32)]
    near = [((vectors.shape[0], width), f32), ((rows, 128), f32), ((rows, 128), f32), ((rows, width), bf16), ((rows, width), f32),
            ((rows, width), bf16), ((8, width), f32)]
    v = lambda *shape: pltpu.VMEM(shape, bf16)
    vf = lambda *shape: pltpu.VMEM(shape, f32)
    dma = pltpu.SemaphoreType.DMA
    return pl.pallas_call(
        functools.partial(forward_kernel, plan, routes),
        grid=(heads // 2,),
        in_specs=[fixed(weight_in.shape), fixed(weight_out.shape), fixed(vectors.shape), fixed((1, rows)), pair, hbm, hbm],
        out_specs=[pair] + [hbm] * len(far) + [fixed(s) for s, _ in near],
        out_shape=[jax.ShapeDtypeStruct(prev.shape, bf16)] + [jax.ShapeDtypeStruct(s, t) for s, t in far + near],
        scratch_shapes=[
            vf(2, 2, 4, 32, 128), vf(rows, rows), v(*weight_in.shape), v(*weight_out.shape), vf(16, 128), v(2, width, 768), v(hidden, width),
            v(rows, width), v(rows, width), v(rows, 3 * width), v(rows, width), v(rows, width), vf(rows, width), v(rows, hidden),
            v(2, rows, 768), vf(rows, width), vf(rows, width), dma((11, 10)), dma((11, 10)), dma((8,)), dma((13,))],
        compiler_params=pltpu.CompilerParams(collective_id=1, has_side_effects=True, vmem_limit_bytes=64 * 2**20 - 65536),
        name="forward",
    )(weight_in, weight_out, vectors, seg.reshape(1, rows), prev, tokens, grad_out)


class Scatter:
    def __init__(self, full, got, send_sem, recv_sem):
        self.full, self.got = full, got
        self.send_sem, self.recv_sem = send_sem, recv_sem
        y, c, z, x = self.y, self.c, self.z, self.x = coords()
        first, second = (1 - y) * 2 + c, z * 2 + 1 - x
        self.core = dev(y, 1 - c, z, x)
        self.one = (jnp.where(c == 0, first, y * 2 + c), jnp.where(c == 0, z * 2 + x, second))
        self.two = (jnp.where(c == 0, y * 2 + c, first), jnp.where(c == 0, second, z * 2 + x))
        self.at_one = (jnp.where(c == 0, 1 - y, y), jnp.where(c == 0, x, 1 - x))
        self.at_two = (jnp.where(c == 0, y, 1 - y), jnp.where(c == 0, 1 - x, x))

    def copy(self, src, dst, k, slot, who):
        return pltpu.make_async_remote_copy(
            src_ref=src, dst_ref=dst, send_sem=self.send_sem.at[k, slot], recv_sem=self.recv_sem.at[k, slot],
            device_id=who, device_id_type=MESH)

    def to_core(self, k):
        return self.copy(self.full[k]().at[:, 1 - self.c], self.got[k][0], k, 0, self.core)

    def to_one(self, k):
        full = self.full[k]()
        return [self.copy(full.at[1 - self.y, self.c, :, 1 - self.x], self.got[k][1].at[0], k, 1, self.one),
                self.copy(full.at[self.at_one[0], self.c, :, self.at_one[1]], self.got[k][1].at[1], k, 2, self.one)]

    def to_two(self, k):
        return self.copy(self.full[k]().at[self.at_two[0], self.c, :, self.at_two[1]], self.got[k][2], k, 3, self.two)

    def along_z(self, k):
        full = self.full[k]()
        out = []
        for i in range(3):
            z = lax.rem(self.z + i + 1, 4)
            out.append(self.copy(full.at[self.y, self.c, z, self.x], self.got[k][3].at[i], k, 4 + i, dev(self.y, self.c, z, self.x)))
        return out

    def r1(self, k):
        self.to_core(k).start()

    def r2(self, k):
        full, got = self.full[k](), self.got[k][0]
        self.to_core(k).wait_recv()

        @pl.loop(0, 8)
        def _(i):
            for y in range(2):
                z, x = i // 2, lax.rem(i, 2)
                total = full[y, self.c, z, x].astype(jnp.float32) + got[y, z, x].astype(jnp.float32)
                full[y, self.c, z, x] = total.astype(full.dtype)
        for d in self.to_one(k):
            d.start()

    def r3(self, k):
        full, got = self.full[k](), self.got[k][1]
        for d in self.to_one(k):
            d.wait_recv()
        y, x = self.at_two

        @pl.loop(0, 4)
        def _(z):
            total = full[y, self.c, z, x].astype(jnp.float32) + got[0, z].astype(jnp.float32)
            full[y, self.c, z, x] = total.astype(full.dtype)
        self.to_two(k).start()

    def r4(self, k):
        full = self.full[k]()
        self.to_two(k).wait_recv()

        @pl.loop(0, 4)
        def _(z):
            total = full[self.y, self.c, z, self.x].astype(jnp.float32) + self.got[k][1][1, z].astype(jnp.float32)
            total = total + self.got[k][2][z].astype(jnp.float32)
            full[self.y, self.c, z, self.x] = total.astype(full.dtype)
        for d in self.along_z(k):
            d.start()

    def r5(self, k):
        for d in self.along_z(k):
            d.wait_recv()
        total = self.full[k]()[self.y, self.c, self.z, self.x].astype(jnp.float32)
        for i in range(3):
            total = total + self.got[k][3][i].astype(jnp.float32)
        return total

    def finish(self, k):
        for d in [self.to_core(k), *self.to_one(k), self.to_two(k), *self.along_z(k)]:
            d.wait_send()


def put_rows(ref, start, value, columns):
    size, count = ref.shape[4], value.shape[0]
    for d in range(start // size, (start + count - 1) // size + 1):
        low, high = max(start, d * size), min(start + count, (d + 1) * size)
        ref[d // 16, d // 8 % 2, d // 2 % 4, d % 2, low - d * size:high - d * size, :, columns] = value[low - start:high - start]


def own_columns(value, shards, columns):
    for d in range(shards):
        at, off = columns * d // 128, columns * d % 128
        if off + columns <= 128:
            tile = value[:, 128 * at:128 * (at + 1)]
            yield d, pltpu.roll(tile, 128 - off, 1) if off else tile
        else:
            yield d, pltpu.roll(value[:, 128 * at:128 * (at + 2)], 256 - off, 1)[:, :128]


def backward_kernel(heads, plan, columns, *refs):
    (ddown_ref, hlow_ref, small_ref, two_ref, lse_ref, sone_ref, prev_ref, dl_ref,
     act_hbm, gp_hbm, go_hbm, gu_hbm, gq_hbm, dsec_hbm, none_hbm, mixed_hbm, x_hbm, qkv_hbm, mask_hbm,
     dprev_ref, dx_ref, gin_ref, gout_ref, gvec_ref, norm_ref) = refs[:25]
    (mask_ref, p_ref, qkv_ref, do_ref, x_ref, mixed_ref, act_ref, gp_ref, dup_ref, w0_ref, w1_ref, w2_ref, acc_ref, none_ref,
     part_ref, fvec_ref) = refs[25:41]
    ups, outs = refs[41:45], refs[45:48]
    got_flat = refs[48:104]
    nmine, ngot, send_sem, recv_sem, loc_sem, ns_sem, nr_sem = refs[104:]
    g = pl.program_id(0)
    rows, width = ddown_ref.shape
    hidden = act_hbm.shape[1]
    tile = 256
    U, O, Q, V = 0, 4, 7, 13
    got = [got_flat[4 * k:4 * k + 4] for k in range(14)]
    full = [lambda r=r: r for r in ups] + [lambda r=r: r for r in outs]
    full += [lambda r=ups[p // 2], at=384 * (p % 2): r.at[:, :, :, :, :, :, pl.ds(at, 384)] for p in range(6)] + [lambda: fvec_ref]
    sc = Scatter(full, got, send_sem, recv_sem)
    y, c, z, x = coords()
    peers = peers_of(y, c, z, x)
    stages = {1: sc.r1, 2: sc.r2, 3: sc.r3, 4: sc.r4}

    def run(place):
        for stage, k in plan.get(place, ()):
            if stage == 5:
                finish(k)
            else:
                stages[stage](k)

    def finish(k):
        total = sc.r5(k)
        if k < O:
            gin_ref[:, :, 3 * width + 768 * k:3 * width + 768 * (k + 1)] = total
        elif k < Q:
            gout_ref[:, :, 256 * (k - O):256 * (k - O + 1)] = total
        elif k < V:
            for i in range(3):
                gin_ref[:, :, width * i + 128 * (k - Q):width * i + 128 * (k - Q + 1)] = total[:, :, 128 * i:128 * (i + 1)]
        else:
            lane = lax.broadcasted_iota(jnp.int32, total.shape, 1)
            gvec_ref[...] = jnp.where(lane < columns, total, 0.0)

    def load(src, dst, i):
        return pltpu.make_async_copy(src, dst, loc_sem.at[i])

    near = [dev(lax.rem(y + i // 4, 2), lax.rem(c + i // 2 % 2, 2), z, lax.rem(x + i % 2, 2)) for i in range(1, 8)]
    far = [dev(y, c, lax.rem(z + i, 4), x) for i in (1, 2, 3)]

    def share(i):
        return pltpu.make_async_remote_copy(
            src_ref=nmine.at[0 if i < 7 else 1], dst_ref=ngot.at[i], send_sem=ns_sem.at[i], recv_sem=nr_sem.at[i],
            device_id=(near + far)[i], device_id_type=MESH)

    def in_order(values, index):
        total = jnp.zeros_like(values[0])
        for at in range(len(values)):
            for i, v in enumerate(values):
                total = total + jnp.where(index(i) == at, v, 0.0)
        return total

    w_out, w_up, w_qkv = go_hbm.reshape(width + hidden, width), gu_hbm.reshape(width, hidden), gq_hbm.reshape(width, 3 * width)
    late = lambda: [load(dsec_hbm, acc_ref, 0), load(none_hbm, none_ref, 1), load(mixed_hbm, mixed_ref, 2), load(x_hbm, x_ref, 3),
                    load(qkv_hbm, qkv_ref, 4), load(mask_hbm, mask_ref, 9), load(act_hbm, act_ref, 8)]
    last_w = lambda: [load(w_qkv.at[:, pl.ds(768 * i, 768)], w, 5 + i) for i, w in enumerate((w0_ref, w1_ref, w2_ref))]

    @pl.when(g == 0)
    def _():
        barrier = pltpu.get_barrier_semaphore()
        met = far + near
        for p in met:
            pl.semaphore_signal(barrier, inc=1, device_id=p, device_id_type=MESH)

        def ahead(k):
            return [load(w_out.at[pl.ds(width + 768 * k, 768), :], w0_ref, 5), load(gp_hbm.at[:, pl.ds(768 * k, 768)], gp_ref, 6)]

        def behind(k):
            return [load(w_up.at[:, pl.ds(768 * k, 768)], w1_ref, 7)]
        for d in ahead(0) + behind(0) + late():
            d.start()
        part_ref[...] = jnp.zeros_like(part_ref)
        part_ref[1:2, :] = two_ref[0:1, :]
        part_ref[3:4, :] = two_ref[1:2, :]
        part_ref[7:8, :] = two_ref[2:3, :]
        pl.semaphore_wait(barrier, len(met))
        for k in range(4):
            for d in ahead(k):
                d.wait()

            @pl.loop(0, 768 // tile)
            def _(j):
                sl = pl.ds(pl.multiple_of(j * tile, tile), tile)
                grad = dotf(ddown_ref[...], w0_ref[sl, :], NT) * gp_ref[:, sl].astype(jnp.float32)
                low = grad.astype(jnp.bfloat16)
                dup_ref[:, sl] = low
                part_ref[8 + k:9 + k, sl] = jnp.sum(low.astype(jnp.float32), axis=0, keepdims=True)
                ups[k][:, :, :, :, :, :, sl] = dotf(hlow_ref[...], low, TN).reshape(ups[k].shape[:6] + (tile,)).astype(jnp.bfloat16)
            sc.r1(U + k)
            if k < 3:
                for d in ahead(k + 1):
                    d.start()
            run(("down", k))
            if k == 0:
                late()[0].wait()
            for d in behind(k):
                d.wait()
            for j in range(3):
                sl = slice(j * tile, (j + 1) * tile)
                acc_ref[:, sl] += dotf(dup_ref[...], w1_ref[sl, :], NT)
            if k < 3:
                for d in behind(k + 1):
                    d.start()
            run(("up", k))
        wo = load(w_out.at[pl.ds(0, width), :], w0_ref, 5)
        wo.start()
        late()[1].wait()

        @pl.loop(0, rows // 128)
        def _(i):
            sl = pl.ds(pl.multiple_of(i * 128, 128), 128)
            one, normed = acc_ref[sl, :], none_ref[sl, :]
            part_ref[0:1, :] += jnp.sum(one * normed, axis=0, keepdims=True)
            part_ref[2:3, :] += jnp.sum(one, axis=0, keepdims=True)
            back = norm_back(one, normed, sone_ref[sl, 0:1], small_ref[0:1, :])
            low = back.astype(jnp.bfloat16)
            acc_ref[sl, :] = back
            dup_ref[sl, :] = low
            part_ref[6:7, :] += jnp.sum(low.astype(jnp.float32), axis=0, keepdims=True)
        run("norm")
        late()[2].wait()
        late()[6].wait()
        for j in range(3):
            sl = slice(j * tile, (j + 1) * tile)
            put_rows(outs[j], 0, dotf(mixed_ref[...], dup_ref[:, sl], TN).reshape(96, 8, tile).astype(jnp.bfloat16), slice(None))
            for k in range(4):
                part = dotf(act_ref[:, 768 * k:768 * (k + 1)], ddown_ref[:, sl], TN)
                put_rows(outs[j], (width + 768 * k) // 8, part.reshape(96, 8, tile).astype(jnp.bfloat16), slice(None))
            sc.r1(O + j)
            run(("out", j))
        wo.wait()
        for j in range(3):
            sl = slice(j * tile, (j + 1) * tile)
            do_ref[:, sl] = dotf(dup_ref[...], w0_ref[sl, :], NT).astype(jnp.bfloat16)
        for d in late()[3:6]:
            d.wait()
        for d in last_w():
            d.start()

    for i in range(heads):
        if plan.get(("head", i)):
            @pl.when(g == i)
            def _():
                run(("head", i))

    pair, half = g // 2, lax.rem(g, 2)
    at = lambda off: pl.ds(pl.multiple_of(off * width + pair * 128, 128), 128)
    lane = lax.broadcasted_iota(jnp.int32, (rows, 128), 1)
    pick = lambda v: jnp.where(lane // 64 == half, v, jnp.zeros_like(v))
    q2, k2, v2, do2 = qkv_ref[:, at(0)], qkv_ref[:, at(1)], qkv_ref[:, at(2)], do_ref[:, at(0)]
    lse = jnp.sum(jnp.where(lane == g, lse_ref[...], 0.0), axis=1, keepdims=True)
    s = dotf(pick(q2) * jnp.bfloat16(0.125), k2, NT) + prev_ref[0].astype(jnp.float32) + mask_ref[...]
    p = jnp.exp(s - lse)
    dp = dotf(pick(do2), v2, NT)
    ds = p * (dp - jnp.sum(p * dp, axis=1, keepdims=True))
    grad = (ds + dl_ref[0].astype(jnp.float32)).astype(jnp.bfloat16)
    dprev_ref[0] = grad
    p_ref[...] = p.astype(jnp.bfloat16)
    dq = (dotf(grad, pick(k2), NN) * 0.125).astype(jnp.bfloat16)
    dk = (dotf(dprev_ref[0], pick(q2), TN) * 0.125).astype(jnp.bfloat16)
    dv = dotf(p_ref[...], pick(do2), TN).astype(jnp.bfloat16)

    @pl.when(half == 0)
    def _():
        for i, v in enumerate((dq, dk, dv)):
            gp_ref[:, 128 * i:128 * (i + 1)] = v

    @pl.when(half == 1)
    def _():
        for i, v in enumerate((dq, dk, dv)):
            v = gp_ref[:, 128 * i:128 * (i + 1)] + v
            gp_ref[:, 128 * i:128 * (i + 1)] = v
            qkv_ref[:, at(i)] = v
            if i != 1:
                part_ref[4 + i // 2:5 + i // 2, at(0)] = jnp.sum(v.astype(jnp.float32), axis=0, keepdims=True)
        for p in range(heads // 2):
            @pl.when(pair == p)
            def _():
                if p % 2 == 0:
                    sc.finish(U + p // 2)
                for i in range(3):
                    dst = ups[p // 2]
                    to = 384 * (p % 2) + 128 * i
                    v = dotf(x_ref[...], gp_ref[:, 128 * i:128 * (i + 1)], TN)
                    dst[:, :, :, :, :, :, to:to + 128] = v.reshape(dst.shape[:6] + (128,)).astype(jnp.bfloat16)
                sc.r1(Q + p)

    @pl.when(g == heads - 1)
    def _():
        for d, tile_of in own_columns(part_ref[...], 32, columns):
            fvec_ref[d // 16, d // 8 % 2, d // 2 % 4, d % 2] = tile_of
        sc.r1(V)
        run("end")
        for d in last_w():
            d.wait()
        ws = (w0_ref, w1_ref, w2_ref)
        for j in range(3):
            sl = slice(j * tile, (j + 1) * tile)
            total = acc_ref[:, sl]
            for i in range(3):
                total = total + dotf(qkv_ref[:, 768 * i:768 * (i + 1)], ws[i][sl, :], NT)
            dx_ref[:, sl] = total.astype(jnp.bfloat16)
            run(("dx", j))
        run("last")
        squares = gvec_ref[0:8, :] * gvec_ref[0:8, :] + gvec_ref[8:16, :] * gvec_ref[8:16, :]
        for ref in (gin_ref, gout_ref):
            v = ref[...]
            v = jnp.sum(v * v, axis=0)
            for j in range(v.shape[1] // 128):
                squares = squares + v[:, 128 * j:128 * (j + 1)]
        nmine[0] = jnp.sum(squares, keepdims=True) + jnp.zeros((8, 128), jnp.float32)
        for i in range(7):
            share(i).start()
        for k in range(14):
            if k not in (0, 1, 2):
                sc.finish(k)
        for i in range(7):
            share(i).wait_recv()
        me = y * 4 + c * 2 + x

        def from_near(i):
            return me if i == 0 else lax.rem(y + i // 4, 2) * 4 + lax.rem(c + i // 2 % 2, 2) * 2 + lax.rem(x + i % 2, 2)
        plane = in_order([nmine[0]] + [ngot[i] for i in range(7)], from_near)
        nmine[1] = plane
        for i in range(7, 10):
            share(i).start()
        for i in range(7, 10):
            share(i).wait_recv()
        total = in_order([plane] + [ngot[i] for i in range(7, 10)], lambda i: lax.rem(z - i + 4, 4))
        norm_ref[...] = jnp.sqrt(total)
        for i in range(10):
            share(i).wait_send()


def backward_all(plan, columns, grad_down, hidden_low, small, two_sums, log_sums, scale_one, prev, grad_logits,
                 activated, slope, full_out, full_up, full_qkv, grad_second, normed_one, mixed, tokens, qkv, mask):
    rows, width = tokens.shape
    heads = prev.shape[0]
    hidden = activated.shape[1]
    f32, bf16 = jnp.float32, jnp.bfloat16
    fixed = lambda shape: pl.BlockSpec(shape, lambda g: (0,) * len(shape), pipeline_mode=pl.Buffered(1))
    head = pl.BlockSpec((1, rows, rows), lambda g: (g, 0, 0))
    hbm = pl.BlockSpec(memory_space=pl.ANY)
    r_in, r_out = full_qkv.shape[3] // 2, full_out.shape[3] // 2
    landing = []
    for r, n in [(r_in, 768)] * 4 + [(r_out, 256)] * 3 + [(r_in, 384)] * 6:
        landing += [pltpu.VMEM(lead + (r // 8, 8, n), bf16) for lead in ((2, 4, 2), (2, 4), (4,), (3,))]
    landing += [pltpu.VMEM(lead + (16, 128), f32) for lead in ((2, 4, 2), (2, 4), (4,), (3,))]
    lead = (2, 2, 4, 2)
    v = lambda *shape: pltpu.VMEM(shape, bf16)
    vf = lambda *shape: pltpu.VMEM(shape, f32)
    shapes = [((r_in // 8, 8, 3 * width + hidden), f32), ((r_out // 8, 8, width), f32), ((16, 128), f32), ((8, 128), f32)]
    dma = pltpu.SemaphoreType.DMA
    return pl.pallas_call(
        functools.partial(backward_kernel, heads, plan, columns),
        grid=(heads,),
        in_specs=[fixed((rows, width)), fixed((rows, width)), fixed(small.shape), fixed(two_sums.shape), fixed(log_sums.shape),
                  fixed(scale_one.shape), head, head] + [hbm] * 11,
        out_specs=[head, fixed((rows, width))] + [fixed(s) for s, _ in shapes],
        out_shape=[jax.ShapeDtypeStruct(prev.shape, bf16), jax.ShapeDtypeStruct((rows, width), bf16)]
        + [jax.ShapeDtypeStruct(s, t) for s, t in shapes],
        scratch_shapes=[vf(rows, rows), v(rows, rows), v(rows, 3 * width), v(rows, width), v(rows, width), v(rows, width), v(rows, hidden),
                        v(rows, 768), v(rows, 768), v(768, width), v(768, width), v(768, width), vf(rows, width), vf(rows, width),
                        vf(16, width), vf(*lead, 16, 128)]
        + [v(*lead, r_in // 8, 8, 768)] * 4 + [v(*lead, r_out // 8, 8, 256)] * 3 + landing
        + [vf(2, 8, 128), vf(10, 8, 128), dma((14, 7)), dma((14, 7)), dma((10,)), dma((10,)), dma((10,))],
        compiler_params=pltpu.CompilerParams(collective_id=2, has_side_effects=True, vmem_limit_bytes=64 * 2**20 - 65536),
        name="backward",
    )(grad_down, hidden_low, small, two_sums, log_sums, scale_one, prev, grad_logits,
      activated, slope, full_out, full_up, full_qkv, grad_second, normed_one, mixed, tokens, qkv, mask)


def update_kernel(norm_ref, step_ref, *refs):
    through, refs = refs[:4], refs[4:]
    trios, refs = [refs[4 * i:4 * i + 4] for i in range(3)], refs[12:]
    through_out, refs = refs[:4], refs[4:]
    outs, gn_ref = [refs[5 * i:5 * i + 5] for i in range(3)], refs[15]
    for a, b in zip(through, through_out):
        b[...] = a[...]
    norm = norm_ref[0:1, 0:1]
    gn_ref[...] = norm
    factor = jnp.minimum(1.0, clip_scale * math.sqrt(PARAMS) / (norm + 1e-06))
    step = jnp.full((1, 1), step_ref[0], jnp.int32).astype(jnp.float32)
    one = 1.0 - jnp.exp(step * math.log(beta_one))
    two = 1.0 - jnp.exp(step * math.log(beta_two))
    for i, ((g_ref, w_ref, m_ref, v_ref), out) in enumerate(zip(trios, outs)):
        rate, decay = (rate_vector, 0.0) if i == 2 else (rate_matrix, decay_matrix)
        grad = g_ref[...].reshape(w_ref.shape) if i < 2 else g_ref[0:w_ref.shape[0], 0:w_ref.shape[1]]
        clipped = grad * factor
        moment = beta_one * m_ref[...] + (1.0 - beta_one) * clipped
        square = beta_two * v_ref[...] + (1.0 - beta_two) * clipped * clipped
        weight = w_ref[...] - rate * ((moment / one) / (jnp.sqrt(square / two) + adam_eps) + decay * w_ref[...])
        for ref, val in zip(out, (clipped, moment, square, weight, weight.astype(jnp.bfloat16))):
            ref[...] = val


def update_all(norm, step_count, through, trios):
    steps = 6
    f32 = jnp.float32

    def spec(a):
        if a.shape[-1] < 128 * steps:
            return pl.BlockSpec(a.shape, lambda g: (0,) * a.ndim)
        return pl.BlockSpec(a.shape[:-1] + (a.shape[-1] // steps,), lambda g: (0,) * (a.ndim - 1) + (g,))
    slabs = [pl.BlockSpec((a.shape[0] // steps,) + a.shape[1:], lambda g: (g, 0, 0)) if a.ndim == 3 else spec(a) for a in through]
    shapes = []
    for g, w, m, v in trios:
        shapes += [jax.ShapeDtypeStruct(w.shape, t) for t in (f32, f32, f32, f32, jnp.bfloat16)]
    flat = [a for trio in trios for a in trio]
    return pl.pallas_call(
        update_kernel,
        grid=(steps,),
        in_specs=[pl.BlockSpec((8, 128), lambda g: (0, 0)), pl.BlockSpec(memory_space=pltpu.SMEM)] + slabs + [spec(a) for a in flat],
        out_specs=slabs + [spec(s) for s in shapes] + [pl.BlockSpec((1, 1), lambda g: (0, 0))],
        out_shape=[jax.ShapeDtypeStruct(a.shape, a.dtype) for a in through] + shapes + [jax.ShapeDtypeStruct((1, 1), f32)],
        compiler_params=pltpu.CompilerParams(vmem_limit_bytes=64 * 2**20 - 65536),
        name="update",
    )(norm, step_count, *through, *flat)


def adam_update(master, moment, square, gradient, factor, step_value, step_rate, decay_rate):
    clipped = gradient * factor
    new_moment = beta_one * moment + (1.0 - beta_one) * clipped
    new_square = beta_two * square + (1.0 - beta_two) * clipped * clipped
    fixed_moment = new_moment / (1.0 - jnp.power(beta_one, step_value))
    fixed_square = new_square / (1.0 - jnp.power(beta_two, step_value))
    updated = master - step_rate * (
        fixed_moment / (jnp.sqrt(fixed_square) + adam_eps) + decay_rate * master
    )
    return (clipped, new_moment, new_square, updated)


def rounded(v):
    return lax.reduce_precision(v, 8, 7)


def gather_all(weight_in, weight_out, vectors, width):
    whole = lambda v: lax.all_gather(v, AXES, axis=0, tiled=True)
    low_in = weight_in.astype(jnp.bfloat16)
    small = lax.all_gather(rounded(vectors), AXES, axis=1, tiled=True)
    return whole(low_in[:, : 3 * width]), whole(low_in[:, 3 * width :]), whole(weight_out.astype(jnp.bfloat16)), small


def forward_plain(tokens, grad_out, full_qkv, full_up, full_out, small, prev, segments):
    width = tokens.shape[1]
    dot = lambda a, b: jnp.dot(a, b, preferred_element_type=jnp.float32)
    sums = lambda v: jnp.sum(v, axis=0, dtype=jnp.float32)
    offsets = jnp.concatenate([small[4], jnp.zeros_like(small[4]), small[5]])
    qkv = (dot(tokens, full_qkv) + offsets).astype(jnp.bfloat16)
    logits, mixed, log_sums = attn_fwd(qkv, prev, segments, 640)
    first = tokens.astype(jnp.float32) + (dot(mixed, full_out[:width]) + small[6])
    hidden_one, normed_one, scale_one = norm_rows(first, small[0], small[2])
    hidden_low = hidden_one.astype(jnp.bfloat16)
    upward = dot(hidden_low, full_up) + small[8:].reshape(-1)
    activated, gelu_pull = jax.vjp(gelu_exact, upward)
    activated, slope = activated.astype(jnp.bfloat16), gelu_pull(jnp.ones_like(upward))[0]
    second = hidden_one + (dot(activated, full_out[width:]) + small[7])
    output, normed_two, scale_two = norm_rows(second, small[1], small[3])
    grad_output = grad_out.astype(jnp.float32)
    grad_second = norm_back(grad_output, normed_two, scale_two, small[1])
    grad_down = grad_second.astype(jnp.bfloat16)
    two_sums = jnp.stack([sums(grad_output * normed_two), sums(grad_output), sums(grad_down)])
    return (logits, qkv, mixed, log_sums, hidden_low, normed_one, scale_one, activated, slope, output.astype(jnp.bfloat16),
            grad_second, grad_down, two_sums)


def reduce_all(grad_qkv, grad_up, grad_out, small, shards):
    part = lambda v: lax.psum_scatter(v, AXES, scatter_dimension=0, tiled=True).astype(jnp.float32)
    owned_in = jnp.concatenate([part(grad_qkv), part(grad_up)], axis=1)
    owned_out = part(grad_out)
    owned_small = lax.psum_scatter(small, AXES, scatter_dimension=1, tiled=True)
    total = lax.psum(jnp.sum(owned_in**2) + jnp.sum(owned_out**2) + jnp.sum(owned_small**2), AXES)
    return owned_in, owned_out, owned_small, jnp.sqrt(total)


def body(remote, hidden_in, prev_logits, segment_ids, d_hidden, d_logits, weight_in, weight_out, vectors,
         moment_in, moment_out, moment_vectors, square_in, square_out, square_vectors, step_count):
    width = weight_out.shape[1]
    shards = lax.axis_size("dp") * lax.axis_size("fsdp")
    dot = lambda spec, a, b: jnp.einsum(spec, a, b, preferred_element_type=jnp.float32)
    sums = lambda v: jnp.sum(v, axis=0, dtype=jnp.float32)
    segments = segment_ids[0]
    if remote:
        (logits, full_qkv, full_up, full_out, qkv, mixed, hidden_low, normed_one, activated, slope, mask, small, log_sums, scale_one,
         output, grad_second, grad_down, two_sums) = forward_all(
             FORWARD_PLAN, ROUTES, hidden_in, d_hidden, weight_in, weight_out, vectors, prev_logits[0], segments)
        grad_prev, grad_tokens, grad_in, grad_out, grad_vec, norm = backward_all(
            BACKWARD_PLAN, vectors.shape[1], grad_down, hidden_low, small, two_sums, log_sums, scale_one, prev_logits[0], d_logits[0],
            activated, slope, full_out, full_up, full_qkv, grad_second, normed_one, mixed, hidden_in, qkv, mask)
        (logits, grad_prev, output, grad_tokens, *states, grad_norm) = update_all(
            norm, step_count, [logits, grad_prev, output, grad_tokens],
            [(grad_in, weight_in, moment_in, square_in), (grad_out, weight_out, moment_out, square_out),
             (grad_vec, vectors, moment_vectors, square_vectors)])
        clipped, moments, squares, updated, copies = [states[i::5] for i in range(5)]
        return (output, logits[None], grad_tokens, grad_prev[None], *clipped, *moments, *squares, *updated, *copies, grad_norm[0, 0])
    (full_qkv, full_up, full_out, small) = gather_all(weight_in, weight_out, vectors, width)
    (logits, qkv, mixed, log_sums, hidden_low, normed_one, scale_one, activated, slope, output,
     grad_second, grad_down, two_sums) = forward_plain(hidden_in, d_hidden, full_qkv, full_up, full_out, small, prev_logits[0], segments)
    w_attn, w_down = full_out[:width], full_out[width:]
    down_grad = dot("tf,td->fd", activated, grad_down).astype(jnp.bfloat16)
    grad_up = (dot("td,fd->tf", grad_down, w_down) * slope).astype(jnp.bfloat16)
    up_grad = dot("td,tf->df", hidden_low, grad_up).astype(jnp.bfloat16)
    grad_one = grad_second + dot("tf,df->td", grad_up, full_up)
    grad_first = norm_back(grad_one, normed_one, scale_one, small[0])
    grad_attn = grad_first.astype(jnp.bfloat16)
    attn_grad = dot("tc,td->cd", mixed, grad_attn).astype(jnp.bfloat16)
    grad_mixed = dot("td,cd->tc", grad_attn, w_attn).astype(jnp.bfloat16)
    grad_prev, grad_q, grad_k, grad_v = attn_bwd(qkv, grad_mixed, prev_logits[0], d_logits[0], log_sums, segments, 640)
    grad_qkv = jnp.concatenate([grad_q, grad_k, grad_v], axis=1)
    qkv_grad = dot("td,tc->dc", hidden_in, grad_qkv).astype(jnp.bfloat16)
    grad_tokens = (grad_first + dot("tc,dc->td", grad_qkv, full_qkv)).astype(jnp.bfloat16)
    small_grad = jnp.concatenate([
        jnp.stack([sums(grad_one * normed_one), two_sums[0], sums(grad_one), two_sums[1],
                   sums(grad_q), sums(grad_v), sums(grad_attn), two_sums[2]]),
        sums(grad_up).reshape(-1, width)], axis=0)

    owned_in, owned_out, owned_small, grad_norm = reduce_all(
        qkv_grad, up_grad, jnp.concatenate([attn_grad, down_grad], axis=0), small_grad, shards)
    factor = jnp.minimum(1.0, clip_scale * math.sqrt(PARAMS) / (grad_norm + 1e-06))
    step_value = step_count[0].astype(jnp.float32)
    new = [
        adam_update(weight_in, moment_in, square_in, owned_in, factor, step_value, rate_matrix, decay_matrix),
        adam_update(weight_out, moment_out, square_out, owned_out, factor, step_value, rate_matrix, decay_matrix),
        adam_update(vectors, moment_vectors, square_vectors, owned_small, factor, step_value, rate_vector, 0.0),
    ]
    clipped, moments, squares, updated = zip(*new)
    return (output.astype(jnp.bfloat16), logits[None], grad_tokens, grad_prev[None],
            *clipped, *moments, *squares, *updated, *[u.astype(jnp.bfloat16) for u in updated], grad_norm)


def solution(mesh):
    remote = (mesh.shape["dp"], mesh.shape["fsdp"]) == (4, 8)
    rows = P(AXES, None)
    heads = P(AXES, None, None, None)
    cols = P(None, AXES)
    trio = (rows, rows, cols)
    return jax.shard_map(
        functools.partial(body, remote),
        mesh=mesh,
        in_specs=(rows, heads, rows, rows, heads, *trio, *trio, *trio, P()),
        out_specs=(rows, heads, rows, heads, *trio, *trio, *trio, *trio, *trio, P()),
        check_vma=False,
    )
```

```python
import functools
import math

import jax
import jax.numpy as jnp
from jax import lax
from jax.experimental import pallas as pl
from jax.experimental.pallas import tpu as pltpu
from jax.sharding import PartitionSpec as P

PARAMS = 7087104


norm_eps = 1e-12
clip_scale = 1.0
beta_one = 0.9
beta_two = 0.999
adam_eps = 1e-08
rate_matrix = 0.06
rate_vector = 0.25
decay_matrix = 0.01
NEG = -1e30
NT = (((1,), (1,)), ((), ()))
NN = (((1,), (0,)), ((), ()))
TN = (((0,), (0,)), ((), ()))
AXES = ("dp", "fsdp")


def gelu_exact(upward):
    return jax.nn.gelu(upward, approximate=False)


def norm_rows(residual, gain_row, shift_row):
    centered = residual - jnp.mean(residual, axis=1, keepdims=True)
    scaling = lax.rsqrt(jnp.mean(centered * centered, axis=1, keepdims=True) + norm_eps)
    normed = centered * scaling
    return (normed * gain_row + shift_row, normed, scaling)


def norm_back(grad_after, normed, scaling, gain_row):
    scaled_grad = grad_after * gain_row
    return scaling * (
        scaled_grad
        - jnp.mean(scaled_grad, axis=1, keepdims=True)
        - normed * jnp.mean(scaled_grad * normed, axis=1, keepdims=True)
    )


def dotf(a, b, dims):
    return lax.dot_general(a, b, dims, preferred_element_type=jnp.float32)

def half_masks(rows):
    lane = lax.broadcasted_iota(jnp.int32, (rows, 128), 1)
    return lane < 64

def attn_fwd_kernel(BR, q_ref, k_ref, v_ref, prev_ref, srow_ref, scol_ref, logits_ref, mixed_ref, lse_ref, mask_ref):
    g = pl.program_id(0)
    rows = q_ref.shape[0]
    @pl.when(g == 0)
    def _():
        mask_ref[...] = jnp.where(scol_ref[...] == srow_ref[...], 0.0, NEG)
        lse_ref[...] = jnp.zeros_like(lse_ref)
    k2 = k_ref[...]
    v2 = v_ref[...]
    left = half_masks(rows)
    zero = jnp.zeros_like(v2)
    va = jnp.where(left, v2, zero)
    vb = jnp.where(left, zero, v2)
    for rb in range(rows // BR):
        sl = pl.ds(rb * BR, BR)
        q2 = q_ref[sl, :] * jnp.bfloat16(0.125)
        lb = half_masks(BR)
        outs = []
        lses = []
        for h in range(2):
            qh = jnp.where(lb if h == 0 else ~lb, q2, jnp.zeros_like(q2))
            raw = dotf(qh, k2, NT) + prev_ref[h, sl, :].astype(jnp.float32)
            logits_ref[h, sl, :] = raw.astype(jnp.bfloat16)
            s = raw + mask_ref[sl, :]
            m = jnp.max(s, axis=1, keepdims=True)
            e = jnp.exp(s - m)
            tot = jnp.sum(e, axis=1, keepdims=True)
            o = dotf(e.astype(jnp.bfloat16), va if h == 0 else vb, NN)
            outs.append(o / tot)
            lses.append(m + jnp.log(tot))
        mixed_ref[sl, :] = (outs[0] + outs[1]).astype(jnp.bfloat16)
        lane = lax.broadcasted_iota(jnp.int32, (BR, 128), 1)
        cur = lse_ref[sl, :]
        cur = jnp.where(lane == 2 * g, lses[0], cur)
        cur = jnp.where(lane == 2 * g + 1, lses[1], cur)
        lse_ref[sl, :] = cur

def attn_fwd(qkv, prev, seg, BR=128):
    rows = qkv.shape[0]
    heads = prev.shape[0]
    G = heads // 2
    srow = seg.reshape(1, rows); scol = seg.reshape(rows, 1)
    return pl.pallas_call(
        functools.partial(attn_fwd_kernel, BR),
        grid=(G,),
        in_specs=[
            pl.BlockSpec((rows, 128), lambda g: (0, g)),
            pl.BlockSpec((rows, 128), lambda g: (0, G + g)),
            pl.BlockSpec((rows, 128), lambda g: (0, 2 * G + g)),
            pl.BlockSpec((2, rows, rows), lambda g: (g, 0, 0)),
            pl.BlockSpec((1, rows), lambda g: (0, 0)),
            pl.BlockSpec((rows, 1), lambda g: (0, 0)),
        ],
        out_specs=[
            pl.BlockSpec((2, rows, rows), lambda g: (g, 0, 0)),
            pl.BlockSpec((rows, 128), lambda g: (0, g)),
            pl.BlockSpec((rows, 128), lambda g: (0, 0)),
        ],
        out_shape=[
            jax.ShapeDtypeStruct((heads, rows, rows), jnp.bfloat16),
            jax.ShapeDtypeStruct((rows, heads * 64), jnp.bfloat16),
            jax.ShapeDtypeStruct((rows, 128), jnp.float32),
        ],
        scratch_shapes=[pltpu.VMEM((rows, rows), jnp.float32)],
        compiler_params=pltpu.CompilerParams(vmem_limit_bytes=60 * 2**20),
        name="attn_fwd",
    )(qkv, qkv, qkv, prev, srow, scol)

def attn_bwd_kernel(BR, q_ref, k_ref, v_ref, do_ref, prev_ref, dl_ref, lse_ref, srow_ref, scol_ref,
                    dprev_ref, dq_ref, dk_ref, dv_ref, mask_ref, p_ref, g_ref):
    g = pl.program_id(0)
    rows = q_ref.shape[0]
    @pl.when(g == 0)
    def _():
        mask_ref[...] = jnp.where(scol_ref[...] == srow_ref[...], 0.0, NEG)
    k2 = k_ref[...]
    v2 = v_ref[...]
    left = half_masks(rows)
    zero = jnp.zeros_like(v2)
    for h in range(2):
        lm = left if h == 0 else ~left
        kh = jnp.where(lm, k2, zero)
        for rb in range(rows // BR):
            sl = pl.ds(rb * BR, BR)
            lb = half_masks(BR)
            lb = lb if h == 0 else ~lb
            q2 = q_ref[sl, :] * jnp.bfloat16(0.125)
            qh = jnp.where(lb, q2, jnp.zeros_like(q2))
            doh = jnp.where(lb, do_ref[sl, :], jnp.zeros_like(q2))
            lane = lax.broadcasted_iota(jnp.int32, (BR, 128), 1)
            lse = jnp.sum(jnp.where(lane == 2 * g + h, lse_ref[sl, :], 0.0), axis=1, keepdims=True)
            s = dotf(qh, k2, NT) + prev_ref[h, sl, :].astype(jnp.float32) + mask_ref[sl, :]
            p = jnp.exp(s - lse)
            dp = dotf(doh, v2, NT)
            delta = jnp.sum(p * dp, axis=1, keepdims=True)
            ds = p * (dp - delta)
            gt = (ds + dl_ref[h, sl, :].astype(jnp.float32)).astype(jnp.bfloat16)
            dprev_ref[h, sl, :] = gt
            p_ref[sl, :] = p.astype(jnp.bfloat16)
            dq = dotf(gt, kh, NN) * 0.125
            if h == 0:
                dq_ref[sl, :] = dq.astype(jnp.bfloat16)
            else:
                dq_ref[sl, :] = dq_ref[sl, :] + dq.astype(jnp.bfloat16)
        qh = jnp.where(lm, q_ref[...], zero)
        doh = jnp.where(lm, do_ref[...], zero)
        dk = (dotf(dprev_ref[h], qh, TN) * 0.125).astype(jnp.bfloat16)
        dv = dotf(p_ref[...], doh, TN).astype(jnp.bfloat16)
        if h == 0:
            dk_ref[...] = dk
            dv_ref[...] = dv
        else:
            dk_ref[...] = dk_ref[...] + dk
            dv_ref[...] = dv_ref[...] + dv

def attn_bwd(qkv, do, prev, dl, lse, seg, BR=128):
    rows = qkv.shape[0]
    heads = prev.shape[0]
    G = heads // 2
    srow = seg.reshape(1, rows); scol = seg.reshape(rows, 1)
    col = lambda off: pl.BlockSpec((rows, 128), lambda g: (0, off + g))
    return pl.pallas_call(
        functools.partial(attn_bwd_kernel, BR),
        grid=(G,),
        in_specs=[
            col(0), col(G), col(2 * G), col(0),
            pl.BlockSpec((2, rows, rows), lambda g: (g, 0, 0)),
            pl.BlockSpec((2, rows, rows), lambda g: (g, 0, 0)),
            pl.BlockSpec((rows, 128), lambda g: (0, 0)),
            pl.BlockSpec((1, rows), lambda g: (0, 0)),
            pl.BlockSpec((rows, 1), lambda g: (0, 0)),
        ],
        out_specs=[
            pl.BlockSpec((2, rows, rows), lambda g: (g, 0, 0)),
            col(0), col(0), col(0),
        ],
        out_shape=[
            jax.ShapeDtypeStruct((heads, rows, rows), jnp.bfloat16),
        ] + [jax.ShapeDtypeStruct((rows, heads * 64), jnp.bfloat16)] * 3,
        scratch_shapes=[pltpu.VMEM((rows, rows), jnp.float32), pltpu.VMEM((rows, rows), jnp.bfloat16), pltpu.VMEM((8, 128), jnp.float32)],
        compiler_params=pltpu.CompilerParams(vmem_limit_bytes=60 * 2**20),
        name="attn_bwd",
    )(qkv, qkv, qkv, do, prev, dl, lse, srow, scol)


MESH = pl.DeviceIdType.MESH


def coords():
    dp = lax.axis_index("dp"); fs = lax.axis_index("fsdp")
    y = dp // 2; c = lax.rem(dp, 2)
    z = fs // 2; x = lax.rem(fs, 2)
    return y, c, z, x

def dev(y, c, z, x):
    return (y * 2 + c, z * 2 + x)


ROUTES = "zzzzzzznnnn"
FORWARD_PLAN = {
    "start": [(1, 7), (1, 8), (1, 9), (1, 10), (1, 0), (2, 0), (1, 1), (3, 0)],
    ("q", 0): [(1, 2), (2, 1), (1, 3), (2, 2), (3, 1)],
    ("q", 1): [(2, 3), (1, 4), (3, 2)],
    ("q", 2): [(3, 3), (1, 5)],
    ("pair", 0): [(2, 4), (1, 6)],
    ("pair", 2): [(2, 5)],
    ("pair", 3): [(3, 4)],
    ("pair", 5): [(2, 6)],
    "out": [(3, 5), (2, 7), (3, 6), (2, 8)],
    "norm": [(3, 7), (2, 9)],
    ("up", 0): [(3, 8), (2, 10)],
    ("up", 1): [(3, 9)],
    ("up", 2): [(3, 10)],
}
BACKWARD_PLAN = {
    ("up", 1): [(2, 0)],
    ("down", 2): [(2, 1)],
    ("down", 3): [(3, 0), (2, 2)],
    "norm": [(3, 1), (4, 0), (2, 3)],
    "out": [(4, 1), (3, 2)],
    ("head", 0): [(3, 3), (5, 0)],
    ("head", 2): [(4, 2), (4, 3), (2, 4), (2, 5), (5, 1)],
    ("head", 3): [(2, 6), (2, 7)],
    ("head", 4): [(5, 2)],
    ("head", 5): [(3, 4)],
    ("head", 6): [(2, 8), (5, 3)],
    ("head", 7): [(3, 5)],
    ("head", 8): [(2, 9)],
    ("head", 9): [(3, 6)],
    ("head", 10): [(3, 7), (2, 10), (4, 4)],
    ("head", 11): [(3, 8), (2, 11)],
    "end": [(4, 5), (3, 9)],
    ("dx", 1): [(4, 6), (4, 7), (2, 12), (2, 13), (3, 10), (5, 4)],
    "last": [(4, 8), (4, 9), (3, 11), (3, 12), (5, 5), (3, 13), (4, 10), (4, 11), (4, 12), (4, 13), (5, 6), (5, 7), (5, 8), (5, 9), (5, 10), (5, 11), (5, 12), (5, 13)],
}


class Gather:
    def __init__(self, chunks, routes, sources, wholes, send_sem, recv_sem):
        self.chunks, self.routes, self.sources, self.wholes = chunks, routes, sources, wholes
        self.send_sem, self.recv_sem = send_sem, recv_sem
        self.y, self.c, self.z, self.x = coords()

    def part(self, k):
        array, start, size, origin = self.chunks[k]
        return self.wholes[array], pl.ds(start, size), self.sources[array].at[:, pl.ds(origin, size)]

    def rows_of(self, k, x):
        size = self.sources[self.chunks[k][0]].shape[0]
        return pl.ds(pl.multiple_of(size * x, 8), size)

    def copy(self, src, dst, k, slot, who):
        return pltpu.make_async_remote_copy(
            src_ref=src, dst_ref=dst, send_sem=self.send_sem.at[k, slot], recv_sem=self.recv_sem.at[k, slot],
            device_id=who, device_id_type=MESH)

    def along_z(self, k):
        whole, cols, mine = self.part(k)
        spot = whole.at[self.y, self.c, self.z, self.rows_of(k, self.x), cols]
        return [self.copy(mine, spot, k, d, dev(self.y, self.c, lax.rem(self.z + d + 1, 4), self.x)) for d in range(3)]

    def across(self):
        return jnp.where(self.c == 0, self.y, 1 - self.y), jnp.where(self.c == 0, 1 - self.x, self.x)

    def other(self):
        return (jnp.where(self.c == 0, 1 - self.y, self.y) * 2 + self.c, self.z * 2 + jnp.where(self.c == 0, self.x, 1 - self.x))

    def block(self, k, y, x):
        whole, cols, _ = self.part(k)
        return whole.at[y, self.c, :, self.rows_of(k, x), cols]

    def to_neighbours(self, k):
        block = self.block(k, self.y, self.x)
        return [self.copy(block, block, k, 3, dev(self.y, self.c, self.z, 1 - self.x)),
                self.copy(block, block, k, 4, dev(1 - self.y, self.c, self.z, self.x))]

    def handed_on(self, k):
        block = self.block(k, *self.across())
        return self.copy(block, block, k, 3 + self.c, self.other()), self.copy(block, block, k, 5, self.other()), self.copy(block, block, k, 4 - self.c, self.other())

    def early(self, k):
        whole, cols, mine = self.part(k)
        y, x = self.across()
        return self.copy(mine, whole.at[self.y, self.c, self.z, self.rows_of(k, self.x), cols], k, 3, dev(y, self.c, self.z, x))

    def relayed(self, k):
        whole, cols, _ = self.part(k)
        y, x = self.across()
        spot = whole.at[y, self.c, self.z, self.rows_of(k, x), cols]
        return [self.copy(spot, spot, k, 4 + d, dev(self.y, self.c, lax.rem(self.z + d + 1, 4), self.x)) for d in range(3)]

    def halves(self, k):
        own, far = self.block(k, self.y, self.x), self.block(k, *self.across())
        return [self.copy(own, own, k, 7, self.other()), self.copy(far, far, k, 8, self.other())]

    def to_core(self, k):
        whole, cols, _ = self.part(k)
        plane = whole.at[:, self.c, :, :, cols]
        return self.copy(plane, plane, k, 9, dev(self.y, 1 - self.c, self.z, self.x))

    def start(self, k):
        if self.routes[k] == "n":
            self.early(k).start()
        for d in self.along_z(k):
            d.start()

    def s1(self, k):
        if self.routes[k] == "n":
            self.early(k).wait_recv()
            for d in self.relayed(k):
                d.start()
            return
        for d in self.along_z(k):
            d.wait_recv()
        for d in self.to_neighbours(k):
            d.start()

    def s2(self, k):
        if self.routes[k] == "n":
            for d in self.along_z(k) + self.relayed(k):
                d.wait_recv()
            for d in self.halves(k):
                d.start()
            return
        got, on, _ = self.handed_on(k)
        got.wait_recv()
        on.start()

    def s3(self, k):
        if self.routes[k] == "n":
            for d in self.halves(k):
                d.wait_recv()
        else:
            _, on, other = self.handed_on(k)
            other.wait_recv()
            on.wait_recv()
        self.to_core(k).start()

    def s4(self, k):
        self.to_core(k).wait_recv()

    def finish(self, k):
        if self.routes[k] == "n":
            sent = [self.early(k), *self.relayed(k), *self.halves(k)]
        else:
            sent = self.to_neighbours(k) + [self.handed_on(k)[1]]
        for d in self.along_z(k) + sent + [self.to_core(k)]:
            d.wait_send()


def peers_of(y, c, z, x):
    return [dev(y, c, lax.rem(z + d, 4), x) for d in (1, 2, 3)] + [dev(y, c, z, 1 - x), dev(1 - y, c, z, x), dev(y, 1 - c, z, x)]


def normalise(v):
    centered = v - jnp.mean(v, axis=1, keepdims=True)
    scaling = lax.rsqrt(jnp.mean(centered * centered, axis=1, keepdims=True) + norm_eps)
    return centered * scaling, scaling


def spread_columns(ref, shards, columns, rows, width):
    lane = lax.broadcasted_iota(jnp.int32, (rows, 128), 1)
    blocks = [jnp.zeros((rows, 128), jnp.float32) for _ in range(width // 128)]
    for d in range(shards):
        at, off = columns * d // 128, columns * d % 128
        tile = ref[d // 16, d // 8 % 2, d // 2 % 4, 16 * (d % 2):16 * (d % 2) + 16, :][:rows]
        tile = pltpu.roll(tile, off, 1) if off else tile
        if off + columns > 128:
            blocks[at + 1] = blocks[at + 1] + jnp.where(lane < off, tile, 0.0)
            tile = jnp.where(lane < off, 0.0, tile)
        blocks[at] = blocks[at] + tile
    return blocks


def forward_kernel(plan, routes, win_ref, wout_ref, vec_ref, srow_ref, prev_ref, x_hbm, dout_hbm,
                   logits_ref, probs_ref, gq_ref, gu_ref, go_ref, qkv_hbm, mixed_hbm, hlow_hbm, none_hbm, act_hbm, gp_hbm,
                   small_ref, sone_ref, out_ref, dsec_ref, ddown_ref, sums_ref,
                   gv_ref, mask_ref, cin_ref, cout_ref, cvec_ref, w_ref, wo_ref, x_ref, dout_ref, qkv_ref, mixed_ref, hlow_ref, none_ref,
                   act_ref, gp_ref, hid_ref, sec_ref, send_sem, recv_sem, loc_sem, out_sem):
    g = pl.program_id(0)
    rows, width = x_hbm.shape
    hidden = act_hbm.shape[1]
    last = pl.num_programs(0) - 1
    tile = 256
    y, c, z, x = coords()
    V, Q, O, U = 0, 1, 4, 7
    chunks = [(3, 0, 128, 0)] + [(0, 768 * i, 768, 768 * i) for i in range(3)] + [(2, 256 * i, 256, 256 * i) for i in range(3)]
    chunks += [(1, 768 * i, 768, 3 * width + 768 * i) for i in range(4)]
    ga = Gather(chunks, routes, [cin_ref, cin_ref, cout_ref, cvec_ref], [gq_ref, gu_ref, go_ref, gv_ref], send_sem, recv_sem)

    def run(place):
        for stage, k in plan.get(place, ()):
            (ga.s1, ga.s2, ga.s3)[stage - 1](k)

    def load(src, dst, i):
        return pltpu.make_async_copy(src, dst, loc_sem.at[i])

    def save(src, dst, i):
        return pltpu.make_async_copy(src, dst, out_sem.at[i])

    stores = lambda: [load(cin_ref.at[:, pl.ds(0, 3 * width)], gq_ref.at[y, c, z, ga.rows_of(Q, x)], 0),
                      load(cin_ref.at[:, pl.ds(3 * width, hidden)], gu_ref.at[y, c, z, ga.rows_of(U, x)], 1),
                      load(cout_ref, go_ref.at[y, c, z, ga.rows_of(O, x)], 2)]
    x_in, dout_in = lambda: load(x_hbm, x_ref, 3), lambda: load(dout_hbm, dout_ref, 4)
    w_out, w_up, w_qkv = go_ref.reshape(width + hidden, width), gu_ref.reshape(width, hidden), gq_ref.reshape(width, 3 * width)
    w_q = lambda k: load(w_qkv.at[:, pl.ds(768 * k, 768)], w_ref.at[k % 2], 5 + k % 2)
    w_u = lambda k: load(w_up.at[:, pl.ds(768 * k, 768)], w_ref.at[(k + 1) % 2], 5 + (k + 1) % 2)
    w_o = lambda: load(w_out.at[pl.ds(0, width), :], w_ref.at[0], 5)
    w_down = lambda: load(w_out.at[pl.ds(width, hidden), :], wo_ref, 7)
    saves = {"mixed": lambda: save(mixed_ref, mixed_hbm, 1), "hlow": lambda: save(hlow_ref, hlow_hbm, 2),
             "none": lambda: save(none_ref, none_hbm, 3), "qkv": lambda: save(qkv_ref, qkv_hbm, 4)}
    save_act = lambda k: save(act_ref.at[:, pl.ds(768 * k, 768)], act_hbm.at[:, pl.ds(768 * k, 768)], 5 + k)
    save_gp = lambda k: save(gp_ref.at[k % 2], gp_hbm.at[:, pl.ds(768 * k, 768)], 9 + k)

    @pl.when(g == 0)
    def _():
        barrier = pltpu.get_barrier_semaphore()
        peers = peers_of(y, c, z, x)
        for p in peers:
            pl.semaphore_signal(barrier, inc=1, device_id=p, device_id_type=MESH)
        cvec_ref[...] = jnp.zeros_like(cvec_ref)
        vec = vec_ref[...].astype(jnp.bfloat16).astype(jnp.float32)
        cvec_ref[0:vec.shape[0], 0:vec.shape[1]] = vec
        gv_ref[y, c, z, ga.rows_of(V, x), :] = cvec_ref[...]
        cin_ref[...] = win_ref[...].astype(jnp.bfloat16)
        cout_ref[...] = wout_ref[...].astype(jnp.bfloat16)
        pl.semaphore_wait(barrier, len(peers))
        for k in range(len(chunks)):
            ga.start(k)
        for s in stores():
            s.start()
        x_in().start()
        seg = jnp.broadcast_to(srow_ref[...].astype(jnp.float32), (rows, rows))
        mask_ref[...] = jnp.where(seg == seg.T, 0.0, NEG)
        for s in stores():
            s.wait()
        dout_in().start()
        run("start")
        ga.s4(V)
        run("small")
        spread = spread_columns(gv_ref, 32, vec_ref.shape[1], vec_ref.shape[0], width)
        for i, v in enumerate(spread):
            small_ref[:, 128 * i:128 * (i + 1)] = v
        x_in().wait()

        @pl.loop(0, 3)
        def _(k):
            for i in range(3):
                @pl.when(k == i)
                def _():
                    run(("q", i))
                    ga.s4(Q + i)
                    w_q(i).start()
                    run(("qw", i))
                    w_q(i).wait()
            bias = jnp.where(k == 1, 0.0, small_ref[pl.ds(4 + k // 2, 1), :])
            v = dotf(x_ref[...], w_ref[lax.rem(k, 2)], NN) + bias
            qkv_ref[:, pl.ds(pl.multiple_of(768 * k, 768), 768)] = v.astype(jnp.bfloat16)
        saves["qkv"]().start()

    for i in range(6):
        if plan.get(("pair", i)):
            @pl.when(g == i)
            def _():
                run(("pair", i))

    at = lambda off: pl.ds(pl.multiple_of(off * width + g * 128, 128), 128)
    left = half_masks(rows)
    q2 = qkv_ref[:, at(0)] * jnp.bfloat16(0.125)
    k2 = qkv_ref[:, at(1)]
    v2 = qkv_ref[:, at(2)]
    zero = jnp.zeros_like(v2)
    outs = []
    for h in range(2):
        pick = (lambda v: jnp.where(left, v, zero)) if h == 0 else (lambda v: jnp.where(left, zero, v))
        raw = dotf(pick(q2), k2, NT) + prev_ref[h].astype(jnp.float32)
        logits_ref[h] = raw.astype(jnp.bfloat16)
        s = raw + mask_ref[...]
        e = jnp.exp(s - jnp.max(s, axis=1, keepdims=True))
        probs = (e * (1.0 / jnp.sum(e, axis=1, keepdims=True))).astype(jnp.bfloat16)
        probs_ref[h] = probs
        outs.append(dotf(probs, pick(v2), NN))
    mixed_ref[:, pl.ds(pl.multiple_of(g * 128, 128), 128)] = (outs[0] + outs[1]).astype(jnp.bfloat16)

    @pl.when(g == last)
    def _():
        saves["mixed"]().start()
        run("out")
        for k in range(3):
            ga.s4(O + k)
        w_o().start()
        w_down().start()
        run("outw")
        w_o().wait()
        hid_ref[...] = x_ref[...].astype(jnp.float32) + (dotf(mixed_ref[...], w_ref[0], NN) + small_ref[6:7, :])
        run("norm")

        @pl.loop(0, rows // 128)
        def _(i):
            sl = pl.ds(pl.multiple_of(i * 128, 128), 128)
            normed, scaling = normalise(hid_ref[sl, :])
            none_ref[sl, :] = normed
            sone_ref[sl, :] = jnp.broadcast_to(scaling, (128, 128))
            hid = normed * small_ref[0:1, :] + small_ref[2:3, :]
            hid_ref[sl, :] = hid
            hlow_ref[sl, :] = hid.astype(jnp.bfloat16)

        saves["none"]().start()
        saves["hlow"]().start()

        @pl.loop(0, 4)
        def _(k):
            for i in range(4):
                @pl.when(k == i)
                def _():
                    run(("up", i))
                    ga.s4(U + i)
                    w_u(i).start()
                    run(("upw", i))
                    w_u(i).wait()
                    if i >= 2:
                        save_gp(i - 2).wait()

            @pl.loop(0, 768 // tile)
            def _(j):
                sl = pl.ds(pl.multiple_of(j * tile, tile), tile)
                to = pl.ds(pl.multiple_of(768 * k + j * tile, tile), tile)
                u = dotf(hlow_ref[...], w_ref[lax.rem(k + 1, 2), :, sl], NN) + small_ref[pl.ds(8 + k, 1), sl]
                cdf = 0.5 * (1.0 + lax.erf(u * math.sqrt(0.5)))
                act_ref[:, to] = (u * cdf).astype(jnp.bfloat16)
                gp_ref[lax.rem(k, 2), :, sl] = (cdf + u * (jnp.exp(-0.5 * (u * u)) * (1.0 / math.sqrt(2.0 * math.pi)))).astype(jnp.bfloat16)
            for i in range(4):
                @pl.when(k == i)
                def _():
                    save_act(i).start()
                    save_gp(i).start()
        w_down().wait()
        sec_ref[...] = hid_ref[...] + (dotf(act_ref[...], wo_ref[...], NN) + small_ref[7:8, :])
        sums_ref[...] = jnp.zeros_like(sums_ref)
        dout_in().wait()

        @pl.loop(0, rows // 128)
        def _(i):
            sl = pl.ds(pl.multiple_of(i * 128, 128), 128)
            normed, scaling = normalise(sec_ref[sl, :])
            out_ref[sl, :] = (normed * small_ref[1:2, :] + small_ref[3:4, :]).astype(jnp.bfloat16)
            dy = dout_ref[sl, :].astype(jnp.float32)
            back = norm_back(dy, normed, scaling, small_ref[1:2, :])
            low = back.astype(jnp.bfloat16)
            dsec_ref[sl, :] = back
            ddown_ref[sl, :] = low
            sums_ref[0:1, :] += jnp.sum(dy * normed, axis=0, keepdims=True)
            sums_ref[1:2, :] += jnp.sum(dy, axis=0, keepdims=True)
            sums_ref[2:3, :] += jnp.sum(low.astype(jnp.float32), axis=0, keepdims=True)
        for k in range(len(chunks)):
            ga.finish(k)
        for s in saves.values():
            s().wait()
        for k in range(4):
            save_act(k).wait()
        for k in (2, 3):
            save_gp(k).wait()


def forward_all(plan, routes, tokens, grad_out, weight_in, weight_out, vectors, prev, seg):
    rows, width = tokens.shape
    heads = prev.shape[0]
    hidden = weight_in.shape[1] - 3 * width
    f32, bf16 = jnp.float32, jnp.bfloat16
    fixed = lambda shape: pl.BlockSpec(shape, lambda g: (0,) * len(shape), pipeline_mode=pl.Buffered(1))
    pair = pl.BlockSpec((2, rows, rows), lambda g: (g, 0, 0))
    hbm = pl.BlockSpec(memory_space=pl.ANY)
    far = [((2, 2, 4, 2 * weight_in.shape[0], 3 * width), bf16), ((2, 2, 4, 2 * weight_in.shape[0], hidden), bf16),
           ((2, 2, 4, 2 * weight_out.shape[0], width), bf16), ((rows, 3 * width), bf16), ((rows, width), bf16), ((rows, width), bf16),
           ((rows, width), f32), ((rows, hidden), bf16), ((rows, hidden), bf16)]
    near = [((vectors.shape[0], width), f32), ((rows, 128), f32), ((rows, width), bf16), ((rows, width), f32),
            ((rows, width), bf16), ((8, width), f32)]
    v = lambda *shape: pltpu.VMEM(shape, bf16)
    vf = lambda *shape: pltpu.VMEM(shape, f32)
    dma = pltpu.SemaphoreType.DMA
    return pl.pallas_call(
        functools.partial(forward_kernel, plan, routes),
        grid=(heads // 2,),
        in_specs=[fixed(weight_in.shape), fixed(weight_out.shape), fixed(vectors.shape), fixed((1, rows)), pair, hbm, hbm],
        out_specs=[pair, pair] + [hbm] * len(far) + [fixed(s) for s, _ in near],
        out_shape=[jax.ShapeDtypeStruct(prev.shape, bf16)] * 2 + [jax.ShapeDtypeStruct(s, t) for s, t in far + near],
        scratch_shapes=[
            vf(2, 2, 4, 32, 128), vf(rows, rows), v(*weight_in.shape), v(*weight_out.shape), vf(16, 128), v(2, width, 768), v(hidden, width),
            v(rows, width), v(rows, width), v(rows, 3 * width), v(rows, width), v(rows, width), vf(rows, width), v(rows, hidden),
            v(2, rows, 768), vf(rows, width), vf(rows, width), dma((11, 10)), dma((11, 10)), dma((8,)), dma((13,))],
        compiler_params=pltpu.CompilerParams(collective_id=1, has_side_effects=True, vmem_limit_bytes=64 * 2**20 - 65536),
        name="forward",
    )(weight_in, weight_out, vectors, seg.reshape(1, rows), prev, tokens, grad_out)


class Scatter:
    def __init__(self, full, got, send_sem, recv_sem):
        self.full, self.got = full, got
        self.send_sem, self.recv_sem = send_sem, recv_sem
        y, c, z, x = self.y, self.c, self.z, self.x = coords()
        first, second = (1 - y) * 2 + c, z * 2 + 1 - x
        self.core = dev(y, 1 - c, z, x)
        self.one = (jnp.where(c == 0, first, y * 2 + c), jnp.where(c == 0, z * 2 + x, second))
        self.two = (jnp.where(c == 0, y * 2 + c, first), jnp.where(c == 0, second, z * 2 + x))
        self.at_one = (jnp.where(c == 0, 1 - y, y), jnp.where(c == 0, x, 1 - x))
        self.at_two = (jnp.where(c == 0, y, 1 - y), jnp.where(c == 0, 1 - x, x))

    def copy(self, src, dst, k, slot, who):
        return pltpu.make_async_remote_copy(
            src_ref=src, dst_ref=dst, send_sem=self.send_sem.at[k, slot], recv_sem=self.recv_sem.at[k, slot],
            device_id=who, device_id_type=MESH)

    def to_core(self, k):
        return self.copy(self.full[k]().at[:, 1 - self.c], self.got[k][0], k, 0, self.core)

    def to_one(self, k):
        full = self.full[k]()
        return [self.copy(full.at[1 - self.y, self.c, :, 1 - self.x], self.got[k][1].at[0], k, 1, self.one),
                self.copy(full.at[self.at_one[0], self.c, :, self.at_one[1]], self.got[k][1].at[1], k, 2, self.one)]

    def to_two(self, k):
        return self.copy(self.full[k]().at[self.at_two[0], self.c, :, self.at_two[1]], self.got[k][2], k, 3, self.two)

    def along_z(self, k):
        full = self.full[k]()
        out = []
        for i in range(3):
            z = lax.rem(self.z + i + 1, 4)
            out.append(self.copy(full.at[self.y, self.c, z, self.x], self.got[k][3].at[i], k, 4 + i, dev(self.y, self.c, z, self.x)))
        return out

    def r1(self, k):
        self.to_core(k).start()

    def r2(self, k):
        full, got = self.full[k](), self.got[k][0]
        self.to_core(k).wait_recv()

        @pl.loop(0, 8)
        def _(i):
            for y in range(2):
                z, x = i // 2, lax.rem(i, 2)
                total = full[y, self.c, z, x].astype(jnp.float32) + got[y, z, x].astype(jnp.float32)
                full[y, self.c, z, x] = total.astype(full.dtype)
        for d in self.to_one(k):
            d.start()

    def r3(self, k):
        full, got = self.full[k](), self.got[k][1]
        for d in self.to_one(k):
            d.wait_recv()
        y, x = self.at_two

        @pl.loop(0, 4)
        def _(z):
            total = full[y, self.c, z, x].astype(jnp.float32) + got[0, z].astype(jnp.float32)
            full[y, self.c, z, x] = total.astype(full.dtype)
        self.to_two(k).start()

    def r4(self, k):
        full = self.full[k]()
        self.to_two(k).wait_recv()

        @pl.loop(0, 4)
        def _(z):
            total = full[self.y, self.c, z, self.x].astype(jnp.float32) + self.got[k][1][1, z].astype(jnp.float32)
            total = total + self.got[k][2][z].astype(jnp.float32)
            full[self.y, self.c, z, self.x] = total.astype(full.dtype)
        for d in self.along_z(k):
            d.start()

    def r5(self, k):
        for d in self.along_z(k):
            d.wait_recv()
        total = self.full[k]()[self.y, self.c, self.z, self.x].astype(jnp.float32)
        for i in range(3):
            total = total + self.got[k][3][i].astype(jnp.float32)
        return total

    def finish(self, k):
        for d in [self.to_core(k), *self.to_one(k), self.to_two(k), *self.along_z(k)]:
            d.wait_send()


def put_rows(ref, start, value):
    size, count = ref.shape[4], value.shape[0]
    for d in range(start // size, (start + count - 1) // size + 1):
        low, high = max(start, d * size), min(start + count, (d + 1) * size)
        ref[d // 16, d // 8 % 2, d // 2 % 4, d % 2, low - d * size:high - d * size] = value[low - start:high - start]


def own_columns(value, shards, columns):
    for d in range(shards):
        at, off = columns * d // 128, columns * d % 128
        if off + columns <= 128:
            tile = value[:, 128 * at:128 * (at + 1)]
            yield d, pltpu.roll(tile, 128 - off, 1) if off else tile
        else:
            yield d, pltpu.roll(value[:, 128 * at:128 * (at + 2)], 256 - off, 1)[:, :128]


def backward_kernel(heads, plan, columns, *refs):
    (ddown_ref, hlow_ref, small_ref, two_ref, sone_ref, probs_ref, dl_ref,
     act_hbm, gp_hbm, go_hbm, gu_hbm, gq_hbm, dsec_hbm, none_hbm, mixed_hbm, x_hbm, qkv_hbm,
     dprev_ref, dx_ref, gin_ref, gout_ref, gvec_ref, norm_ref) = refs[:23]
    qkv_ref, do_ref, x_ref, mixed_ref, act_ref, gp_ref, dup_ref, w_ref, acc_ref, none_ref, part_ref, fvec_ref = refs[23:35]
    ups, outs = refs[35:37]
    got_flat = refs[37:93]
    nmine, ngot, send_sem, recv_sem, loc_sem, ns_sem, nr_sem = refs[93:]
    g = pl.program_id(0)
    rows, width = ddown_ref.shape
    hidden = act_hbm.shape[1]
    tile = 256
    U, O, Q, V = 0, 4, 7, 13
    got = [got_flat[4 * k:4 * k + 4] for k in range(14)]
    full = [lambda k=k: ups.at[k] for k in range(4)] + [lambda j=j: outs.at[j] for j in range(3)]
    full += [lambda p=p: ups.at[p // 2, :, :, :, :, :, :, pl.ds(384 * (p % 2), 384)] for p in range(6)] + [lambda: fvec_ref]
    sc = Scatter(full, got, send_sem, recv_sem)
    y, c, z, x = coords()
    peers = peers_of(y, c, z, x)
    stages = {1: sc.r1, 2: sc.r2, 3: sc.r3, 4: sc.r4}

    def run(place):
        for stage, k in plan.get(place, ()):
            if stage == 5:
                finish(k)
            else:
                stages[stage](k)

    def finish(k):
        total = sc.r5(k)
        if k < O:
            gin_ref[:, :, 3 * width + 768 * k:3 * width + 768 * (k + 1)] = total
        elif k < Q:
            gout_ref[:, :, 256 * (k - O):256 * (k - O + 1)] = total
        elif k < V:
            for i in range(3):
                gin_ref[:, :, width * i + 128 * (k - Q):width * i + 128 * (k - Q + 1)] = total[:, :, 128 * i:128 * (i + 1)]
        else:
            lane = lax.broadcasted_iota(jnp.int32, total.shape, 1)
            gvec_ref[...] = jnp.where(lane < columns, total, 0.0)

    def load(src, dst, i):
        return pltpu.make_async_copy(src, dst, loc_sem.at[i])

    near = [dev(lax.rem(y + i // 4, 2), lax.rem(c + i // 2 % 2, 2), z, lax.rem(x + i % 2, 2)) for i in range(1, 8)]
    far = [dev(y, c, lax.rem(z + i, 4), x) for i in (1, 2, 3)]

    def share(i):
        return pltpu.make_async_remote_copy(
            src_ref=nmine.at[0 if i < 7 else 1], dst_ref=ngot.at[i], send_sem=ns_sem.at[i], recv_sem=nr_sem.at[i],
            device_id=(near + far)[i], device_id_type=MESH)

    def in_order(values, index):
        total = jnp.zeros_like(values[0])
        for at in range(len(values)):
            for i, v in enumerate(values):
                total = total + jnp.where(index(i) == at, v, 0.0)
        return total

    w_out, w_up, w_qkv = go_hbm.reshape(width + hidden, width), gu_hbm.reshape(width, hidden), gq_hbm.reshape(width, 3 * width)
    late = lambda: [load(dsec_hbm, acc_ref, 0), load(none_hbm, none_ref, 1), load(mixed_hbm, mixed_ref, 2), load(x_hbm, x_ref, 3),
                    load(qkv_hbm, qkv_ref, 4), load(act_hbm, act_ref, 8)]
    last_w = lambda: [load(w_qkv.at[:, pl.ds(768 * i, 768)], w_ref.at[i], 5 + i) for i in range(3)]

    @pl.when(g == 0)
    def _():
        barrier = pltpu.get_barrier_semaphore()
        met = far + near
        for p in met:
            pl.semaphore_signal(barrier, inc=1, device_id=p, device_id_type=MESH)

        def ahead(k):
            return [load(w_out.at[pl.ds(width + 768 * k, 768), :], w_ref.at[0], 5), load(gp_hbm.at[:, pl.ds(768 * k, 768)], gp_ref, 6)]

        def behind(k):
            return [load(w_up.at[:, pl.ds(768 * k, 768)], w_ref.at[1], 7)]
        for d in ahead(0) + behind(0) + late():
            d.start()
        part_ref[...] = jnp.zeros_like(part_ref)
        part_ref[1:2, :] = two_ref[0:1, :]
        part_ref[3:4, :] = two_ref[1:2, :]
        part_ref[7:8, :] = two_ref[2:3, :]
        pl.semaphore_wait(barrier, len(met))

        @pl.loop(0, 4)
        def _(k):
            for i in range(4):
                @pl.when(k == i)
                def _():
                    for d in ahead(i):
                        d.wait()
            low = (dotf(ddown_ref[...], w_ref[0], NT) * gp_ref[...].astype(jnp.float32)).astype(jnp.bfloat16)
            dup_ref[...] = low
            part_ref[pl.ds(8 + k, 1), :] = jnp.sum(low.astype(jnp.float32), axis=0, keepdims=True)
            ups[k] = dotf(hlow_ref[...], dup_ref[...], TN).reshape(ups.shape[1:]).astype(jnp.bfloat16)
            for i in range(4):
                @pl.when(k == i)
                def _():
                    sc.r1(U + i)
                    if i < 3:
                        for d in ahead(i + 1):
                            d.start()
                    run(("down", i))
                    if i == 0:
                        late()[0].wait()
                    for d in behind(i):
                        d.wait()
            acc_ref[...] += dotf(dup_ref[...], w_ref[1], NT)
            for i in range(4):
                @pl.when(k == i)
                def _():
                    if i < 3:
                        for d in behind(i + 1):
                            d.start()
                    run(("up", i))

        wo = load(w_out.at[pl.ds(0, width), :], w_ref.at[0], 5)
        wo.start()
        late()[1].wait()

        @pl.loop(0, rows // 128)
        def _(i):
            sl = pl.ds(pl.multiple_of(i * 128, 128), 128)
            one, normed = acc_ref[sl, :], none_ref[sl, :]
            part_ref[0:1, :] += jnp.sum(one * normed, axis=0, keepdims=True)
            part_ref[2:3, :] += jnp.sum(one, axis=0, keepdims=True)
            back = norm_back(one, normed, sone_ref[sl, 0:1], small_ref[0:1, :])
            low = back.astype(jnp.bfloat16)
            acc_ref[sl, :] = back
            dup_ref[sl, :] = low
            part_ref[6:7, :] += jnp.sum(low.astype(jnp.float32), axis=0, keepdims=True)
        run("norm")
        late()[2].wait()
        late()[5].wait()

        def put(start, value):
            for j in range(3):
                put_rows(outs.at[j], start, value[:, tile * j:tile * (j + 1)].reshape(96, 8, tile).astype(jnp.bfloat16))
        put(0, dotf(mixed_ref[...], dup_ref[...], TN))
        for k in range(4):
            put((width + 768 * k) // 8, dotf(act_ref[:, 768 * k:768 * (k + 1)], ddown_ref[...], TN))
        for j in range(3):
            sc.r1(O + j)
        run("out")
        wo.wait()
        do_ref[...] = dotf(dup_ref[...], w_ref[0], NT).astype(jnp.bfloat16)
        for d in late()[3:5]:
            d.wait()
        for d in last_w():
            d.start()

    for i in range(heads):
        if plan.get(("head", i)):
            @pl.when(g == i)
            def _():
                run(("head", i))

    pair, half = g // 2, lax.rem(g, 2)
    at = lambda off: pl.ds(pl.multiple_of(off * width + pair * 128, 128), 128)
    lane = lax.broadcasted_iota(jnp.int32, (rows, 128), 1)
    pick = lambda v: jnp.where(lane // 64 == half, v, jnp.zeros_like(v))
    q2, k2, v2, do2 = qkv_ref[:, at(0)], qkv_ref[:, at(1)], qkv_ref[:, at(2)], do_ref[:, at(0)]
    p = probs_ref[0].astype(jnp.float32)
    dp = dotf(pick(do2), v2, NT)
    ds = p * (dp - jnp.sum(p * dp, axis=1, keepdims=True))
    grad = (ds + dl_ref[0].astype(jnp.float32)).astype(jnp.bfloat16)
    dprev_ref[0] = grad
    dq = (dotf(grad, pick(k2), NN) * 0.125).astype(jnp.bfloat16)
    dk = (dotf(dprev_ref[0], pick(q2), TN) * 0.125).astype(jnp.bfloat16)
    dv = dotf(probs_ref[0], pick(do2), TN).astype(jnp.bfloat16)

    @pl.when(half == 0)
    def _():
        for i, v in enumerate((dq, dk, dv)):
            gp_ref[:, 128 * i:128 * (i + 1)] = v

    @pl.when(half == 1)
    def _():
        for i, v in enumerate((dq, dk, dv)):
            v = gp_ref[:, 128 * i:128 * (i + 1)] + v
            gp_ref[:, 128 * i:128 * (i + 1)] = v
            qkv_ref[:, at(i)] = v
            if i != 1:
                part_ref[4 + i // 2:5 + i // 2, at(0)] = jnp.sum(v.astype(jnp.float32), axis=0, keepdims=True)
        for p in range(0, heads // 2, 2):
            @pl.when(pair == p)
            def _():
                sc.finish(U + p // 2)
        to = pl.ds(pl.multiple_of(384 * lax.rem(pair, 2), 384), 384)
        ups[pair // 2, :, :, :, :, :, :, to] = dotf(x_ref[...], gp_ref[:, 0:384], TN).reshape(ups.shape[1:7] + (384,)).astype(jnp.bfloat16)
        for p in range(heads // 2):
            @pl.when(pair == p)
            def _():
                sc.r1(Q + p)

    @pl.when(g == heads - 1)
    def _():
        for d, tile_of in own_columns(part_ref[...], 32, columns):
            fvec_ref[d // 16, d // 8 % 2, d // 2 % 4, d % 2] = tile_of
        sc.r1(V)
        run("end")
        for d in last_w():
            d.wait()

        @pl.loop(0, 3)
        def _(i):
            acc_ref[...] += dotf(qkv_ref[:, pl.ds(pl.multiple_of(768 * i, 768), 768)], w_ref[i], NT)
            for j in range(3):
                @pl.when(i == j)
                def _():
                    run(("dx", j))
        dx_ref[...] = acc_ref[...].astype(jnp.bfloat16)
        run("last")
        squares = gvec_ref[0:8, :] * gvec_ref[0:8, :] + gvec_ref[8:16, :] * gvec_ref[8:16, :]
        for ref in (gin_ref, gout_ref):
            v = ref[...]
            v = jnp.sum(v * v, axis=0)
            for j in range(v.shape[1] // 128):
                squares = squares + v[:, 128 * j:128 * (j + 1)]
        nmine[0] = jnp.sum(squares, keepdims=True) + jnp.zeros((8, 128), jnp.float32)
        for i in range(7):
            share(i).start()
        for k in range(14):
            if k not in (0, 1, 2):
                sc.finish(k)
        for i in range(7):
            share(i).wait_recv()
        me = y * 4 + c * 2 + x

        def from_near(i):
            return me if i == 0 else lax.rem(y + i // 4, 2) * 4 + lax.rem(c + i // 2 % 2, 2) * 2 + lax.rem(x + i % 2, 2)
        plane = in_order([nmine[0]] + [ngot[i] for i in range(7)], from_near)
        nmine[1] = plane
        for i in range(7, 10):
            share(i).start()
        for i in range(7, 10):
            share(i).wait_recv()
        total = in_order([plane] + [ngot[i] for i in range(7, 10)], lambda i: lax.rem(z - i + 4, 4))
        norm_ref[...] = jnp.sqrt(total)
        for i in range(10):
            share(i).wait_send()


def backward_all(plan, columns, grad_down, hidden_low, small, two_sums, scale_one, probs, grad_logits,
                 activated, slope, full_out, full_up, full_qkv, grad_second, normed_one, mixed, tokens, qkv):
    rows, width = tokens.shape
    heads = probs.shape[0]
    hidden = activated.shape[1]
    f32, bf16 = jnp.float32, jnp.bfloat16
    fixed = lambda shape: pl.BlockSpec(shape, lambda g: (0,) * len(shape), pipeline_mode=pl.Buffered(1))
    head = pl.BlockSpec((1, rows, rows), lambda g: (g, 0, 0))
    hbm = pl.BlockSpec(memory_space=pl.ANY)
    r_in, r_out = full_qkv.shape[3] // 2, full_out.shape[3] // 2
    landing = []
    for r, n in [(r_in, 768)] * 4 + [(r_out, 256)] * 3 + [(r_in, 384)] * 6:
        landing += [pltpu.VMEM(lead + (r // 8, 8, n), bf16) for lead in ((2, 4, 2), (2, 4), (4,), (3,))]
    landing += [pltpu.VMEM(lead + (16, 128), f32) for lead in ((2, 4, 2), (2, 4), (4,), (3,))]
    lead = (2, 2, 4, 2)
    v = lambda *shape: pltpu.VMEM(shape, bf16)
    vf = lambda *shape: pltpu.VMEM(shape, f32)
    shapes = [((r_in // 8, 8, 3 * width + hidden), f32), ((r_out // 8, 8, width), f32), ((16, 128), f32), ((8, 128), f32)]
    dma = pltpu.SemaphoreType.DMA
    return pl.pallas_call(
        functools.partial(backward_kernel, heads, plan, columns),
        grid=(heads,),
        in_specs=[fixed((rows, width)), fixed((rows, width)), fixed(small.shape), fixed(two_sums.shape),
                  fixed(scale_one.shape), head, head] + [hbm] * 10,
        out_specs=[head, fixed((rows, width))] + [fixed(s) for s, _ in shapes],
        out_shape=[jax.ShapeDtypeStruct(probs.shape, bf16), jax.ShapeDtypeStruct((rows, width), bf16)]
        + [jax.ShapeDtypeStruct(s, t) for s, t in shapes],
        scratch_shapes=[v(rows, 3 * width), v(rows, width), v(rows, width), v(rows, width), v(rows, hidden),
                        v(rows, 768), v(rows, 768), v(3, 768, width), vf(rows, width), vf(rows, width),
                        vf(16, width), vf(*lead, 16, 128)]
        + [v(4, *lead, r_in // 8, 8, 768), v(3, *lead, r_out // 8, 8, 256)] + landing
        + [vf(2, 8, 128), vf(10, 8, 128), dma((14, 7)), dma((14, 7)), dma((10,)), dma((10,)), dma((10,))],
        compiler_params=pltpu.CompilerParams(collective_id=2, has_side_effects=True, vmem_limit_bytes=64 * 2**20 - 65536),
        name="backward",
    )(grad_down, hidden_low, small, two_sums, scale_one, probs, grad_logits,
      activated, slope, full_out, full_up, full_qkv, grad_second, normed_one, mixed, tokens, qkv)


def update_kernel(norm_ref, step_ref, *refs):
    through, refs = refs[:4], refs[4:]
    trios, refs = [refs[4 * i:4 * i + 4] for i in range(3)], refs[12:]
    through_out, refs = refs[:4], refs[4:]
    outs, gn_ref = [refs[5 * i:5 * i + 5] for i in range(3)], refs[15]
    for a, b in zip(through, through_out):
        b[...] = a[...]
    norm = norm_ref[0:1, 0:1]
    gn_ref[...] = norm
    factor = jnp.minimum(1.0, clip_scale * math.sqrt(PARAMS) / (norm + 1e-06))
    step = jnp.full((1, 1), step_ref[0], jnp.int32).astype(jnp.float32)
    one = 1.0 - jnp.exp(step * math.log(beta_one))
    two = 1.0 - jnp.exp(step * math.log(beta_two))
    for i, ((g_ref, w_ref, m_ref, v_ref), out) in enumerate(zip(trios, outs)):
        rate, decay = (rate_vector, 0.0) if i == 2 else (rate_matrix, decay_matrix)
        grad = g_ref[...].reshape(w_ref.shape) if i < 2 else g_ref[0:w_ref.shape[0], 0:w_ref.shape[1]]
        clipped = grad * factor
        moment = beta_one * m_ref[...] + (1.0 - beta_one) * clipped
        square = beta_two * v_ref[...] + (1.0 - beta_two) * clipped * clipped
        weight = w_ref[...] - rate * ((moment / one) / (jnp.sqrt(square / two) + adam_eps) + decay * w_ref[...])
        for ref, val in zip(out, (clipped, moment, square, weight, weight.astype(jnp.bfloat16))):
            ref[...] = val


def update_all(norm, step_count, through, trios):
    steps = 6
    f32 = jnp.float32

    def spec(a):
        if a.shape[-1] < 128 * steps:
            return pl.BlockSpec(a.shape, lambda g: (0,) * a.ndim)
        return pl.BlockSpec(a.shape[:-1] + (a.shape[-1] // steps,), lambda g: (0,) * (a.ndim - 1) + (g,))
    slabs = [pl.BlockSpec((a.shape[0] // steps,) + a.shape[1:], lambda g: (g, 0, 0)) if a.ndim == 3 else spec(a) for a in through]
    shapes = []
    for g, w, m, v in trios:
        shapes += [jax.ShapeDtypeStruct(w.shape, t) for t in (f32, f32, f32, f32, jnp.bfloat16)]
    flat = [a for trio in trios for a in trio]
    return pl.pallas_call(
        update_kernel,
        grid=(steps,),
        in_specs=[pl.BlockSpec((8, 128), lambda g: (0, 0)), pl.BlockSpec(memory_space=pltpu.SMEM)] + slabs + [spec(a) for a in flat],
        out_specs=slabs + [spec(s) for s in shapes] + [pl.BlockSpec((1, 1), lambda g: (0, 0))],
        out_shape=[jax.ShapeDtypeStruct(a.shape, a.dtype) for a in through] + shapes + [jax.ShapeDtypeStruct((1, 1), f32)],
        compiler_params=pltpu.CompilerParams(vmem_limit_bytes=64 * 2**20 - 65536),
        name="update",
    )(norm, step_count, *through, *flat)


def adam_update(master, moment, square, gradient, factor, step_value, step_rate, decay_rate):
    clipped = gradient * factor
    new_moment = beta_one * moment + (1.0 - beta_one) * clipped
    new_square = beta_two * square + (1.0 - beta_two) * clipped * clipped
    fixed_moment = new_moment / (1.0 - jnp.power(beta_one, step_value))
    fixed_square = new_square / (1.0 - jnp.power(beta_two, step_value))
    updated = master - step_rate * (
        fixed_moment / (jnp.sqrt(fixed_square) + adam_eps) + decay_rate * master
    )
    return (clipped, new_moment, new_square, updated)


def rounded(v):
    return lax.reduce_precision(v, 8, 7)


def gather_all(weight_in, weight_out, vectors, width):
    whole = lambda v: lax.all_gather(v, AXES, axis=0, tiled=True)
    low_in = weight_in.astype(jnp.bfloat16)
    small = lax.all_gather(rounded(vectors), AXES, axis=1, tiled=True)
    return whole(low_in[:, : 3 * width]), whole(low_in[:, 3 * width :]), whole(weight_out.astype(jnp.bfloat16)), small


def forward_plain(tokens, grad_out, full_qkv, full_up, full_out, small, prev, segments):
    width = tokens.shape[1]
    dot = lambda a, b: jnp.dot(a, b, preferred_element_type=jnp.float32)
    sums = lambda v: jnp.sum(v, axis=0, dtype=jnp.float32)
    offsets = jnp.concatenate([small[4], jnp.zeros_like(small[4]), small[5]])
    qkv = (dot(tokens, full_qkv) + offsets).astype(jnp.bfloat16)
    logits, mixed, log_sums = attn_fwd(qkv, prev, segments, 640)
    first = tokens.astype(jnp.float32) + (dot(mixed, full_out[:width]) + small[6])
    hidden_one, normed_one, scale_one = norm_rows(first, small[0], small[2])
    hidden_low = hidden_one.astype(jnp.bfloat16)
    upward = dot(hidden_low, full_up) + small[8:].reshape(-1)
    activated, gelu_pull = jax.vjp(gelu_exact, upward)
    activated, slope = activated.astype(jnp.bfloat16), gelu_pull(jnp.ones_like(upward))[0]
    second = hidden_one + (dot(activated, full_out[width:]) + small[7])
    output, normed_two, scale_two = norm_rows(second, small[1], small[3])
    grad_output = grad_out.astype(jnp.float32)
    grad_second = norm_back(grad_output, normed_two, scale_two, small[1])
    grad_down = grad_second.astype(jnp.bfloat16)
    two_sums = jnp.stack([sums(grad_output * normed_two), sums(grad_output), sums(grad_down)])
    return (logits, qkv, mixed, log_sums, hidden_low, normed_one, scale_one, activated, slope, output.astype(jnp.bfloat16),
            grad_second, grad_down, two_sums)


def reduce_all(grad_qkv, grad_up, grad_out, small, shards):
    part = lambda v: lax.psum_scatter(v, AXES, scatter_dimension=0, tiled=True).astype(jnp.float32)
    owned_in = jnp.concatenate([part(grad_qkv), part(grad_up)], axis=1)
    owned_out = part(grad_out)
    owned_small = lax.psum_scatter(small, AXES, scatter_dimension=1, tiled=True)
    total = lax.psum(jnp.sum(owned_in**2) + jnp.sum(owned_out**2) + jnp.sum(owned_small**2), AXES)
    return owned_in, owned_out, owned_small, jnp.sqrt(total)


def body(remote, hidden_in, prev_logits, segment_ids, d_hidden, d_logits, weight_in, weight_out, vectors,
         moment_in, moment_out, moment_vectors, square_in, square_out, square_vectors, step_count):
    width = weight_out.shape[1]
    shards = lax.axis_size("dp") * lax.axis_size("fsdp")
    dot = lambda spec, a, b: jnp.einsum(spec, a, b, preferred_element_type=jnp.float32)
    sums = lambda v: jnp.sum(v, axis=0, dtype=jnp.float32)
    segments = segment_ids[0]
    if remote:
        (logits, probs, full_qkv, full_up, full_out, qkv, mixed, hidden_low, normed_one, activated, slope, small, scale_one,
         output, grad_second, grad_down, two_sums) = forward_all(
             FORWARD_PLAN, ROUTES, hidden_in, d_hidden, weight_in, weight_out, vectors, prev_logits[0], segments)
        grad_prev, grad_tokens, grad_in, grad_out, grad_vec, norm = backward_all(
            BACKWARD_PLAN, vectors.shape[1], grad_down, hidden_low, small, two_sums, scale_one, probs, d_logits[0],
            activated, slope, full_out, full_up, full_qkv, grad_second, normed_one, mixed, hidden_in, qkv)
        (logits, grad_prev, output, grad_tokens, *states, grad_norm) = update_all(
            norm, step_count, [logits, grad_prev, output, grad_tokens],
            [(grad_in, weight_in, moment_in, square_in), (grad_out, weight_out, moment_out, square_out),
             (grad_vec, vectors, moment_vectors, square_vectors)])
        clipped, moments, squares, updated, copies = [states[i::5] for i in range(5)]
        return (output, logits[None], grad_tokens, grad_prev[None], *clipped, *moments, *squares, *updated, *copies, grad_norm[0, 0])
    (full_qkv, full_up, full_out, small) = gather_all(weight_in, weight_out, vectors, width)
    (logits, qkv, mixed, log_sums, hidden_low, normed_one, scale_one, activated, slope, output,
     grad_second, grad_down, two_sums) = forward_plain(hidden_in, d_hidden, full_qkv, full_up, full_out, small, prev_logits[0], segments)
    w_attn, w_down = full_out[:width], full_out[width:]
    down_grad = dot("tf,td->fd", activated, grad_down).astype(jnp.bfloat16)
    grad_up = (dot("td,fd->tf", grad_down, w_down) * slope).astype(jnp.bfloat16)
    up_grad = dot("td,tf->df", hidden_low, grad_up).astype(jnp.bfloat16)
    grad_one = grad_second + dot("tf,df->td", grad_up, full_up)
    grad_first = norm_back(grad_one, normed_one, scale_one, small[0])
    grad_attn = grad_first.astype(jnp.bfloat16)
    attn_grad = dot("tc,td->cd", mixed, grad_attn).astype(jnp.bfloat16)
    grad_mixed = dot("td,cd->tc", grad_attn, w_attn).astype(jnp.bfloat16)
    grad_prev, grad_q, grad_k, grad_v = attn_bwd(qkv, grad_mixed, prev_logits[0], d_logits[0], log_sums, segments, 640)
    grad_qkv = jnp.concatenate([grad_q, grad_k, grad_v], axis=1)
    qkv_grad = dot("td,tc->dc", hidden_in, grad_qkv).astype(jnp.bfloat16)
    grad_tokens = (grad_first + dot("tc,dc->td", grad_qkv, full_qkv)).astype(jnp.bfloat16)
    small_grad = jnp.concatenate([
        jnp.stack([sums(grad_one * normed_one), two_sums[0], sums(grad_one), two_sums[1],
                   sums(grad_q), sums(grad_v), sums(grad_attn), two_sums[2]]),
        sums(grad_up).reshape(-1, width)], axis=0)

    owned_in, owned_out, owned_small, grad_norm = reduce_all(
        qkv_grad, up_grad, jnp.concatenate([attn_grad, down_grad], axis=0), small_grad, shards)
    factor = jnp.minimum(1.0, clip_scale * math.sqrt(PARAMS) / (grad_norm + 1e-06))
    step_value = step_count[0].astype(jnp.float32)
    new = [
        adam_update(weight_in, moment_in, square_in, owned_in, factor, step_value, rate_matrix, decay_matrix),
        adam_update(weight_out, moment_out, square_out, owned_out, factor, step_value, rate_matrix, decay_matrix),
        adam_update(vectors, moment_vectors, square_vectors, owned_small, factor, step_value, rate_vector, 0.0),
    ]
    clipped, moments, squares, updated = zip(*new)
    return (output.astype(jnp.bfloat16), logits[None], grad_tokens, grad_prev[None],
            *clipped, *moments, *squares, *updated, *[u.astype(jnp.bfloat16) for u in updated], grad_norm)


def solution(mesh):
    remote = (mesh.shape["dp"], mesh.shape["fsdp"]) == (4, 8)
    rows = P(AXES, None)
    heads = P(AXES, None, None, None)
    cols = P(None, AXES)
    trio = (rows, rows, cols)
    return jax.shard_map(
        functools.partial(body, remote),
        mesh=mesh,
        in_specs=(rows, heads, rows, rows, heads, *trio, *trio, *trio, P()),
        out_specs=(rows, heads, rows, heads, *trio, *trio, *trio, *trio, *trio, P()),
        check_vma=False,
    )
```

```python
import functools
import math

import jax
import jax.numpy as jnp
from jax import lax
from jax.experimental import pallas as pl
from jax.experimental.pallas import tpu as pltpu
from jax.sharding import PartitionSpec as P

PARAMS = 7087104


norm_eps = 1e-12
clip_scale = 1.0
beta_one = 0.9
beta_two = 0.999
adam_eps = 1e-08
rate_matrix = 0.06
rate_vector = 0.25
decay_matrix = 0.01
NEG = -1e30
NT = (((1,), (1,)), ((), ()))
NN = (((1,), (0,)), ((), ()))
TN = (((0,), (0,)), ((), ()))
AXES = ("dp", "fsdp")


def gelu_exact(upward):
    return jax.nn.gelu(upward, approximate=False)


def norm_rows(residual, gain_row, shift_row):
    centered = residual - jnp.mean(residual, axis=1, keepdims=True)
    scaling = lax.rsqrt(jnp.mean(centered * centered, axis=1, keepdims=True) + norm_eps)
    normed = centered * scaling
    return (normed * gain_row + shift_row, normed, scaling)


def norm_back(grad_after, normed, scaling, gain_row):
    scaled_grad = grad_after * gain_row
    return scaling * (
        scaled_grad
        - jnp.mean(scaled_grad, axis=1, keepdims=True)
        - normed * jnp.mean(scaled_grad * normed, axis=1, keepdims=True)
    )


def dotf(a, b, dims):
    return lax.dot_general(a, b, dims, preferred_element_type=jnp.float32)

def half_masks(rows):
    lane = lax.broadcasted_iota(jnp.int32, (rows, 128), 1)
    return lane < 64

def attn_fwd_kernel(BR, q_ref, k_ref, v_ref, prev_ref, srow_ref, scol_ref, logits_ref, mixed_ref, lse_ref, mask_ref):
    g = pl.program_id(0)
    rows = q_ref.shape[0]
    @pl.when(g == 0)
    def _():
        mask_ref[...] = jnp.where(scol_ref[...] == srow_ref[...], 0.0, NEG)
        lse_ref[...] = jnp.zeros_like(lse_ref)
    k2 = k_ref[...]
    v2 = v_ref[...]
    left = half_masks(rows)
    zero = jnp.zeros_like(v2)
    va = jnp.where(left, v2, zero)
    vb = jnp.where(left, zero, v2)
    for rb in range(rows // BR):
        sl = pl.ds(rb * BR, BR)
        q2 = q_ref[sl, :] * jnp.bfloat16(0.125)
        lb = half_masks(BR)
        outs = []
        lses = []
        for h in range(2):
            qh = jnp.where(lb if h == 0 else ~lb, q2, jnp.zeros_like(q2))
            raw = dotf(qh, k2, NT) + prev_ref[h, sl, :].astype(jnp.float32)
            logits_ref[h, sl, :] = raw.astype(jnp.bfloat16)
            s = raw + mask_ref[sl, :]
            m = jnp.max(s, axis=1, keepdims=True)
            e = jnp.exp(s - m)
            tot = jnp.sum(e, axis=1, keepdims=True)
            o = dotf(e.astype(jnp.bfloat16), va if h == 0 else vb, NN)
            outs.append(o / tot)
            lses.append(m + jnp.log(tot))
        mixed_ref[sl, :] = (outs[0] + outs[1]).astype(jnp.bfloat16)
        lane = lax.broadcasted_iota(jnp.int32, (BR, 128), 1)
        cur = lse_ref[sl, :]
        cur = jnp.where(lane == 2 * g, lses[0], cur)
        cur = jnp.where(lane == 2 * g + 1, lses[1], cur)
        lse_ref[sl, :] = cur

def attn_fwd(qkv, prev, seg, BR=128):
    rows = qkv.shape[0]
    heads = prev.shape[0]
    G = heads // 2
    srow = seg.reshape(1, rows); scol = seg.reshape(rows, 1)
    return pl.pallas_call(
        functools.partial(attn_fwd_kernel, BR),
        grid=(G,),
        in_specs=[
            pl.BlockSpec((rows, 128), lambda g: (0, g)),
            pl.BlockSpec((rows, 128), lambda g: (0, G + g)),
            pl.BlockSpec((rows, 128), lambda g: (0, 2 * G + g)),
            pl.BlockSpec((2, rows, rows), lambda g: (g, 0, 0)),
            pl.BlockSpec((1, rows), lambda g: (0, 0)),
            pl.BlockSpec((rows, 1), lambda g: (0, 0)),
        ],
        out_specs=[
            pl.BlockSpec((2, rows, rows), lambda g: (g, 0, 0)),
            pl.BlockSpec((rows, 128), lambda g: (0, g)),
            pl.BlockSpec((rows, 128), lambda g: (0, 0)),
        ],
        out_shape=[
            jax.ShapeDtypeStruct((heads, rows, rows), jnp.bfloat16),
            jax.ShapeDtypeStruct((rows, heads * 64), jnp.bfloat16),
            jax.ShapeDtypeStruct((rows, 128), jnp.float32),
        ],
        scratch_shapes=[pltpu.VMEM((rows, rows), jnp.float32)],
        compiler_params=pltpu.CompilerParams(vmem_limit_bytes=60 * 2**20),
        name="attn_fwd",
    )(qkv, qkv, qkv, prev, srow, scol)

def attn_bwd_kernel(BR, q_ref, k_ref, v_ref, do_ref, prev_ref, dl_ref, lse_ref, srow_ref, scol_ref,
                    dprev_ref, dq_ref, dk_ref, dv_ref, mask_ref, p_ref, g_ref):
    g = pl.program_id(0)
    rows = q_ref.shape[0]
    @pl.when(g == 0)
    def _():
        mask_ref[...] = jnp.where(scol_ref[...] == srow_ref[...], 0.0, NEG)
    k2 = k_ref[...]
    v2 = v_ref[...]
    left = half_masks(rows)
    zero = jnp.zeros_like(v2)
    for h in range(2):
        lm = left if h == 0 else ~left
        kh = jnp.where(lm, k2, zero)
        for rb in range(rows // BR):
            sl = pl.ds(rb * BR, BR)
            lb = half_masks(BR)
            lb = lb if h == 0 else ~lb
            q2 = q_ref[sl, :] * jnp.bfloat16(0.125)
            qh = jnp.where(lb, q2, jnp.zeros_like(q2))
            doh = jnp.where(lb, do_ref[sl, :], jnp.zeros_like(q2))
            lane = lax.broadcasted_iota(jnp.int32, (BR, 128), 1)
            lse = jnp.sum(jnp.where(lane == 2 * g + h, lse_ref[sl, :], 0.0), axis=1, keepdims=True)
            s = dotf(qh, k2, NT) + prev_ref[h, sl, :].astype(jnp.float32) + mask_ref[sl, :]
            p = jnp.exp(s - lse)
            dp = dotf(doh, v2, NT)
            delta = jnp.sum(p * dp, axis=1, keepdims=True)
            ds = p * (dp - delta)
            gt = (ds + dl_ref[h, sl, :].astype(jnp.float32)).astype(jnp.bfloat16)
            dprev_ref[h, sl, :] = gt
            p_ref[sl, :] = p.astype(jnp.bfloat16)
            dq = dotf(gt, kh, NN) * 0.125
            if h == 0:
                dq_ref[sl, :] = dq.astype(jnp.bfloat16)
            else:
                dq_ref[sl, :] = dq_ref[sl, :] + dq.astype(jnp.bfloat16)
        qh = jnp.where(lm, q_ref[...], zero)
        doh = jnp.where(lm, do_ref[...], zero)
        dk = (dotf(dprev_ref[h], qh, TN) * 0.125).astype(jnp.bfloat16)
        dv = dotf(p_ref[...], doh, TN).astype(jnp.bfloat16)
        if h == 0:
            dk_ref[...] = dk
            dv_ref[...] = dv
        else:
            dk_ref[...] = dk_ref[...] + dk
            dv_ref[...] = dv_ref[...] + dv

def attn_bwd(qkv, do, prev, dl, lse, seg, BR=128):
    rows = qkv.shape[0]
    heads = prev.shape[0]
    G = heads // 2
    srow = seg.reshape(1, rows); scol = seg.reshape(rows, 1)
    col = lambda off: pl.BlockSpec((rows, 128), lambda g: (0, off + g))
    return pl.pallas_call(
        functools.partial(attn_bwd_kernel, BR),
        grid=(G,),
        in_specs=[
            col(0), col(G), col(2 * G), col(0),
            pl.BlockSpec((2, rows, rows), lambda g: (g, 0, 0)),
            pl.BlockSpec((2, rows, rows), lambda g: (g, 0, 0)),
            pl.BlockSpec((rows, 128), lambda g: (0, 0)),
            pl.BlockSpec((1, rows), lambda g: (0, 0)),
            pl.BlockSpec((rows, 1), lambda g: (0, 0)),
        ],
        out_specs=[
            pl.BlockSpec((2, rows, rows), lambda g: (g, 0, 0)),
            col(0), col(0), col(0),
        ],
        out_shape=[
            jax.ShapeDtypeStruct((heads, rows, rows), jnp.bfloat16),
        ] + [jax.ShapeDtypeStruct((rows, heads * 64), jnp.bfloat16)] * 3,
        scratch_shapes=[pltpu.VMEM((rows, rows), jnp.float32), pltpu.VMEM((rows, rows), jnp.bfloat16), pltpu.VMEM((8, 128), jnp.float32)],
        compiler_params=pltpu.CompilerParams(vmem_limit_bytes=60 * 2**20),
        name="attn_bwd",
    )(qkv, qkv, qkv, do, prev, dl, lse, srow, scol)


MESH = pl.DeviceIdType.MESH


def coords():
    dp = lax.axis_index("dp"); fs = lax.axis_index("fsdp")
    y = dp // 2; c = lax.rem(dp, 2)
    z = fs // 2; x = lax.rem(fs, 2)
    return y, c, z, x

def dev(y, c, z, x):
    return (y * 2 + c, z * 2 + x)


ROUTES = "zzzzzzznnnn"
BACKWARD_ROUTES = "nzzznzzzzznzzz"
FORWARD_PLAN = {
    "start": [(1, 7), (1, 8), (1, 9), (1, 10), (1, 0), (2, 0), (1, 1), (3, 0)],
    ("q", 0): [(1, 2), (2, 1), (1, 3), (2, 2), (3, 1)],
    ("q", 1): [(2, 3), (1, 4), (3, 2)],
    ("q", 2): [(3, 3), (1, 5)],
    ("pair", 0): [(2, 4), (1, 6)],
    ("pair", 2): [(2, 5)],
    ("pair", 3): [(3, 4)],
    ("pair", 5): [(2, 6)],
    "out": [(3, 5), (2, 7), (3, 6), (2, 8)],
    "norm": [(3, 7), (2, 9)],
    ("up", 0): [(3, 8), (2, 10)],
    ("up", 1): [(3, 9)],
    ("up", 2): [(3, 10)],
}
BACKWARD_PLAN = {
    ("down", 1): [(2, 0)],
    ("down", 2): [(2, 1)],
    ("down", 3): [(3, 0), (2, 2)],
    ("up", 3): [(3, 1)],
    "norm": [(2, 3)],
    "out": [(4, 0), (4, 1), (3, 2), (3, 3)],
    ("head", 1): [(5, 0), (2, 4), (4, 2)],
    ("head", 2): [(4, 3), (5, 1), (2, 5)],
    ("head", 4): [(3, 4), (2, 6), (5, 2)],
    ("head", 5): [(5, 3)],
    ("head", 6): [(3, 5)],
    ("head", 8): [(3, 6)],
    ("head", 9): [(4, 5), (2, 7), (2, 8)],
    ("head", 10): [(4, 4), (4, 6), (2, 9), (3, 7)],
    ("head", 11): [(3, 8), (2, 10), (5, 4), (2, 11)],
    "end": [(4, 7), (4, 8), (3, 9), (5, 5), (3, 10)],
    ("dx", 0): [(2, 12), (3, 11)],
    ("dx", 1): [(4, 9), (2, 13), (5, 6)],
    "last": [(5, 7), (3, 12), (5, 8), (4, 11), (3, 13), (4, 12), (4, 10), (4, 13), (5, 9), (5, 10), (5, 11), (5, 12), (5, 13)],
}


class Gather:
    def __init__(self, chunks, routes, sources, wholes, send_sem, recv_sem):
        self.chunks, self.routes, self.sources, self.wholes = chunks, routes, sources, wholes
        self.send_sem, self.recv_sem = send_sem, recv_sem
        self.y, self.c, self.z, self.x = coords()

    def part(self, k):
        array, start, size, origin = self.chunks[k]
        return self.wholes[array], pl.ds(start, size), self.sources[array].at[:, pl.ds(origin, size)]

    def rows_of(self, k, x):
        size = self.sources[self.chunks[k][0]].shape[0]
        return pl.ds(pl.multiple_of(size * x, 8), size)

    def copy(self, src, dst, k, slot, who):
        return pltpu.make_async_remote_copy(
            src_ref=src, dst_ref=dst, send_sem=self.send_sem.at[k, slot], recv_sem=self.recv_sem.at[k, slot],
            device_id=who, device_id_type=MESH)

    def along_z(self, k):
        whole, cols, mine = self.part(k)
        spot = whole.at[self.y, self.c, self.z, self.rows_of(k, self.x), cols]
        return [self.copy(mine, spot, k, d, dev(self.y, self.c, lax.rem(self.z + d + 1, 4), self.x)) for d in range(3)]

    def across(self):
        return jnp.where(self.c == 0, self.y, 1 - self.y), jnp.where(self.c == 0, 1 - self.x, self.x)

    def other(self):
        return (jnp.where(self.c == 0, 1 - self.y, self.y) * 2 + self.c, self.z * 2 + jnp.where(self.c == 0, self.x, 1 - self.x))

    def block(self, k, y, x):
        whole, cols, _ = self.part(k)
        return whole.at[y, self.c, :, self.rows_of(k, x), cols]

    def to_neighbours(self, k):
        block = self.block(k, self.y, self.x)
        return [self.copy(block, block, k, 3, dev(self.y, self.c, self.z, 1 - self.x)),
                self.copy(block, block, k, 4, dev(1 - self.y, self.c, self.z, self.x))]

    def handed_on(self, k):
        block = self.block(k, *self.across())
        return self.copy(block, block, k, 3 + self.c, self.other()), self.copy(block, block, k, 5, self.other()), self.copy(block, block, k, 4 - self.c, self.other())

    def early(self, k):
        whole, cols, mine = self.part(k)
        y, x = self.across()
        return self.copy(mine, whole.at[self.y, self.c, self.z, self.rows_of(k, self.x), cols], k, 3, dev(y, self.c, self.z, x))

    def relayed(self, k):
        whole, cols, _ = self.part(k)
        y, x = self.across()
        spot = whole.at[y, self.c, self.z, self.rows_of(k, x), cols]
        return [self.copy(spot, spot, k, 4 + d, dev(self.y, self.c, lax.rem(self.z + d + 1, 4), self.x)) for d in range(3)]

    def halves(self, k):
        own, far = self.block(k, self.y, self.x), self.block(k, *self.across())
        return [self.copy(own, own, k, 7, self.other()), self.copy(far, far, k, 8, self.other())]

    def to_core(self, k):
        whole, cols, _ = self.part(k)
        plane = whole.at[:, self.c, :, :, cols]
        return self.copy(plane, plane, k, 9, dev(self.y, 1 - self.c, self.z, self.x))

    def start(self, k):
        if self.routes[k] == "n":
            self.early(k).start()
        for d in self.along_z(k):
            d.start()

    def s1(self, k):
        if self.routes[k] == "n":
            self.early(k).wait_recv()
            for d in self.relayed(k):
                d.start()
            return
        for d in self.along_z(k):
            d.wait_recv()
        for d in self.to_neighbours(k):
            d.start()

    def s2(self, k):
        if self.routes[k] == "n":
            for d in self.along_z(k) + self.relayed(k):
                d.wait_recv()
            for d in self.halves(k):
                d.start()
            return
        got, on, _ = self.handed_on(k)
        got.wait_recv()
        on.start()

    def s3(self, k):
        if self.routes[k] == "n":
            for d in self.halves(k):
                d.wait_recv()
        else:
            _, on, other = self.handed_on(k)
            other.wait_recv()
            on.wait_recv()
        self.to_core(k).start()

    def s4(self, k):
        self.to_core(k).wait_recv()

    def finish(self, k):
        if self.routes[k] == "n":
            sent = [self.early(k), *self.relayed(k), *self.halves(k)]
        else:
            sent = self.to_neighbours(k) + [self.handed_on(k)[1]]
        for d in self.along_z(k) + sent + [self.to_core(k)]:
            d.wait_send()


def peers_of(y, c, z, x):
    return [dev(y, c, lax.rem(z + d, 4), x) for d in (1, 2, 3)] + [dev(y, c, z, 1 - x), dev(1 - y, c, z, x), dev(y, 1 - c, z, x)]


def normalise(v):
    centered = v - jnp.mean(v, axis=1, keepdims=True)
    scaling = lax.rsqrt(jnp.mean(centered * centered, axis=1, keepdims=True) + norm_eps)
    return centered * scaling, scaling


def spread_columns(ref, shards, columns, rows, width):
    lane = lax.broadcasted_iota(jnp.int32, (rows, 128), 1)
    blocks = [jnp.zeros((rows, 128), jnp.float32) for _ in range(width // 128)]
    for d in range(shards):
        at, off = columns * d // 128, columns * d % 128
        tile = ref[d // 16, d // 8 % 2, d // 2 % 4, 16 * (d % 2):16 * (d % 2) + 16, :][:rows]
        tile = pltpu.roll(tile, off, 1) if off else tile
        if off + columns > 128:
            blocks[at + 1] = blocks[at + 1] + jnp.where(lane < off, tile, 0.0)
            tile = jnp.where(lane < off, 0.0, tile)
        blocks[at] = blocks[at] + tile
    return blocks


def forward_kernel(plan, routes, win_ref, wout_ref, vec_ref, srow_ref, prev_ref, x_hbm, dout_hbm,
                   logits_ref, probs_ref, gq_ref, gu_ref, go_ref, qkv_hbm, mixed_hbm, hlow_hbm, none_hbm, act_hbm, gp_hbm, out_hbm, dsec_hbm, ddown_hbm,
                   small_ref, sone_ref, sums_ref,
                   gv_ref, mask_ref, cin_ref, cout_ref, cvec_ref, w_ref, wo_ref, x_ref, dout_ref, qkv_ref, mixed_ref, hlow_ref, none_ref,
                   act_ref, gp_ref, hid_ref, sec_ref, out_ref, dsec_ref, ddown_ref, send_sem, recv_sem, loc_sem, out_sem, row_sem):
    g = pl.program_id(0)
    rows, width = x_hbm.shape
    hidden = act_hbm.shape[1]
    last = pl.num_programs(0) - 1
    tile = 256
    y, c, z, x = coords()
    V, Q, O, U = 0, 1, 4, 7
    chunks = [(3, 0, 128, 0)] + [(0, 768 * i, 768, 768 * i) for i in range(3)] + [(2, 256 * i, 256, 256 * i) for i in range(3)]
    chunks += [(1, 768 * i, 768, 3 * width + 768 * i) for i in range(4)]
    ga = Gather(chunks, routes, [cin_ref, cin_ref, cout_ref, cvec_ref], [gq_ref, gu_ref, go_ref, gv_ref], send_sem, recv_sem)

    def run(place):
        for stage, k in plan.get(place, ()):
            (ga.s1, ga.s2, ga.s3)[stage - 1](k)

    def load(src, dst, i):
        return pltpu.make_async_copy(src, dst, loc_sem.at[i])

    def save(src, dst, i):
        return pltpu.make_async_copy(src, dst, out_sem.at[i])

    stores = lambda: [load(cin_ref.at[:, pl.ds(0, 3 * width)], gq_ref.at[y, c, z, ga.rows_of(Q, x)], 0),
                      load(cin_ref.at[:, pl.ds(3 * width, hidden)], gu_ref.at[y, c, z, ga.rows_of(U, x)], 1),
                      load(cout_ref, go_ref.at[y, c, z, ga.rows_of(O, x)], 2)]
    x_in, dout_in = lambda: load(x_hbm, x_ref, 3), lambda: load(dout_hbm, dout_ref, 4)
    w_out, w_up, w_qkv = go_ref.reshape(width + hidden, width), gu_ref.reshape(width, hidden), gq_ref.reshape(width, 3 * width)

    def quarters(src, columns, slot):
        size = width // 4
        return [load(src.at[pl.ds(size * i, size), columns], w_ref.at[slot, pl.ds(size * i, size), :], 8 + 4 * slot + i) for i in range(4)]
    w_q = lambda k: quarters(w_qkv, pl.ds(768 * k, 768), k % 2)
    w_u = lambda k: quarters(w_up, pl.ds(768 * k, 768), (k + 1) % 2)
    w_o = lambda: quarters(w_out, slice(None), 0)
    w_down = lambda: load(w_out.at[pl.ds(width, hidden), :], wo_ref, 7)
    saves = {"mixed": lambda: save(mixed_ref, mixed_hbm, 1), "hlow": lambda: save(hlow_ref, hlow_hbm, 2),
             "none": lambda: save(none_ref, none_hbm, 3), "qkv": lambda: save(qkv_ref, qkv_hbm, 4)}
    save_act = lambda k: save(act_ref.at[:, pl.ds(768 * k, 768)], act_hbm.at[:, pl.ds(768 * k, 768)], 5 + k)
    save_gp = lambda k: save(gp_ref.at[k % 2], gp_hbm.at[:, pl.ds(768 * k, 768)], 9 + k)

    @pl.when(g == 0)
    def _():
        barrier = pltpu.get_barrier_semaphore()
        peers = peers_of(y, c, z, x)
        for p in peers:
            pl.semaphore_signal(barrier, inc=1, device_id=p, device_id_type=MESH)
        cvec_ref[...] = jnp.zeros_like(cvec_ref)
        vec = vec_ref[...].astype(jnp.bfloat16).astype(jnp.float32)
        cvec_ref[0:vec.shape[0], 0:vec.shape[1]] = vec
        gv_ref[y, c, z, ga.rows_of(V, x), :] = cvec_ref[...]
        cin_ref[...] = win_ref[...].astype(jnp.bfloat16)
        cout_ref[...] = wout_ref[...].astype(jnp.bfloat16)
        pl.semaphore_wait(barrier, len(peers))
        for k in range(len(chunks)):
            ga.start(k)
        for s in stores():
            s.start()
        x_in().start()
        seg = jnp.broadcast_to(srow_ref[...].astype(jnp.float32), (rows, rows))
        mask_ref[...] = jnp.where(seg == seg.T, 0.0, NEG)
        for s in stores():
            s.wait()
        dout_in().start()
        run("start")
        ga.s4(V)
        run("small")
        spread = spread_columns(gv_ref, 32, vec_ref.shape[1], vec_ref.shape[0], width)
        for i, v in enumerate(spread):
            small_ref[:, 128 * i:128 * (i + 1)] = v
        x_in().wait()

        @pl.loop(0, 3)
        def _(k):
            for i in range(3):
                @pl.when(k == i)
                def _():
                    run(("q", i))
                    ga.s4(Q + i)
                    for d in w_q(i):
                        d.start()
                    run(("qw", i))
                    for d in w_q(i):
                        d.wait()
            bias = jnp.where(k == 1, 0.0, small_ref[pl.ds(4 + k // 2, 1), :])
            v = dotf(x_ref[...], w_ref[lax.rem(k, 2)], NN) + bias
            qkv_ref[:, pl.ds(pl.multiple_of(768 * k, 768), 768)] = v.astype(jnp.bfloat16)
        saves["qkv"]().start()

    for i in range(6):
        if plan.get(("pair", i)):
            @pl.when(g == i)
            def _():
                run(("pair", i))

    at = lambda off: pl.ds(pl.multiple_of(off * width + g * 128, 128), 128)
    left = half_masks(rows)
    q2 = qkv_ref[:, at(0)] * jnp.bfloat16(0.125)
    k2 = qkv_ref[:, at(1)]
    v2 = qkv_ref[:, at(2)]
    zero = jnp.zeros_like(v2)
    outs = []
    for h in range(2):
        pick = (lambda v: jnp.where(left, v, zero)) if h == 0 else (lambda v: jnp.where(left, zero, v))
        raw = dotf(pick(q2), k2, NT) + prev_ref[h].astype(jnp.float32)
        logits_ref[h] = raw.astype(jnp.bfloat16)
        s = raw + mask_ref[...]
        e = jnp.exp(s - jnp.max(s, axis=1, keepdims=True))
        probs = (e * (1.0 / jnp.sum(e, axis=1, keepdims=True))).astype(jnp.bfloat16)
        probs_ref[h] = probs
        outs.append(dotf(probs, pick(v2), NN))
    mixed_ref[:, pl.ds(pl.multiple_of(g * 128, 128), 128)] = (outs[0] + outs[1]).astype(jnp.bfloat16)

    @pl.when(g == last)
    def _():
        saves["mixed"]().start()
        run("out")
        for k in range(3):
            ga.s4(O + k)
        for d in w_o():
            d.start()
        w_down().start()
        run("outw")
        for d in w_o():
            d.wait()
        hid_ref[...] = x_ref[...].astype(jnp.float32) + (dotf(mixed_ref[...], w_ref[0], NN) + small_ref[6:7, :])
        run("norm")

        @pl.loop(0, rows // 128)
        def _(i):
            sl = pl.ds(pl.multiple_of(i * 128, 128), 128)
            normed, scaling = normalise(hid_ref[sl, :])
            none_ref[sl, :] = normed
            sone_ref[sl, :] = jnp.broadcast_to(scaling, (128, 128))
            hid = normed * small_ref[0:1, :] + small_ref[2:3, :]
            sec_ref[sl, :] = hid + small_ref[7:8, :]
            hlow_ref[sl, :] = hid.astype(jnp.bfloat16)

        saves["none"]().start()
        saves["hlow"]().start()

        @pl.loop(0, 4)
        def _(k):
            for i in range(4):
                @pl.when(k == i)
                def _():
                    run(("up", i))
                    ga.s4(U + i)
                    for d in w_u(i):
                        d.start()
                    run(("upw", i))
                    for d in w_u(i):
                        d.wait()
                    if i >= 2:
                        save_gp(i - 2).wait()

            @pl.loop(0, 768 // tile)
            def _(j):
                sl = pl.ds(pl.multiple_of(j * tile, tile), tile)
                to = pl.ds(pl.multiple_of(768 * k + j * tile, tile), tile)
                u = dotf(hlow_ref[...], w_ref[lax.rem(k + 1, 2), :, sl], NN) + small_ref[pl.ds(8 + k, 1), sl]
                cdf = 0.5 * (1.0 + lax.erf(u * math.sqrt(0.5)))
                act_ref[:, to] = (u * cdf).astype(jnp.bfloat16)
                gp_ref[lax.rem(k, 2), :, sl] = (cdf + u * (jnp.exp(-0.5 * (u * u)) * (1.0 / math.sqrt(2.0 * math.pi)))).astype(jnp.bfloat16)
            for i in range(4):
                @pl.when(k == i)
                def _():
                    save_act(i).start()
                    save_gp(i).start()
                    if i == 0:
                        w_down().wait()
            part = pl.ds(pl.multiple_of(768 * k, 768), 768)
            sec_ref[...] += dotf(act_ref[:, part], wo_ref[part, :], NN)
        sums_ref[...] = jnp.zeros_like(sums_ref)
        dout_in().wait()

        def row_saves(i):
            sl = pl.ds(pl.multiple_of(i * 128, 128), 128)
            return [pltpu.make_async_copy(a.at[sl, :], b.at[sl, :], row_sem.at[n, i])
                    for n, (a, b) in enumerate(((out_ref, out_hbm), (dsec_ref, dsec_hbm), (ddown_ref, ddown_hbm)))]

        @pl.loop(0, rows // 128)
        def _(i):
            sl = pl.ds(pl.multiple_of(i * 128, 128), 128)
            normed, scaling = normalise(sec_ref[sl, :])
            out_ref[sl, :] = (normed * small_ref[1:2, :] + small_ref[3:4, :]).astype(jnp.bfloat16)
            dy = dout_ref[sl, :].astype(jnp.float32)
            back = norm_back(dy, normed, scaling, small_ref[1:2, :])
            low = back.astype(jnp.bfloat16)
            dsec_ref[sl, :] = back
            ddown_ref[sl, :] = low
            sums_ref[0:1, :] += jnp.sum(dy * normed, axis=0, keepdims=True)
            sums_ref[1:2, :] += jnp.sum(dy, axis=0, keepdims=True)
            sums_ref[2:3, :] += jnp.sum(low.astype(jnp.float32), axis=0, keepdims=True)
            for d in row_saves(i):
                d.start()
        for k in range(len(chunks)):
            ga.finish(k)
        for s in saves.values():
            s().wait()
        for k in range(4):
            save_act(k).wait()
        for k in (2, 3):
            save_gp(k).wait()

        @pl.loop(0, rows // 128)
        def _(i):
            for d in row_saves(i):
                d.wait()


def forward_all(plan, routes, tokens, grad_out, weight_in, weight_out, vectors, prev, seg):
    rows, width = tokens.shape
    heads = prev.shape[0]
    hidden = weight_in.shape[1] - 3 * width
    f32, bf16 = jnp.float32, jnp.bfloat16
    fixed = lambda shape: pl.BlockSpec(shape, lambda g: (0,) * len(shape), pipeline_mode=pl.Buffered(1))
    pair = pl.BlockSpec((2, rows, rows), lambda g: (g, 0, 0))
    hbm = pl.BlockSpec(memory_space=pl.ANY)
    far = [((2, 2, 4, 2 * weight_in.shape[0], 3 * width), bf16), ((2, 2, 4, 2 * weight_in.shape[0], hidden), bf16),
           ((2, 2, 4, 2 * weight_out.shape[0], width), bf16), ((rows, 3 * width), bf16), ((rows, width), bf16), ((rows, width), bf16),
           ((rows, width), f32), ((rows, hidden), bf16), ((rows, hidden), bf16), ((rows, width), bf16), ((rows, width), f32), ((rows, width), bf16)]
    near = [((vectors.shape[0], width), f32), ((rows, 128), f32), ((8, width), f32)]
    v = lambda *shape: pltpu.VMEM(shape, bf16)
    vf = lambda *shape: pltpu.VMEM(shape, f32)
    dma = pltpu.SemaphoreType.DMA
    return pl.pallas_call(
        functools.partial(forward_kernel, plan, routes),
        grid=(heads // 2,),
        in_specs=[fixed(weight_in.shape), fixed(weight_out.shape), fixed(vectors.shape), fixed((1, rows)), pair, hbm, hbm],
        out_specs=[pair, pair] + [hbm] * len(far) + [fixed(s) for s, _ in near],
        out_shape=[jax.ShapeDtypeStruct(prev.shape, bf16)] * 2 + [jax.ShapeDtypeStruct(s, t) for s, t in far + near],
        scratch_shapes=[
            vf(2, 2, 4, 32, 128), vf(rows, rows), v(*weight_in.shape), v(*weight_out.shape), vf(16, 128), v(2, width, 768), v(hidden, width),
            v(rows, width), v(rows, width), v(rows, 3 * width), v(rows, width), v(rows, width), vf(rows, width), v(rows, hidden),
            v(2, rows, 768), vf(rows, width), vf(rows, width), v(rows, width), vf(rows, width), v(rows, width), dma((11, 10)),
            dma((11, 10)), dma((16,)), dma((13,)), dma((3, rows // 128))],
        compiler_params=pltpu.CompilerParams(collective_id=1, has_side_effects=True, vmem_limit_bytes=64 * 2**20 - 65536),
        name="forward",
    )(weight_in, weight_out, vectors, seg.reshape(1, rows), prev, tokens, grad_out)


class Scatter:
    def __init__(self, routes, full, got, send_sem, recv_sem):
        self.routes, self.full, self.got = routes, full, got
        self.send_sem, self.recv_sem = send_sem, recv_sem
        y, c, z, x = self.y, self.c, self.z, self.x = coords()
        first, second = (1 - y) * 2 + c, z * 2 + 1 - x
        self.core = dev(y, 1 - c, z, x)
        self.one = (jnp.where(c == 0, first, y * 2 + c), jnp.where(c == 0, z * 2 + x, second))
        self.two = (jnp.where(c == 0, y * 2 + c, first), jnp.where(c == 0, second, z * 2 + x))
        self.at_one = (jnp.where(c == 0, 1 - y, y), jnp.where(c == 0, x, 1 - x))
        self.at_two = (jnp.where(c == 0, y, 1 - y), jnp.where(c == 0, 1 - x, x))

    def copy(self, src, dst, k, slot, who):
        return pltpu.make_async_remote_copy(
            src_ref=src, dst_ref=dst, send_sem=self.send_sem.at[k, slot], recv_sem=self.recv_sem.at[k, slot],
            device_id=who, device_id_type=MESH)

    def to_core(self, k):
        return self.copy(self.full[k]().at[:, 1 - self.c], self.got[k][0], k, 0, self.core)

    def to_one(self, k):
        full = self.full[k]()
        return [self.copy(full.at[1 - self.y, self.c, :, 1 - self.x], self.got[k][1].at[0], k, 1, self.one),
                self.copy(full.at[self.at_one[0], self.c, :, self.at_one[1]], self.got[k][1].at[1], k, 2, self.one)]

    def to_two(self, k):
        return self.copy(self.full[k]().at[self.at_two[0], self.c, :, self.at_two[1]], self.got[k][2], k, 3, self.two)

    def along_z(self, k):
        full = self.full[k]()
        out = []
        for i in range(3):
            z = lax.rem(self.z + i + 1, 4)
            out.append(self.copy(full.at[self.y, self.c, z, self.x], self.got[k][3].at[i], k, 4 + i, dev(self.y, self.c, z, self.x)))
        return out

    def r1(self, k):
        self.to_core(k).start()

    def r2(self, k):
        full, got = self.full[k](), self.got[k][0]
        self.to_core(k).wait_recv()

        @pl.loop(0, 8)
        def _(i):
            for y in range(2):
                z, x = i // 2, lax.rem(i, 2)
                total = full[y, self.c, z, x].astype(jnp.float32) + got[y, z, x].astype(jnp.float32)
                full[y, self.c, z, x] = total.astype(full.dtype)
        for d in self.to_one(k):
            d.start()

    def early_z(self, k):
        full, (y, x) = self.full[k](), self.at_two
        out = []
        for i in range(3):
            z = lax.rem(self.z + i + 1, 4)
            who = dev(self.y, self.c, z, self.x)
            out.append(self.copy(full.at[self.y, self.c, z, self.x], self.got[k][2].at[i, 0], k, 3 + 2 * i, who))
            out.append(self.copy(full.at[y, self.c, z, x], self.got[k][2].at[i, 1], k, 4 + 2 * i, who))
        return out

    def last_two(self, k):
        y, x = self.at_two
        return self.copy(self.full[k]().at[y, self.c, self.z, x], self.got[k][3].at[0], k, 9, self.two)

    def add(self, full, spot, *terms):
        total = full[spot].astype(jnp.float32)
        for t in terms:
            total = total + t.astype(jnp.float32)
        full[spot] = total.astype(full.dtype)

    def r3(self, k):
        full, got = self.full[k](), self.got[k][1]
        for d in self.to_one(k):
            d.wait_recv()
        y, x = self.at_two
        straight = self.routes[k] == "z"

        @pl.loop(0, 4)
        def _(z):
            self.add(full, (y, self.c, z, x), got[0, z])
            if not straight:
                self.add(full, (self.y, self.c, z, self.x), got[1, z])
        for d in [self.to_two(k)] if straight else self.early_z(k):
            d.start()

    def r4(self, k):
        full, got = self.full[k](), self.got[k]
        mine = (self.y, self.c, self.z, self.x)
        if self.routes[k] == "n":
            for d in self.early_z(k):
                d.wait_recv()
            y, x = self.at_two
            self.add(full, (y, self.c, self.z, x), *[got[2][i, 1] for i in range(3)])
            self.last_two(k).start()
            self.add(full, mine, *[got[2][i, 0] for i in range(3)])
            return
        self.to_two(k).wait_recv()

        @pl.loop(0, 4)
        def _(z):
            self.add(full, (self.y, self.c, z, self.x), got[1][1, z], got[2][z])
        for d in self.along_z(k):
            d.start()

    def r5(self, k):
        last = [self.last_two(k)] if self.routes[k] == "n" else self.along_z(k)
        for d in last:
            d.wait_recv()
        total = self.full[k]()[self.y, self.c, self.z, self.x].astype(jnp.float32)
        for i in range(len(last)):
            total = total + self.got[k][3][i].astype(jnp.float32)
        return total

    def finish(self, k):
        rest = [*self.early_z(k), self.last_two(k)] if self.routes[k] == "n" else [self.to_two(k), *self.along_z(k)]
        for d in [self.to_core(k), *self.to_one(k), *rest]:
            d.wait_send()


def put_rows(ref, start, value):
    size, count = ref.shape[4], value.shape[0]
    for d in range(start // size, (start + count - 1) // size + 1):
        low, high = max(start, d * size), min(start + count, (d + 1) * size)
        ref[d // 16, d // 8 % 2, d // 2 % 4, d % 2, low - d * size:high - d * size] = value[low - start:high - start]


def own_columns(value, shards, columns):
    for d in range(shards):
        at, off = columns * d // 128, columns * d % 128
        if off + columns <= 128:
            tile = value[:, 128 * at:128 * (at + 1)]
            yield d, pltpu.roll(tile, 128 - off, 1) if off else tile
        else:
            yield d, pltpu.roll(value[:, 128 * at:128 * (at + 2)], 256 - off, 1)[:, :128]


def backward_kernel(heads, plan, routes, columns, *refs):
    (ddown_ref, hlow_ref, small_ref, two_ref, sone_ref, probs_ref, dl_ref,
     act_hbm, gp_hbm, go_hbm, gu_hbm, gq_hbm, dsec_hbm, none_hbm, mixed_hbm, x_hbm, qkv_hbm,
     dprev_ref, dx_ref, gin_ref, gout_ref, gvec_ref, norm_ref) = refs[:23]
    qkv_ref, do_ref, x_ref, mixed_ref, act_ref, gp_ref, dup_ref, w_ref, acc_ref, none_ref, part_ref, fvec_ref = refs[23:35]
    ups, outs = refs[35:37]
    got_flat = refs[37:93]
    nmine, ngot, send_sem, recv_sem, loc_sem, ns_sem, nr_sem = refs[93:]
    g = pl.program_id(0)
    rows, width = ddown_ref.shape
    hidden = act_hbm.shape[1]
    tile = 256
    U, O, Q, V = 0, 4, 7, 13
    got = [got_flat[4 * k:4 * k + 4] for k in range(14)]
    full = [lambda k=k: ups.at[k] for k in range(4)] + [lambda j=j: outs.at[j] for j in range(3)]
    full += [lambda p=p: ups.at[p // 2, :, :, :, :, :, :, pl.ds(384 * (p % 2), 384)] for p in range(6)] + [lambda: fvec_ref]
    sc = Scatter(routes, full, got, send_sem, recv_sem)
    y, c, z, x = coords()
    peers = peers_of(y, c, z, x)
    stages = {1: sc.r1, 2: sc.r2, 3: sc.r3, 4: sc.r4}

    def run(place):
        for stage, k in plan.get(place, ()):
            if stage == 5:
                finish(k)
            else:
                stages[stage](k)

    def finish(k):
        total = sc.r5(k)
        if k < O:
            gin_ref[:, :, 3 * width + 768 * k:3 * width + 768 * (k + 1)] = total
        elif k < Q:
            gout_ref[:, :, 256 * (k - O):256 * (k - O + 1)] = total
        elif k < V:
            for i in range(3):
                gin_ref[:, :, width * i + 128 * (k - Q):width * i + 128 * (k - Q + 1)] = total[:, :, 128 * i:128 * (i + 1)]
        else:
            lane = lax.broadcasted_iota(jnp.int32, total.shape, 1)
            gvec_ref[...] = jnp.where(lane < columns, total, 0.0)

    def load(src, dst, i):
        return pltpu.make_async_copy(src, dst, loc_sem.at[i])

    near = [dev(lax.rem(y + i // 4, 2), lax.rem(c + i // 2 % 2, 2), z, lax.rem(x + i % 2, 2)) for i in range(1, 8)]
    far = [dev(y, c, lax.rem(z + i, 4), x) for i in (1, 2, 3)]

    def share(i):
        return pltpu.make_async_remote_copy(
            src_ref=nmine.at[0 if i < 7 else 1], dst_ref=ngot.at[i], send_sem=ns_sem.at[i], recv_sem=nr_sem.at[i],
            device_id=(near + far)[i], device_id_type=MESH)

    def in_order(values, index):
        total = jnp.zeros_like(values[0])
        for at in range(len(values)):
            for i, v in enumerate(values):
                total = total + jnp.where(index(i) == at, v, 0.0)
        return total

    w_out, w_up, w_qkv = go_hbm.reshape(width + hidden, width), gu_hbm.reshape(width, hidden), gq_hbm.reshape(width, 3 * width)
    late = lambda: [load(dsec_hbm, acc_ref, 0), load(none_hbm, none_ref, 1), load(mixed_hbm, mixed_ref, 2), load(x_hbm, x_ref, 3),
                    load(qkv_hbm, qkv_ref, 4), load(act_hbm, act_ref, 8)]
    last_w = lambda: [load(w_qkv.at[:, pl.ds(768 * i, 768)], w_ref.at[i], 5 + i) for i in range(3)]

    @pl.when(g == 0)
    def _():
        barrier = pltpu.get_barrier_semaphore()
        met = far + near
        for p in met:
            pl.semaphore_signal(barrier, inc=1, device_id=p, device_id_type=MESH)

        def ahead(k):
            return [load(w_out.at[pl.ds(width + 768 * k, 768), :], w_ref.at[0], 5), load(gp_hbm.at[:, pl.ds(768 * k, 768)], gp_ref, 6)]

        def behind(k):
            return [load(w_up.at[:, pl.ds(768 * k, 768)], w_ref.at[1], 7)]
        for d in ahead(0) + behind(0) + late():
            d.start()
        part_ref[...] = jnp.zeros_like(part_ref)
        part_ref[1:2, :] = two_ref[0:1, :]
        part_ref[3:4, :] = two_ref[1:2, :]
        part_ref[7:8, :] = two_ref[2:3, :]
        pl.semaphore_wait(barrier, len(met))

        @pl.loop(0, 4)
        def _(k):
            for i in range(4):
                @pl.when(k == i)
                def _():
                    for d in ahead(i):
                        d.wait()
            low = (dotf(ddown_ref[...], w_ref[0], NT) * gp_ref[...].astype(jnp.float32)).astype(jnp.bfloat16)
            dup_ref[...] = low
            part_ref[pl.ds(8 + k, 1), :] = jnp.sum(low.astype(jnp.float32), axis=0, keepdims=True)
            ups[k] = dotf(hlow_ref[...], dup_ref[...], TN).reshape(ups.shape[1:]).astype(jnp.bfloat16)
            for i in range(4):
                @pl.when(k == i)
                def _():
                    sc.r1(U + i)
                    if i < 3:
                        for d in ahead(i + 1):
                            d.start()
                    run(("down", i))
                    if i == 0:
                        late()[0].wait()
                    for d in behind(i):
                        d.wait()
            acc_ref[...] += dotf(dup_ref[...], w_ref[1], NT)
            for i in range(4):
                @pl.when(k == i)
                def _():
                    if i < 3:
                        for d in behind(i + 1):
                            d.start()
                    run(("up", i))

        wo = load(w_out.at[pl.ds(0, width), :], w_ref.at[0], 5)
        wo.start()
        late()[1].wait()

        @pl.loop(0, rows // 128)
        def _(i):
            sl = pl.ds(pl.multiple_of(i * 128, 128), 128)
            one, normed = acc_ref[sl, :], none_ref[sl, :]
            part_ref[0:1, :] += jnp.sum(one * normed, axis=0, keepdims=True)
            part_ref[2:3, :] += jnp.sum(one, axis=0, keepdims=True)
            back = norm_back(one, normed, sone_ref[sl, 0:1], small_ref[0:1, :])
            low = back.astype(jnp.bfloat16)
            acc_ref[sl, :] = back
            dup_ref[sl, :] = low
            part_ref[6:7, :] += jnp.sum(low.astype(jnp.float32), axis=0, keepdims=True)
        run("norm")
        late()[2].wait()
        late()[5].wait()

        def put(start, value):
            for j in range(3):
                put_rows(outs.at[j], start, value[:, tile * j:tile * (j + 1)].reshape(96, 8, tile).astype(jnp.bfloat16))
        put(0, dotf(mixed_ref[...], dup_ref[...], TN))
        for k in range(4):
            put((width + 768 * k) // 8, dotf(act_ref[:, 768 * k:768 * (k + 1)], ddown_ref[...], TN))
        for j in range(3):
            sc.r1(O + j)
        run("out")
        wo.wait()
        do_ref[...] = dotf(dup_ref[...], w_ref[0], NT).astype(jnp.bfloat16)
        for d in late()[3:5]:
            d.wait()
        for d in last_w():
            d.start()

    for i in range(heads):
        if plan.get(("head", i)):
            @pl.when(g == i)
            def _():
                run(("head", i))

    pair, half = g // 2, lax.rem(g, 2)
    at = lambda off: pl.ds(pl.multiple_of(off * width + pair * 128, 128), 128)
    lane = lax.broadcasted_iota(jnp.int32, (rows, 128), 1)
    pick = lambda v: jnp.where(lane // 64 == half, v, jnp.zeros_like(v))
    q2, k2, v2, do2 = qkv_ref[:, at(0)], qkv_ref[:, at(1)], qkv_ref[:, at(2)], do_ref[:, at(0)]
    p = probs_ref[0].astype(jnp.float32)
    dp = dotf(pick(do2), v2, NT)
    ds = p * (dp - jnp.sum(p * dp, axis=1, keepdims=True))
    grad = (ds + dl_ref[0].astype(jnp.float32)).astype(jnp.bfloat16)
    dprev_ref[0] = grad
    dq = (dotf(grad, pick(k2), NN) * 0.125).astype(jnp.bfloat16)
    dk = (dotf(dprev_ref[0], pick(q2), TN) * 0.125).astype(jnp.bfloat16)
    dv = dotf(probs_ref[0], pick(do2), TN).astype(jnp.bfloat16)

    @pl.when(half == 0)
    def _():
        for i, v in enumerate((dq, dk, dv)):
            gp_ref[:, 128 * i:128 * (i + 1)] = v

    @pl.when(half == 1)
    def _():
        for i, v in enumerate((dq, dk, dv)):
            v = gp_ref[:, 128 * i:128 * (i + 1)] + v
            gp_ref[:, 128 * i:128 * (i + 1)] = v
            qkv_ref[:, at(i)] = v
            if i != 1:
                part_ref[4 + i // 2:5 + i // 2, at(0)] = jnp.sum(v.astype(jnp.float32), axis=0, keepdims=True)
        for p in range(0, heads // 2, 2):
            @pl.when(pair == p)
            def _():
                sc.finish(U + p // 2)
        to = pl.ds(pl.multiple_of(384 * lax.rem(pair, 2), 384), 384)
        ups[pair // 2, :, :, :, :, :, :, to] = dotf(x_ref[...], gp_ref[:, 0:384], TN).reshape(ups.shape[1:7] + (384,)).astype(jnp.bfloat16)
        for p in range(heads // 2):
            @pl.when(pair == p)
            def _():
                sc.r1(Q + p)

    @pl.when(g == heads - 1)
    def _():
        for d, tile_of in own_columns(part_ref[...], 32, columns):
            fvec_ref[d // 16, d // 8 % 2, d // 2 % 4, d % 2] = tile_of
        sc.r1(V)
        run("end")
        for d in last_w():
            d.wait()

        @pl.loop(0, 3)
        def _(i):
            acc_ref[...] += dotf(qkv_ref[:, pl.ds(pl.multiple_of(768 * i, 768), 768)], w_ref[i], NT)
            for j in range(3):
                @pl.when(i == j)
                def _():
                    run(("dx", j))
        dx_ref[...] = acc_ref[...].astype(jnp.bfloat16)
        run("last")
        squares = gvec_ref[0:8, :] * gvec_ref[0:8, :] + gvec_ref[8:16, :] * gvec_ref[8:16, :]
        for ref in (gin_ref, gout_ref):
            v = ref[...]
            v = jnp.sum(v * v, axis=0)
            for j in range(v.shape[1] // 128):
                squares = squares + v[:, 128 * j:128 * (j + 1)]
        nmine[0] = jnp.sum(squares, keepdims=True) + jnp.zeros((8, 128), jnp.float32)
        for i in range(7):
            share(i).start()
        for k in range(14):
            if k not in (0, 1, 2):
                sc.finish(k)
        for i in range(7):
            share(i).wait_recv()
        me = y * 4 + c * 2 + x

        def from_near(i):
            return me if i == 0 else lax.rem(y + i // 4, 2) * 4 + lax.rem(c + i // 2 % 2, 2) * 2 + lax.rem(x + i % 2, 2)
        plane = in_order([nmine[0]] + [ngot[i] for i in range(7)], from_near)
        nmine[1] = plane
        for i in range(7, 10):
            share(i).start()
        for i in range(7, 10):
            share(i).wait_recv()
        total = in_order([plane] + [ngot[i] for i in range(7, 10)], lambda i: lax.rem(z - i + 4, 4))
        norm_ref[...] = jnp.sqrt(total)
        for i in range(10):
            share(i).wait_send()


def backward_all(plan, routes, columns, grad_down, hidden_low, small, two_sums, scale_one, probs, grad_logits,
                 activated, slope, full_out, full_up, full_qkv, grad_second, normed_one, mixed, tokens, qkv):
    rows, width = tokens.shape
    heads = probs.shape[0]
    hidden = activated.shape[1]
    f32, bf16 = jnp.float32, jnp.bfloat16
    fixed = lambda shape: pl.BlockSpec(shape, lambda g: (0,) * len(shape), pipeline_mode=pl.Buffered(1))
    head = pl.BlockSpec((1, rows, rows), lambda g: (g, 0, 0))
    hbm = pl.BlockSpec(memory_space=pl.ANY)
    r_in, r_out = full_qkv.shape[3] // 2, full_out.shape[3] // 2
    landing = []
    kinds = [((r_in // 8, 8, 768), bf16)] * 4 + [((r_out // 8, 8, 256), bf16)] * 3 + [((r_in // 8, 8, 384), bf16)] * 6 + [((16, 128), f32)]
    for (shape, kind), route in zip(kinds, routes):
        rest = [(4,), (3,)] if route == "z" else [(3, 2), (1,)]
        landing += [pltpu.VMEM(first + shape, kind) for first in [(2, 4, 2), (2, 4)] + rest]
    lead = (2, 2, 4, 2)
    v = lambda *shape: pltpu.VMEM(shape, bf16)
    vf = lambda *shape: pltpu.VMEM(shape, f32)
    shapes = [((r_in // 8, 8, 3 * width + hidden), f32), ((r_out // 8, 8, width), f32), ((16, 128), f32), ((8, 128), f32)]
    dma = pltpu.SemaphoreType.DMA
    return pl.pallas_call(
        functools.partial(backward_kernel, heads, plan, routes, columns),
        grid=(heads,),
        in_specs=[fixed((rows, width)), fixed((rows, width)), fixed(small.shape), fixed(two_sums.shape),
                  fixed(scale_one.shape), head, head] + [hbm] * 10,
        out_specs=[head, fixed((rows, width))] + [fixed(s) for s, _ in shapes],
        out_shape=[jax.ShapeDtypeStruct(probs.shape, bf16), jax.ShapeDtypeStruct((rows, width), bf16)]
        + [jax.ShapeDtypeStruct(s, t) for s, t in shapes],
        scratch_shapes=[v(rows, 3 * width), v(rows, width), v(rows, width), v(rows, width), v(rows, hidden),
                        v(rows, 768), v(rows, 768), v(3, 768, width), vf(rows, width), vf(rows, width),
                        vf(16, width), vf(*lead, 16, 128)]
        + [v(4, *lead, r_in // 8, 8, 768), v(3, *lead, r_out // 8, 8, 256)] + landing
        + [vf(2, 8, 128), vf(10, 8, 128), dma((14, 10)), dma((14, 10)), dma((10,)), dma((10,)), dma((10,))],
        compiler_params=pltpu.CompilerParams(collective_id=2, has_side_effects=True, vmem_limit_bytes=64 * 2**20 - 65536),
        name="backward",
    )(grad_down, hidden_low, small, two_sums, scale_one, probs, grad_logits,
      activated, slope, full_out, full_up, full_qkv, grad_second, normed_one, mixed, tokens, qkv)


def update_kernel(norm_ref, step_ref, *refs):
    through, refs = refs[:4], refs[4:]
    trios, refs = [refs[4 * i:4 * i + 4] for i in range(3)], refs[12:]
    through_out, refs = refs[:4], refs[4:]
    outs, gn_ref = [refs[5 * i:5 * i + 5] for i in range(3)], refs[15]
    for a, b in zip(through, through_out):
        b[...] = a[...]
    norm = norm_ref[0:1, 0:1]
    gn_ref[...] = norm
    factor = jnp.minimum(1.0, clip_scale * math.sqrt(PARAMS) / (norm + 1e-06))
    step = jnp.full((1, 1), step_ref[0], jnp.int32).astype(jnp.float32)
    one = 1.0 - jnp.exp(step * math.log(beta_one))
    two = 1.0 - jnp.exp(step * math.log(beta_two))
    for i, ((g_ref, w_ref, m_ref, v_ref), out) in enumerate(zip(trios, outs)):
        rate, decay = (rate_vector, 0.0) if i == 2 else (rate_matrix, decay_matrix)
        grad = g_ref[...].reshape(w_ref.shape) if i < 2 else g_ref[0:w_ref.shape[0], 0:w_ref.shape[1]]
        clipped = grad * factor
        moment = beta_one * m_ref[...] + (1.0 - beta_one) * clipped
        square = beta_two * v_ref[...] + (1.0 - beta_two) * clipped * clipped
        weight = w_ref[...] - rate * ((moment / one) / (jnp.sqrt(square / two) + adam_eps) + decay * w_ref[...])
        for ref, val in zip(out, (clipped, moment, square, weight, weight.astype(jnp.bfloat16))):
            ref[...] = val


def update_all(norm, step_count, through, trios):
    steps = 2
    f32 = jnp.float32

    def spec(a):
        if a.shape[-1] < 128 * steps:
            return pl.BlockSpec(a.shape, lambda g: (0,) * a.ndim)
        return pl.BlockSpec(a.shape[:-1] + (a.shape[-1] // steps,), lambda g: (0,) * (a.ndim - 1) + (g,))
    slabs = [pl.BlockSpec((a.shape[0] // steps,) + a.shape[1:], lambda g: (g, 0, 0)) if a.ndim == 3 else spec(a) for a in through]
    shapes = []
    for g, w, m, v in trios:
        shapes += [jax.ShapeDtypeStruct(w.shape, t) for t in (f32, f32, f32, f32, jnp.bfloat16)]
    flat = [a for trio in trios for a in trio]
    return pl.pallas_call(
        update_kernel,
        grid=(steps,),
        in_specs=[pl.BlockSpec((8, 128), lambda g: (0, 0)), pl.BlockSpec(memory_space=pltpu.SMEM)] + slabs + [spec(a) for a in flat],
        out_specs=slabs + [spec(s) for s in shapes] + [pl.BlockSpec((1, 1), lambda g: (0, 0))],
        out_shape=[jax.ShapeDtypeStruct(a.shape, a.dtype) for a in through] + shapes + [jax.ShapeDtypeStruct((1, 1), f32)],
        compiler_params=pltpu.CompilerParams(vmem_limit_bytes=64 * 2**20 - 65536),
        name="update",
    )(norm, step_count, *through, *flat)


def adam_update(master, moment, square, gradient, factor, step_value, step_rate, decay_rate):
    clipped = gradient * factor
    new_moment = beta_one * moment + (1.0 - beta_one) * clipped
    new_square = beta_two * square + (1.0 - beta_two) * clipped * clipped
    fixed_moment = new_moment / (1.0 - jnp.power(beta_one, step_value))
    fixed_square = new_square / (1.0 - jnp.power(beta_two, step_value))
    updated = master - step_rate * (
        fixed_moment / (jnp.sqrt(fixed_square) + adam_eps) + decay_rate * master
    )
    return (clipped, new_moment, new_square, updated)


def rounded(v):
    return lax.reduce_precision(v, 8, 7)


def gather_all(weight_in, weight_out, vectors, width):
    whole = lambda v: lax.all_gather(v, AXES, axis=0, tiled=True)
    low_in = weight_in.astype(jnp.bfloat16)
    small = lax.all_gather(rounded(vectors), AXES, axis=1, tiled=True)
    return whole(low_in[:, : 3 * width]), whole(low_in[:, 3 * width :]), whole(weight_out.astype(jnp.bfloat16)), small


def forward_plain(tokens, grad_out, full_qkv, full_up, full_out, small, prev, segments):
    width = tokens.shape[1]
    dot = lambda a, b: jnp.dot(a, b, preferred_element_type=jnp.float32)
    sums = lambda v: jnp.sum(v, axis=0, dtype=jnp.float32)
    offsets = jnp.concatenate([small[4], jnp.zeros_like(small[4]), small[5]])
    qkv = (dot(tokens, full_qkv) + offsets).astype(jnp.bfloat16)
    logits, mixed, log_sums = attn_fwd(qkv, prev, segments, 640)
    first = tokens.astype(jnp.float32) + (dot(mixed, full_out[:width]) + small[6])
    hidden_one, normed_one, scale_one = norm_rows(first, small[0], small[2])
    hidden_low = hidden_one.astype(jnp.bfloat16)
    upward = dot(hidden_low, full_up) + small[8:].reshape(-1)
    activated, gelu_pull = jax.vjp(gelu_exact, upward)
    activated, slope = activated.astype(jnp.bfloat16), gelu_pull(jnp.ones_like(upward))[0]
    second = hidden_one + (dot(activated, full_out[width:]) + small[7])
    output, normed_two, scale_two = norm_rows(second, small[1], small[3])
    grad_output = grad_out.astype(jnp.float32)
    grad_second = norm_back(grad_output, normed_two, scale_two, small[1])
    grad_down = grad_second.astype(jnp.bfloat16)
    two_sums = jnp.stack([sums(grad_output * normed_two), sums(grad_output), sums(grad_down)])
    return (logits, qkv, mixed, log_sums, hidden_low, normed_one, scale_one, activated, slope, output.astype(jnp.bfloat16),
            grad_second, grad_down, two_sums)


def reduce_all(grad_qkv, grad_up, grad_out, small, shards):
    part = lambda v: lax.psum_scatter(v, AXES, scatter_dimension=0, tiled=True).astype(jnp.float32)
    owned_in = jnp.concatenate([part(grad_qkv), part(grad_up)], axis=1)
    owned_out = part(grad_out)
    owned_small = lax.psum_scatter(small, AXES, scatter_dimension=1, tiled=True)
    total = lax.psum(jnp.sum(owned_in**2) + jnp.sum(owned_out**2) + jnp.sum(owned_small**2), AXES)
    return owned_in, owned_out, owned_small, jnp.sqrt(total)


def body(remote, hidden_in, prev_logits, segment_ids, d_hidden, d_logits, weight_in, weight_out, vectors,
         moment_in, moment_out, moment_vectors, square_in, square_out, square_vectors, step_count):
    width = weight_out.shape[1]
    shards = lax.axis_size("dp") * lax.axis_size("fsdp")
    dot = lambda spec, a, b: jnp.einsum(spec, a, b, preferred_element_type=jnp.float32)
    sums = lambda v: jnp.sum(v, axis=0, dtype=jnp.float32)
    segments = segment_ids[0]
    if remote:
        (logits, probs, full_qkv, full_up, full_out, qkv, mixed, hidden_low, normed_one, activated, slope, output, grad_second, grad_down,
         small, scale_one, two_sums) = forward_all(
             FORWARD_PLAN, ROUTES, hidden_in, d_hidden, weight_in, weight_out, vectors, prev_logits[0], segments)
        grad_prev, grad_tokens, grad_in, grad_out, grad_vec, norm = backward_all(
            BACKWARD_PLAN, BACKWARD_ROUTES, vectors.shape[1], grad_down, hidden_low, small, two_sums, scale_one, probs, d_logits[0],
            activated, slope, full_out, full_up, full_qkv, grad_second, normed_one, mixed, hidden_in, qkv)
        (logits, grad_prev, output, grad_tokens, *states, grad_norm) = update_all(
            norm, step_count, [logits, grad_prev, output, grad_tokens],
            [(grad_in, weight_in, moment_in, square_in), (grad_out, weight_out, moment_out, square_out),
             (grad_vec, vectors, moment_vectors, square_vectors)])
        clipped, moments, squares, updated, copies = [states[i::5] for i in range(5)]
        return (output, logits[None], grad_tokens, grad_prev[None], *clipped, *moments, *squares, *updated, *copies, grad_norm[0, 0])
    (full_qkv, full_up, full_out, small) = gather_all(weight_in, weight_out, vectors, width)
    (logits, qkv, mixed, log_sums, hidden_low, normed_one, scale_one, activated, slope, output,
     grad_second, grad_down, two_sums) = forward_plain(hidden_in, d_hidden, full_qkv, full_up, full_out, small, prev_logits[0], segments)
    w_attn, w_down = full_out[:width], full_out[width:]
    down_grad = dot("tf,td->fd", activated, grad_down).astype(jnp.bfloat16)
    grad_up = (dot("td,fd->tf", grad_down, w_down) * slope).astype(jnp.bfloat16)
    up_grad = dot("td,tf->df", hidden_low, grad_up).astype(jnp.bfloat16)
    grad_one = grad_second + dot("tf,df->td", grad_up, full_up)
    grad_first = norm_back(grad_one, normed_one, scale_one, small[0])
    grad_attn = grad_first.astype(jnp.bfloat16)
    attn_grad = dot("tc,td->cd", mixed, grad_attn).astype(jnp.bfloat16)
    grad_mixed = dot("td,cd->tc", grad_attn, w_attn).astype(jnp.bfloat16)
    grad_prev, grad_q, grad_k, grad_v = attn_bwd(qkv, grad_mixed, prev_logits[0], d_logits[0], log_sums, segments, 640)
    grad_qkv = jnp.concatenate([grad_q, grad_k, grad_v], axis=1)
    qkv_grad = dot("td,tc->dc", hidden_in, grad_qkv).astype(jnp.bfloat16)
    grad_tokens = (grad_first + dot("tc,dc->td", grad_qkv, full_qkv)).astype(jnp.bfloat16)
    small_grad = jnp.concatenate([
        jnp.stack([sums(grad_one * normed_one), two_sums[0], sums(grad_one), two_sums[1],
                   sums(grad_q), sums(grad_v), sums(grad_attn), two_sums[2]]),
        sums(grad_up).reshape(-1, width)], axis=0)

    owned_in, owned_out, owned_small, grad_norm = reduce_all(
        qkv_grad, up_grad, jnp.concatenate([attn_grad, down_grad], axis=0), small_grad, shards)
    factor = jnp.minimum(1.0, clip_scale * math.sqrt(PARAMS) / (grad_norm + 1e-06))
    step_value = step_count[0].astype(jnp.float32)
    new = [
        adam_update(weight_in, moment_in, square_in, owned_in, factor, step_value, rate_matrix, decay_matrix),
        adam_update(weight_out, moment_out, square_out, owned_out, factor, step_value, rate_matrix, decay_matrix),
        adam_update(vectors, moment_vectors, square_vectors, owned_small, factor, step_value, rate_vector, 0.0),
    ]
    clipped, moments, squares, updated = zip(*new)
    return (output.astype(jnp.bfloat16), logits[None], grad_tokens, grad_prev[None],
            *clipped, *moments, *squares, *updated, *[u.astype(jnp.bfloat16) for u in updated], grad_norm)


def solution(mesh):
    remote = (mesh.shape["dp"], mesh.shape["fsdp"]) == (4, 8)
    rows = P(AXES, None)
    heads = P(AXES, None, None, None)
    cols = P(None, AXES)
    trio = (rows, rows, cols)
    return jax.shard_map(
        functools.partial(body, remote),
        mesh=mesh,
        in_specs=(rows, heads, rows, rows, heads, *trio, *trio, *trio, P()),
        out_specs=(rows, heads, rows, heads, *trio, *trio, *trio, *trio, *trio, P()),
        check_vma=False,
    )
```

```python
import functools
import math

import jax
import jax.numpy as jnp
from jax import lax
from jax.experimental import pallas as pl
from jax.experimental.pallas import tpu as pltpu
from jax.sharding import PartitionSpec as P

PARAMS = 7087104


norm_eps = 1e-12
clip_scale = 1.0
beta_one = 0.9
beta_two = 0.999
adam_eps = 1e-08
rate_matrix = 0.06
rate_vector = 0.25
decay_matrix = 0.01
NEG = -1e30
NT = (((1,), (1,)), ((), ()))
NN = (((1,), (0,)), ((), ()))
TN = (((0,), (0,)), ((), ()))
AXES = ("dp", "fsdp")


def gelu_exact(upward):
    return jax.nn.gelu(upward, approximate=False)


def norm_rows(residual, gain_row, shift_row):
    centered = residual - jnp.mean(residual, axis=1, keepdims=True)
    scaling = lax.rsqrt(jnp.mean(centered * centered, axis=1, keepdims=True) + norm_eps)
    normed = centered * scaling
    return (normed * gain_row + shift_row, normed, scaling)


def norm_back(grad_after, normed, scaling, gain_row):
    scaled_grad = grad_after * gain_row
    return scaling * (
        scaled_grad
        - jnp.mean(scaled_grad, axis=1, keepdims=True)
        - normed * jnp.mean(scaled_grad * normed, axis=1, keepdims=True)
    )


def dotf(a, b, dims):
    return lax.dot_general(a, b, dims, preferred_element_type=jnp.float32)

def half_masks(rows):
    lane = lax.broadcasted_iota(jnp.int32, (rows, 128), 1)
    return lane < 64

def attn_fwd_kernel(BR, q_ref, k_ref, v_ref, prev_ref, srow_ref, scol_ref, logits_ref, mixed_ref, lse_ref, mask_ref):
    g = pl.program_id(0)
    rows = q_ref.shape[0]
    @pl.when(g == 0)
    def _():
        mask_ref[...] = jnp.where(scol_ref[...] == srow_ref[...], 0.0, NEG)
        lse_ref[...] = jnp.zeros_like(lse_ref)
    k2 = k_ref[...]
    v2 = v_ref[...]
    left = half_masks(rows)
    zero = jnp.zeros_like(v2)
    va = jnp.where(left, v2, zero)
    vb = jnp.where(left, zero, v2)
    for rb in range(rows // BR):
        sl = pl.ds(rb * BR, BR)
        q2 = q_ref[sl, :] * jnp.bfloat16(0.125)
        lb = half_masks(BR)
        outs = []
        lses = []
        for h in range(2):
            qh = jnp.where(lb if h == 0 else ~lb, q2, jnp.zeros_like(q2))
            raw = dotf(qh, k2, NT) + prev_ref[h, sl, :].astype(jnp.float32)
            logits_ref[h, sl, :] = raw.astype(jnp.bfloat16)
            s = raw + mask_ref[sl, :]
            m = jnp.max(s, axis=1, keepdims=True)
            e = jnp.exp(s - m)
            tot = jnp.sum(e, axis=1, keepdims=True)
            o = dotf(e.astype(jnp.bfloat16), va if h == 0 else vb, NN)
            outs.append(o / tot)
            lses.append(m + jnp.log(tot))
        mixed_ref[sl, :] = (outs[0] + outs[1]).astype(jnp.bfloat16)
        lane = lax.broadcasted_iota(jnp.int32, (BR, 128), 1)
        cur = lse_ref[sl, :]
        cur = jnp.where(lane == 2 * g, lses[0], cur)
        cur = jnp.where(lane == 2 * g + 1, lses[1], cur)
        lse_ref[sl, :] = cur

def attn_fwd(qkv, prev, seg, BR=128):
    rows = qkv.shape[0]
    heads = prev.shape[0]
    G = heads // 2
    srow = seg.reshape(1, rows); scol = seg.reshape(rows, 1)
    return pl.pallas_call(
        functools.partial(attn_fwd_kernel, BR),
        grid=(G,),
        in_specs=[
            pl.BlockSpec((rows, 128), lambda g: (0, g)),
            pl.BlockSpec((rows, 128), lambda g: (0, G + g)),
            pl.BlockSpec((rows, 128), lambda g: (0, 2 * G + g)),
            pl.BlockSpec((2, rows, rows), lambda g: (g, 0, 0)),
            pl.BlockSpec((1, rows), lambda g: (0, 0)),
            pl.BlockSpec((rows, 1), lambda g: (0, 0)),
        ],
        out_specs=[
            pl.BlockSpec((2, rows, rows), lambda g: (g, 0, 0)),
            pl.BlockSpec((rows, 128), lambda g: (0, g)),
            pl.BlockSpec((rows, 128), lambda g: (0, 0)),
        ],
        out_shape=[
            jax.ShapeDtypeStruct((heads, rows, rows), jnp.bfloat16),
            jax.ShapeDtypeStruct((rows, heads * 64), jnp.bfloat16),
            jax.ShapeDtypeStruct((rows, 128), jnp.float32),
        ],
        scratch_shapes=[pltpu.VMEM((rows, rows), jnp.float32)],
        compiler_params=pltpu.CompilerParams(vmem_limit_bytes=60 * 2**20),
        name="attn_fwd",
    )(qkv, qkv, qkv, prev, srow, scol)

def attn_bwd_kernel(BR, q_ref, k_ref, v_ref, do_ref, prev_ref, dl_ref, lse_ref, srow_ref, scol_ref,
                    dprev_ref, dq_ref, dk_ref, dv_ref, mask_ref, p_ref, g_ref):
    g = pl.program_id(0)
    rows = q_ref.shape[0]
    @pl.when(g == 0)
    def _():
        mask_ref[...] = jnp.where(scol_ref[...] == srow_ref[...], 0.0, NEG)
    k2 = k_ref[...]
    v2 = v_ref[...]
    left = half_masks(rows)
    zero = jnp.zeros_like(v2)
    for h in range(2):
        lm = left if h == 0 else ~left
        kh = jnp.where(lm, k2, zero)
        for rb in range(rows // BR):
            sl = pl.ds(rb * BR, BR)
            lb = half_masks(BR)
            lb = lb if h == 0 else ~lb
            q2 = q_ref[sl, :] * jnp.bfloat16(0.125)
            qh = jnp.where(lb, q2, jnp.zeros_like(q2))
            doh = jnp.where(lb, do_ref[sl, :], jnp.zeros_like(q2))
            lane = lax.broadcasted_iota(jnp.int32, (BR, 128), 1)
            lse = jnp.sum(jnp.where(lane == 2 * g + h, lse_ref[sl, :], 0.0), axis=1, keepdims=True)
            s = dotf(qh, k2, NT) + prev_ref[h, sl, :].astype(jnp.float32) + mask_ref[sl, :]
            p = jnp.exp(s - lse)
            dp = dotf(doh, v2, NT)
            delta = jnp.sum(p * dp, axis=1, keepdims=True)
            ds = p * (dp - delta)
            gt = (ds + dl_ref[h, sl, :].astype(jnp.float32)).astype(jnp.bfloat16)
            dprev_ref[h, sl, :] = gt
            p_ref[sl, :] = p.astype(jnp.bfloat16)
            dq = dotf(gt, kh, NN) * 0.125
            if h == 0:
                dq_ref[sl, :] = dq.astype(jnp.bfloat16)
            else:
                dq_ref[sl, :] = dq_ref[sl, :] + dq.astype(jnp.bfloat16)
        qh = jnp.where(lm, q_ref[...], zero)
        doh = jnp.where(lm, do_ref[...], zero)
        dk = (dotf(dprev_ref[h], qh, TN) * 0.125).astype(jnp.bfloat16)
        dv = dotf(p_ref[...], doh, TN).astype(jnp.bfloat16)
        if h == 0:
            dk_ref[...] = dk
            dv_ref[...] = dv
        else:
            dk_ref[...] = dk_ref[...] + dk
            dv_ref[...] = dv_ref[...] + dv

def attn_bwd(qkv, do, prev, dl, lse, seg, BR=128):
    rows = qkv.shape[0]
    heads = prev.shape[0]
    G = heads // 2
    srow = seg.reshape(1, rows); scol = seg.reshape(rows, 1)
    col = lambda off: pl.BlockSpec((rows, 128), lambda g: (0, off + g))
    return pl.pallas_call(
        functools.partial(attn_bwd_kernel, BR),
        grid=(G,),
        in_specs=[
            col(0), col(G), col(2 * G), col(0),
            pl.BlockSpec((2, rows, rows), lambda g: (g, 0, 0)),
            pl.BlockSpec((2, rows, rows), lambda g: (g, 0, 0)),
            pl.BlockSpec((rows, 128), lambda g: (0, 0)),
            pl.BlockSpec((1, rows), lambda g: (0, 0)),
            pl.BlockSpec((rows, 1), lambda g: (0, 0)),
        ],
        out_specs=[
            pl.BlockSpec((2, rows, rows), lambda g: (g, 0, 0)),
            col(0), col(0), col(0),
        ],
        out_shape=[
            jax.ShapeDtypeStruct((heads, rows, rows), jnp.bfloat16),
        ] + [jax.ShapeDtypeStruct((rows, heads * 64), jnp.bfloat16)] * 3,
        scratch_shapes=[pltpu.VMEM((rows, rows), jnp.float32), pltpu.VMEM((rows, rows), jnp.bfloat16), pltpu.VMEM((8, 128), jnp.float32)],
        compiler_params=pltpu.CompilerParams(vmem_limit_bytes=60 * 2**20),
        name="attn_bwd",
    )(qkv, qkv, qkv, do, prev, dl, lse, srow, scol)


MESH = pl.DeviceIdType.MESH


def coords():
    dp = lax.axis_index("dp"); fs = lax.axis_index("fsdp")
    y = dp // 2; c = lax.rem(dp, 2)
    z = fs // 2; x = lax.rem(fs, 2)
    return y, c, z, x

def dev(y, c, z, x):
    return (y * 2 + c, z * 2 + x)


ROUTES = "zzzzzzznnnn"
BACKWARD_ROUTES = "nzzznzzzzznzzz"
FORWARD_PLAN = {
    "start": [(1, 0), (1, 1), (2, 0), (1, 7), (1, 8), (1, 9), (1, 10), (1, 2), (2, 1), (3, 0)],
    ("q", 0): [(1, 3), (2, 2), (3, 1)],
    ("q", 1): [(2, 3), (1, 4), (3, 2)],
    ("q", 2): [(3, 3), (1, 5)],
    ("pair", 0): [(2, 4), (1, 6)],
    ("pair", 2): [(2, 5)],
    ("pair", 3): [(3, 4)],
    ("pair", 5): [(2, 6)],
    "out": [(3, 5), (2, 7), (3, 6), (2, 8)],
    "norm": [(3, 7), (2, 9)],
    ("up", 0): [(3, 8), (2, 10)],
    ("up", 1): [(3, 9)],
    ("up", 2): [(3, 10)],
}
BACKWARD_PLAN = {
    ("down", 1): [(2, 0)],
    ("down", 2): [(2, 1)],
    ("down", 3): [(3, 0), (2, 2)],
    ("up", 3): [(3, 1)],
    "norm": [(2, 3)],
    "out": [(4, 0), (4, 1), (3, 2), (3, 3)],
    ("head", 1): [(5, 0), (2, 4), (4, 2)],
    ("head", 2): [(4, 3), (5, 1), (2, 5)],
    ("head", 4): [(3, 4), (2, 6), (5, 2)],
    ("head", 5): [(5, 3)],
    ("head", 6): [(3, 5)],
    ("head", 8): [(3, 6)],
    ("head", 9): [(4, 5), (2, 7), (2, 8)],
    ("head", 10): [(4, 4), (4, 6), (2, 9), (3, 7)],
    ("head", 11): [(3, 8), (2, 10), (5, 4), (2, 11)],
    "end": [(4, 7), (4, 8), (3, 9), (5, 5), (3, 10)],
    ("dx", 0): [(2, 12), (3, 11)],
    ("dx", 1): [(4, 9), (2, 13), (5, 6)],
    "last": [(5, 7), (3, 12), (5, 8), (4, 11), (3, 13), (4, 12), (4, 10), (4, 13), (5, 9), (5, 10), (5, 11), (5, 12), (5, 13)],
}


class Gather:
    def __init__(self, chunks, routes, sources, wholes, send_sem, recv_sem):
        self.chunks, self.routes, self.sources, self.wholes = chunks, routes, sources, wholes
        self.send_sem, self.recv_sem = send_sem, recv_sem
        self.y, self.c, self.z, self.x = coords()

    def part(self, k):
        array, start, size, origin = self.chunks[k]
        return self.wholes[array], pl.ds(start, size), self.sources[array].at[:, pl.ds(origin, size)]

    def rows_of(self, k, x):
        size = self.sources[self.chunks[k][0]].shape[0]
        return pl.ds(pl.multiple_of(size * x, 8), size)

    def copy(self, src, dst, k, slot, who):
        return pltpu.make_async_remote_copy(
            src_ref=src, dst_ref=dst, send_sem=self.send_sem.at[k, slot], recv_sem=self.recv_sem.at[k, slot],
            device_id=who, device_id_type=MESH)

    def along_z(self, k):
        whole, cols, mine = self.part(k)
        spot = whole.at[self.y, self.c, self.z, self.rows_of(k, self.x), cols]
        return [self.copy(mine, spot, k, d, dev(self.y, self.c, lax.rem(self.z + d + 1, 4), self.x)) for d in range(3)]

    def across(self):
        return jnp.where(self.c == 0, self.y, 1 - self.y), jnp.where(self.c == 0, 1 - self.x, self.x)

    def other(self):
        return (jnp.where(self.c == 0, 1 - self.y, self.y) * 2 + self.c, self.z * 2 + jnp.where(self.c == 0, self.x, 1 - self.x))

    def block(self, k, y, x):
        whole, cols, _ = self.part(k)
        return whole.at[y, self.c, :, self.rows_of(k, x), cols]

    def to_neighbours(self, k):
        block = self.block(k, self.y, self.x)
        return [self.copy(block, block, k, 3, dev(self.y, self.c, self.z, 1 - self.x)),
                self.copy(block, block, k, 4, dev(1 - self.y, self.c, self.z, self.x))]

    def handed_on(self, k):
        block = self.block(k, *self.across())
        return self.copy(block, block, k, 3 + self.c, self.other()), self.copy(block, block, k, 5, self.other()), self.copy(block, block, k, 4 - self.c, self.other())

    def early(self, k):
        whole, cols, mine = self.part(k)
        y, x = self.across()
        return self.copy(mine, whole.at[self.y, self.c, self.z, self.rows_of(k, self.x), cols], k, 3, dev(y, self.c, self.z, x))

    def relayed(self, k):
        whole, cols, _ = self.part(k)
        y, x = self.across()
        spot = whole.at[y, self.c, self.z, self.rows_of(k, x), cols]
        return [self.copy(spot, spot, k, 4 + d, dev(self.y, self.c, lax.rem(self.z + d + 1, 4), self.x)) for d in range(3)]

    def halves(self, k):
        own, far = self.block(k, self.y, self.x), self.block(k, *self.across())
        return [self.copy(own, own, k, 7, self.other()), self.copy(far, far, k, 8, self.other())]

    def to_core(self, k):
        whole, cols, _ = self.part(k)
        plane = whole.at[:, self.c, :, :, cols]
        return self.copy(plane, plane, k, 9, dev(self.y, 1 - self.c, self.z, self.x))

    def start(self, k):
        if self.routes[k] == "n":
            self.early(k).start()
        for d in self.along_z(k):
            d.start()

    def s1(self, k):
        if self.routes[k] == "n":
            self.early(k).wait_recv()
            for d in self.relayed(k):
                d.start()
            return
        for d in self.along_z(k):
            d.wait_recv()
        for d in self.to_neighbours(k):
            d.start()

    def s2(self, k):
        if self.routes[k] == "n":
            for d in self.along_z(k) + self.relayed(k):
                d.wait_recv()
            for d in self.halves(k):
                d.start()
            return
        got, on, _ = self.handed_on(k)
        got.wait_recv()
        on.start()

    def s3(self, k):
        if self.routes[k] == "n":
            for d in self.halves(k):
                d.wait_recv()
        else:
            _, on, other = self.handed_on(k)
            other.wait_recv()
            on.wait_recv()
        self.to_core(k).start()

    def s4(self, k):
        self.to_core(k).wait_recv()

    def finish(self, k):
        if self.routes[k] == "n":
            sent = [self.early(k), *self.relayed(k), *self.halves(k)]
        else:
            sent = self.to_neighbours(k) + [self.handed_on(k)[1]]
        for d in self.along_z(k) + sent + [self.to_core(k)]:
            d.wait_send()


def peers_of(y, c, z, x):
    return [dev(y, c, lax.rem(z + d, 4), x) for d in (1, 2, 3)] + [dev(y, c, z, 1 - x), dev(1 - y, c, z, x), dev(y, 1 - c, z, x)]


def normalise(v):
    centered = v - jnp.mean(v, axis=1, keepdims=True)
    scaling = lax.rsqrt(jnp.mean(centered * centered, axis=1, keepdims=True) + norm_eps)
    return centered * scaling, scaling


def spread_columns(ref, shards, columns, rows, width):
    lane = lax.broadcasted_iota(jnp.int32, (rows, 128), 1)
    blocks = [jnp.zeros((rows, 128), jnp.float32) for _ in range(width // 128)]
    for d in range(shards):
        at, off = columns * d // 128, columns * d % 128
        tile = ref[d // 16, d // 8 % 2, d // 2 % 4, 16 * (d % 2):16 * (d % 2) + 16, :][:rows]
        tile = pltpu.roll(tile, off, 1) if off else tile
        if off + columns > 128:
            blocks[at + 1] = blocks[at + 1] + jnp.where(lane < off, tile, 0.0)
            tile = jnp.where(lane < off, 0.0, tile)
        blocks[at] = blocks[at] + tile
    return blocks


def forward_kernel(plan, routes, win_ref, wout_ref, vec_ref, srow_ref, prev_ref, x_hbm, dout_hbm,
                   logits_ref, probs_ref, gq_ref, gu_ref, go_ref, qkv_hbm, mixed_hbm, hlow_hbm, none_hbm, act_hbm, gp_hbm, out_hbm, dsec_hbm, ddown_hbm,
                   small_ref, sone_ref, sums_ref,
                   gv_ref, mask_ref, cin_ref, cout_ref, cvec_ref, w_ref, wo_ref, x_ref, dout_ref, qkv_ref, mixed_ref, hlow_ref, none_ref,
                   act_ref, gp_ref, hid_ref, sec_ref, out_ref, dsec_ref, ddown_ref, send_sem, recv_sem, loc_sem, out_sem, row_sem):
    g = pl.program_id(0)
    rows, width = x_hbm.shape
    hidden = act_hbm.shape[1]
    last = pl.num_programs(0) - 1
    tile = 256
    y, c, z, x = coords()
    V, Q, O, U = 0, 1, 4, 7
    chunks = [(3, 0, 128, 0)] + [(0, 768 * i, 768, 768 * i) for i in range(3)] + [(2, 256 * i, 256, 256 * i) for i in range(3)]
    chunks += [(1, 768 * i, 768, 3 * width + 768 * i) for i in range(4)]
    ga = Gather(chunks, routes, [cin_ref, cin_ref, cout_ref, cvec_ref], [gq_ref, gu_ref, go_ref, gv_ref], send_sem, recv_sem)

    def run(place):
        for stage, k in plan.get(place, ()):
            (ga.s1, ga.s2, ga.s3)[stage - 1](k)

    def load(src, dst, i):
        return pltpu.make_async_copy(src, dst, loc_sem.at[i])

    def save(src, dst, i):
        return pltpu.make_async_copy(src, dst, out_sem.at[i])

    stores = lambda: [load(cin_ref.at[:, pl.ds(0, 3 * width)], gq_ref.at[y, c, z, ga.rows_of(Q, x)], 0),
                      load(cin_ref.at[:, pl.ds(3 * width, hidden)], gu_ref.at[y, c, z, ga.rows_of(U, x)], 1),
                      load(cout_ref, go_ref.at[y, c, z, ga.rows_of(O, x)], 2)]
    x_in, dout_in = lambda: load(x_hbm, x_ref, 3), lambda: load(dout_hbm, dout_ref, 4)
    w_out, w_up, w_qkv = go_ref.reshape(width + hidden, width), gu_ref.reshape(width, hidden), gq_ref.reshape(width, 3 * width)

    def quarters(src, columns, slot):
        size = width // 4
        return [load(src.at[pl.ds(size * i, size), columns], w_ref.at[slot, pl.ds(size * i, size), :], 8 + 4 * slot + i) for i in range(4)]
    w_q = lambda k: quarters(w_qkv, pl.ds(768 * k, 768), k % 2)
    w_u = lambda k: quarters(w_up, pl.ds(768 * k, 768), (k + 1) % 2)
    w_o = lambda: quarters(w_out, slice(None), 0)
    w_down = lambda: load(w_out.at[pl.ds(width, hidden), :], wo_ref, 7)
    saves = {"mixed": lambda: save(mixed_ref, mixed_hbm, 1), "hlow": lambda: save(hlow_ref, hlow_hbm, 2),
             "none": lambda: save(none_ref, none_hbm, 3), "qkv": lambda: save(qkv_ref, qkv_hbm, 4)}
    save_act = lambda k: save(act_ref.at[:, pl.ds(768 * k, 768)], act_hbm.at[:, pl.ds(768 * k, 768)], 5 + k)
    save_gp = lambda k: save(gp_ref.at[k % 2], gp_hbm.at[:, pl.ds(768 * k, 768)], 9 + k)

    @pl.when(g == 0)
    def _():
        barrier = pltpu.get_barrier_semaphore()
        peers = peers_of(y, c, z, x)
        for p in peers:
            pl.semaphore_signal(barrier, inc=1, device_id=p, device_id_type=MESH)
        cvec_ref[...] = jnp.zeros_like(cvec_ref)
        vec = vec_ref[...].astype(jnp.bfloat16).astype(jnp.float32)
        cvec_ref[0:vec.shape[0], 0:vec.shape[1]] = vec
        gv_ref[y, c, z, ga.rows_of(V, x), :] = cvec_ref[...]
        cin_ref[...] = win_ref[...].astype(jnp.bfloat16)
        cout_ref[...] = wout_ref[...].astype(jnp.bfloat16)
        pl.semaphore_wait(barrier, len(peers))
        for k in range(len(chunks)):
            ga.start(k)
        for s in stores():
            s.start()
        x_in().start()
        seg = jnp.broadcast_to(srow_ref[...].astype(jnp.float32), (rows, rows))
        mask_ref[...] = jnp.where(seg == seg.T, 0.0, NEG)
        for s in stores():
            s.wait()
        dout_in().start()
        run("start")
        ga.s4(V)
        run("small")
        spread = spread_columns(gv_ref, 32, vec_ref.shape[1], vec_ref.shape[0], width)
        for i, v in enumerate(spread):
            small_ref[:, 128 * i:128 * (i + 1)] = v
        x_in().wait()

        @pl.loop(0, 3)
        def _(k):
            for i in range(3):
                @pl.when(k == i)
                def _():
                    run(("q", i))
                    ga.s4(Q + i)
                    for d in w_q(i):
                        d.start()
                    run(("qw", i))
                    for d in w_q(i):
                        d.wait()
            bias = jnp.where(k == 1, 0.0, small_ref[pl.ds(4 + k // 2, 1), :])
            v = dotf(x_ref[...], w_ref[lax.rem(k, 2)], NN) + bias
            qkv_ref[:, pl.ds(pl.multiple_of(768 * k, 768), 768)] = v.astype(jnp.bfloat16)
        saves["qkv"]().start()

    for i in range(6):
        if plan.get(("pair", i)):
            @pl.when(g == i)
            def _():
                run(("pair", i))

    at = lambda off: pl.ds(pl.multiple_of(off * width + g * 128, 128), 128)
    left = half_masks(rows)
    q2 = qkv_ref[:, at(0)] * jnp.bfloat16(0.125)
    k2 = qkv_ref[:, at(1)]
    v2 = qkv_ref[:, at(2)]
    zero = jnp.zeros_like(v2)
    outs = []
    for h in range(2):
        pick = (lambda v: jnp.where(left, v, zero)) if h == 0 else (lambda v: jnp.where(left, zero, v))
        raw = dotf(pick(q2), k2, NT) + prev_ref[h].astype(jnp.float32)
        logits_ref[h] = raw.astype(jnp.bfloat16)
        s = raw + mask_ref[...]
        e = jnp.exp(s - jnp.max(s, axis=1, keepdims=True))
        probs = (e * (1.0 / jnp.sum(e, axis=1, keepdims=True))).astype(jnp.bfloat16)
        probs_ref[h] = probs
        outs.append(dotf(probs, pick(v2), NN))
    mixed_ref[:, pl.ds(pl.multiple_of(g * 128, 128), 128)] = (outs[0] + outs[1]).astype(jnp.bfloat16)

    @pl.when(g == last)
    def _():
        saves["mixed"]().start()
        run("out")
        for k in range(3):
            ga.s4(O + k)
        for d in w_o():
            d.start()
        w_down().start()
        run("outw")
        for d in w_o():
            d.wait()
        hid_ref[...] = x_ref[...].astype(jnp.float32) + (dotf(mixed_ref[...], w_ref[0], NN) + small_ref[6:7, :])
        run("norm")

        @pl.loop(0, rows // 128)
        def _(i):
            sl = pl.ds(pl.multiple_of(i * 128, 128), 128)
            normed, scaling = normalise(hid_ref[sl, :])
            none_ref[sl, :] = normed
            sone_ref[sl, :] = jnp.broadcast_to(scaling, (128, 128))
            hid = normed * small_ref[0:1, :] + small_ref[2:3, :]
            sec_ref[sl, :] = hid + small_ref[7:8, :]
            hlow_ref[sl, :] = hid.astype(jnp.bfloat16)

        saves["none"]().start()
        saves["hlow"]().start()

        @pl.loop(0, 4)
        def _(k):
            for i in range(4):
                @pl.when(k == i)
                def _():
                    run(("up", i))
                    ga.s4(U + i)
                    for d in w_u(i):
                        d.start()
                    run(("upw", i))
                    for d in w_u(i):
                        d.wait()
                    if i >= 2:
                        save_gp(i - 2).wait()

            @pl.loop(0, 768 // tile)
            def _(j):
                sl = pl.ds(pl.multiple_of(j * tile, tile), tile)
                to = pl.ds(pl.multiple_of(768 * k + j * tile, tile), tile)
                u = dotf(hlow_ref[...], w_ref[lax.rem(k + 1, 2), :, sl], NN) + small_ref[pl.ds(8 + k, 1), sl]
                cdf = 0.5 * (1.0 + lax.erf(u * math.sqrt(0.5)))
                act_ref[:, to] = (u * cdf).astype(jnp.bfloat16)
                gp_ref[lax.rem(k, 2), :, sl] = (cdf + u * (jnp.exp(-0.5 * (u * u)) * (1.0 / math.sqrt(2.0 * math.pi)))).astype(jnp.bfloat16)
            for i in range(4):
                @pl.when(k == i)
                def _():
                    save_act(i).start()
                    save_gp(i).start()
                    if i == 0:
                        w_down().wait()
            part = pl.ds(pl.multiple_of(768 * k, 768), 768)
            sec_ref[...] += dotf(act_ref[:, part], wo_ref[part, :], NN)
        sums_ref[...] = jnp.zeros_like(sums_ref)
        dout_in().wait()

        def row_saves(i):
            sl = pl.ds(pl.multiple_of(i * 128, 128), 128)
            return [pltpu.make_async_copy(a.at[sl, :], b.at[sl, :], row_sem.at[n, i])
                    for n, (a, b) in enumerate(((out_ref, out_hbm), (dsec_ref, dsec_hbm), (ddown_ref, ddown_hbm)))]

        @pl.loop(0, rows // 128)
        def _(i):
            sl = pl.ds(pl.multiple_of(i * 128, 128), 128)
            normed, scaling = normalise(sec_ref[sl, :])
            out_ref[sl, :] = (normed * small_ref[1:2, :] + small_ref[3:4, :]).astype(jnp.bfloat16)
            dy = dout_ref[sl, :].astype(jnp.float32)
            back = norm_back(dy, normed, scaling, small_ref[1:2, :])
            low = back.astype(jnp.bfloat16)
            dsec_ref[sl, :] = back
            ddown_ref[sl, :] = low
            sums_ref[0:1, :] += jnp.sum(dy * normed, axis=0, keepdims=True)
            sums_ref[1:2, :] += jnp.sum(dy, axis=0, keepdims=True)
            sums_ref[2:3, :] += jnp.sum(low.astype(jnp.float32), axis=0, keepdims=True)
            for d in row_saves(i):
                d.start()
        for k in range(len(chunks)):
            ga.finish(k)
        for s in saves.values():
            s().wait()
        for k in range(4):
            save_act(k).wait()
        for k in (2, 3):
            save_gp(k).wait()

        @pl.loop(0, rows // 128)
        def _(i):
            for d in row_saves(i):
                d.wait()


def forward_all(plan, routes, tokens, grad_out, weight_in, weight_out, vectors, prev, seg):
    rows, width = tokens.shape
    heads = prev.shape[0]
    hidden = weight_in.shape[1] - 3 * width
    f32, bf16 = jnp.float32, jnp.bfloat16
    fixed = lambda shape: pl.BlockSpec(shape, lambda g: (0,) * len(shape), pipeline_mode=pl.Buffered(1))
    pair = pl.BlockSpec((2, rows, rows), lambda g: (g, 0, 0))
    hbm = pl.BlockSpec(memory_space=pl.ANY)
    far = [((2, 2, 4, 2 * weight_in.shape[0], 3 * width), bf16), ((2, 2, 4, 2 * weight_in.shape[0], hidden), bf16),
           ((2, 2, 4, 2 * weight_out.shape[0], width), bf16), ((rows, 3 * width), bf16), ((rows, width), bf16), ((rows, width), bf16),
           ((rows, width), f32), ((rows, hidden), bf16), ((rows, hidden), bf16), ((rows, width), bf16), ((rows, width), f32), ((rows, width), bf16)]
    near = [((vectors.shape[0], width), f32), ((rows, 128), f32), ((8, width), f32)]
    v = lambda *shape: pltpu.VMEM(shape, bf16)
    vf = lambda *shape: pltpu.VMEM(shape, f32)
    dma = pltpu.SemaphoreType.DMA
    return pl.pallas_call(
        functools.partial(forward_kernel, plan, routes),
        grid=(heads // 2,),
        in_specs=[fixed(weight_in.shape), fixed(weight_out.shape), fixed(vectors.shape), fixed((1, rows)), pair, hbm, hbm],
        out_specs=[pair, pair] + [hbm] * len(far) + [fixed(s) for s, _ in near],
        out_shape=[jax.ShapeDtypeStruct(prev.shape, bf16)] * 2 + [jax.ShapeDtypeStruct(s, t) for s, t in far + near],
        scratch_shapes=[
            vf(2, 2, 4, 32, 128), vf(rows, rows), v(*weight_in.shape), v(*weight_out.shape), vf(16, 128), v(2, width, 768), v(hidden, width),
            v(rows, width), v(rows, width), v(rows, 3 * width), v(rows, width), v(rows, width), vf(rows, width), v(rows, hidden),
            v(2, rows, 768), vf(rows, width), vf(rows, width), v(rows, width), vf(rows, width), v(rows, width), dma((11, 10)),
            dma((11, 10)), dma((16,)), dma((13,)), dma((3, rows // 128))],
        compiler_params=pltpu.CompilerParams(collective_id=1, has_side_effects=True, vmem_limit_bytes=64 * 2**20 - 65536),
        name="forward",
    )(weight_in, weight_out, vectors, seg.reshape(1, rows), prev, tokens, grad_out)


class Scatter:
    def __init__(self, routes, full, got, send_sem, recv_sem):
        self.routes, self.full, self.got = routes, full, got
        self.send_sem, self.recv_sem = send_sem, recv_sem
        y, c, z, x = self.y, self.c, self.z, self.x = coords()
        first, second = (1 - y) * 2 + c, z * 2 + 1 - x
        self.core = dev(y, 1 - c, z, x)
        self.one = (jnp.where(c == 0, first, y * 2 + c), jnp.where(c == 0, z * 2 + x, second))
        self.two = (jnp.where(c == 0, y * 2 + c, first), jnp.where(c == 0, second, z * 2 + x))
        self.at_one = (jnp.where(c == 0, 1 - y, y), jnp.where(c == 0, x, 1 - x))
        self.at_two = (jnp.where(c == 0, y, 1 - y), jnp.where(c == 0, 1 - x, x))

    def copy(self, src, dst, k, slot, who):
        return pltpu.make_async_remote_copy(
            src_ref=src, dst_ref=dst, send_sem=self.send_sem.at[k, slot], recv_sem=self.recv_sem.at[k, slot],
            device_id=who, device_id_type=MESH)

    def to_core(self, k):
        return self.copy(self.full[k]().at[:, 1 - self.c], self.got[k][0], k, 0, self.core)

    def to_one(self, k):
        full = self.full[k]()
        return [self.copy(full.at[1 - self.y, self.c, :, 1 - self.x], self.got[k][1].at[0], k, 1, self.one),
                self.copy(full.at[self.at_one[0], self.c, :, self.at_one[1]], self.got[k][1].at[1], k, 2, self.one)]

    def to_two(self, k):
        return self.copy(self.full[k]().at[self.at_two[0], self.c, :, self.at_two[1]], self.got[k][2], k, 3, self.two)

    def along_z(self, k):
        full = self.full[k]()
        out = []
        for i in range(3):
            z = lax.rem(self.z + i + 1, 4)
            out.append(self.copy(full.at[self.y, self.c, z, self.x], self.got[k][3].at[i], k, 4 + i, dev(self.y, self.c, z, self.x)))
        return out

    def r1(self, k):
        self.to_core(k).start()

    def r2(self, k):
        full, got = self.full[k](), self.got[k][0]
        self.to_core(k).wait_recv()

        @pl.loop(0, 8)
        def _(i):
            for y in range(2):
                z, x = i // 2, lax.rem(i, 2)
                total = full[y, self.c, z, x].astype(jnp.float32) + got[y, z, x].astype(jnp.float32)
                full[y, self.c, z, x] = total.astype(full.dtype)
        for d in self.to_one(k):
            d.start()

    def early_z(self, k):
        full, (y, x) = self.full[k](), self.at_two
        out = []
        for i in range(3):
            z = lax.rem(self.z + i + 1, 4)
            who = dev(self.y, self.c, z, self.x)
            out.append(self.copy(full.at[self.y, self.c, z, self.x], self.got[k][2].at[i, 0], k, 3 + 2 * i, who))
            out.append(self.copy(full.at[y, self.c, z, x], self.got[k][2].at[i, 1], k, 4 + 2 * i, who))
        return out

    def last_two(self, k):
        y, x = self.at_two
        return self.copy(self.full[k]().at[y, self.c, self.z, x], self.got[k][3].at[0], k, 9, self.two)

    def add(self, full, spot, *terms):
        total = full[spot].astype(jnp.float32)
        for t in terms:
            total = total + t.astype(jnp.float32)
        full[spot] = total.astype(full.dtype)

    def r3(self, k):
        full, got = self.full[k](), self.got[k][1]
        for d in self.to_one(k):
            d.wait_recv()
        y, x = self.at_two
        straight = self.routes[k] == "z"

        @pl.loop(0, 4)
        def _(z):
            self.add(full, (y, self.c, z, x), got[0, z])
            if not straight:
                self.add(full, (self.y, self.c, z, self.x), got[1, z])
        for d in [self.to_two(k)] if straight else self.early_z(k):
            d.start()

    def r4(self, k):
        full, got = self.full[k](), self.got[k]
        mine = (self.y, self.c, self.z, self.x)
        if self.routes[k] == "n":
            for d in self.early_z(k):
                d.wait_recv()
            y, x = self.at_two
            self.add(full, (y, self.c, self.z, x), *[got[2][i, 1] for i in range(3)])
            self.last_two(k).start()
            self.add(full, mine, *[got[2][i, 0] for i in range(3)])
            return
        self.to_two(k).wait_recv()

        @pl.loop(0, 4)
        def _(z):
            self.add(full, (self.y, self.c, z, self.x), got[1][1, z], got[2][z])
        for d in self.along_z(k):
            d.start()

    def r5(self, k):
        last = [self.last_two(k)] if self.routes[k] == "n" else self.along_z(k)
        for d in last:
            d.wait_recv()
        total = self.full[k]()[self.y, self.c, self.z, self.x].astype(jnp.float32)
        for i in range(len(last)):
            total = total + self.got[k][3][i].astype(jnp.float32)
        return total

    def finish(self, k):
        rest = [*self.early_z(k), self.last_two(k)] if self.routes[k] == "n" else [self.to_two(k), *self.along_z(k)]
        for d in [self.to_core(k), *self.to_one(k), *rest]:
            d.wait_send()


def put_rows(ref, start, value):
    size, count = ref.shape[4], value.shape[0]
    for d in range(start // size, (start + count - 1) // size + 1):
        low, high = max(start, d * size), min(start + count, (d + 1) * size)
        ref[d // 16, d // 8 % 2, d // 2 % 4, d % 2, low - d * size:high - d * size] = value[low - start:high - start]


def own_columns(value, shards, columns):
    for d in range(shards):
        at, off = columns * d // 128, columns * d % 128
        if off + columns <= 128:
            tile = value[:, 128 * at:128 * (at + 1)]
            yield d, pltpu.roll(tile, 128 - off, 1) if off else tile
        else:
            yield d, pltpu.roll(value[:, 128 * at:128 * (at + 2)], 256 - off, 1)[:, :128]


def backward_kernel(heads, plan, routes, columns, *refs):
    (ddown_ref, hlow_ref, small_ref, two_ref, sone_ref, probs_ref, dl_ref,
     act_hbm, gp_hbm, go_hbm, gu_hbm, gq_hbm, dsec_hbm, none_hbm, mixed_hbm, x_hbm, qkv_hbm,
     dprev_ref, dx_ref, gin_ref, gout_ref, gvec_ref, norm_ref) = refs[:23]
    qkv_ref, do_ref, x_ref, mixed_ref, act_ref, gp_ref, dup_ref, w_ref, acc_ref, none_ref, part_ref, fvec_ref = refs[23:35]
    ups, outs = refs[35:37]
    got_flat = refs[37:93]
    nmine, ngot, send_sem, recv_sem, loc_sem, ns_sem, nr_sem = refs[93:]
    g = pl.program_id(0)
    rows, width = ddown_ref.shape
    hidden = act_hbm.shape[1]
    tile = 256
    U, O, Q, V = 0, 4, 7, 13
    got = [got_flat[4 * k:4 * k + 4] for k in range(14)]
    full = [lambda k=k: ups.at[k] for k in range(4)] + [lambda j=j: outs.at[j] for j in range(3)]
    full += [lambda p=p: ups.at[p // 2, :, :, :, :, :, :, pl.ds(384 * (p % 2), 384)] for p in range(6)] + [lambda: fvec_ref]
    sc = Scatter(routes, full, got, send_sem, recv_sem)
    y, c, z, x = coords()
    peers = peers_of(y, c, z, x)
    stages = {1: sc.r1, 2: sc.r2, 3: sc.r3, 4: sc.r4}

    def run(place):
        for stage, k in plan.get(place, ()):
            if stage == 5:
                finish(k)
            else:
                stages[stage](k)

    def finish(k):
        total = sc.r5(k)
        if k < O:
            gin_ref[:, :, 3 * width + 768 * k:3 * width + 768 * (k + 1)] = total
        elif k < Q:
            gout_ref[:, :, 256 * (k - O):256 * (k - O + 1)] = total
        elif k < V:
            for i in range(3):
                gin_ref[:, :, width * i + 128 * (k - Q):width * i + 128 * (k - Q + 1)] = total[:, :, 128 * i:128 * (i + 1)]
        else:
            lane = lax.broadcasted_iota(jnp.int32, total.shape, 1)
            gvec_ref[...] = jnp.where(lane < columns, total, 0.0)

    def load(src, dst, i):
        return pltpu.make_async_copy(src, dst, loc_sem.at[i])

    near = [dev(lax.rem(y + i // 4, 2), lax.rem(c + i // 2 % 2, 2), z, lax.rem(x + i % 2, 2)) for i in range(1, 8)]
    far = [dev(y, c, lax.rem(z + i, 4), x) for i in (1, 2, 3)]

    def share(i):
        return pltpu.make_async_remote_copy(
            src_ref=nmine.at[0 if i < 7 else 1], dst_ref=ngot.at[i], send_sem=ns_sem.at[i], recv_sem=nr_sem.at[i],
            device_id=(near + far)[i], device_id_type=MESH)

    def in_order(values, index):
        total = jnp.zeros_like(values[0])
        for at in range(len(values)):
            for i, v in enumerate(values):
                total = total + jnp.where(index(i) == at, v, 0.0)
        return total

    w_out, w_up, w_qkv = go_hbm.reshape(width + hidden, width), gu_hbm.reshape(width, hidden), gq_hbm.reshape(width, 3 * width)
    late = lambda: [load(dsec_hbm, acc_ref, 0), load(none_hbm, none_ref, 1), load(mixed_hbm, mixed_ref, 2), load(x_hbm, x_ref, 3),
                    load(qkv_hbm, qkv_ref, 4), load(act_hbm, act_ref, 8)]
    last_w = lambda: [load(w_qkv.at[:, pl.ds(768 * i, 768)], w_ref.at[i], 5 + i) for i in range(3)]

    @pl.when(g == 0)
    def _():
        barrier = pltpu.get_barrier_semaphore()
        met = far + near
        for p in met:
            pl.semaphore_signal(barrier, inc=1, device_id=p, device_id_type=MESH)

        def ahead(k):
            return [load(w_out.at[pl.ds(width + 768 * k, 768), :], w_ref.at[0], 5), load(gp_hbm.at[:, pl.ds(768 * k, 768)], gp_ref, 6)]

        def behind(k):
            return [load(w_up.at[:, pl.ds(768 * k, 768)], w_ref.at[1], 7)]
        for d in ahead(0) + behind(0) + late():
            d.start()
        part_ref[...] = jnp.zeros_like(part_ref)
        part_ref[1:2, :] = two_ref[0:1, :]
        part_ref[3:4, :] = two_ref[1:2, :]
        part_ref[7:8, :] = two_ref[2:3, :]
        pl.semaphore_wait(barrier, len(met))

        @pl.loop(0, 4)
        def _(k):
            for i in range(4):
                @pl.when(k == i)
                def _():
                    for d in ahead(i):
                        d.wait()
            low = (dotf(ddown_ref[...], w_ref[0], NT) * gp_ref[...].astype(jnp.float32)).astype(jnp.bfloat16)
            dup_ref[...] = low
            part_ref[pl.ds(8 + k, 1), :] = jnp.sum(low.astype(jnp.float32), axis=0, keepdims=True)
            ups[k] = dotf(hlow_ref[...], dup_ref[...], TN).reshape(ups.shape[1:]).astype(jnp.bfloat16)
            for i in range(4):
                @pl.when(k == i)
                def _():
                    sc.r1(U + i)
                    if i < 3:
                        for d in ahead(i + 1):
                            d.start()
                    run(("down", i))
                    if i == 0:
                        late()[0].wait()
                    for d in behind(i):
                        d.wait()
            acc_ref[...] += dotf(dup_ref[...], w_ref[1], NT)
            for i in range(4):
                @pl.when(k == i)
                def _():
                    if i < 3:
                        for d in behind(i + 1):
                            d.start()
                    run(("up", i))

        wo = load(w_out.at[pl.ds(0, width), :], w_ref.at[0], 5)
        wo.start()
        late()[1].wait()

        @pl.loop(0, rows // 64)
        def _(i):
            sl = pl.ds(pl.multiple_of(i * 64, 64), 64)
            one, normed = acc_ref[sl, :], none_ref[sl, :]
            part_ref[0:1, :] += jnp.sum(one * normed, axis=0, keepdims=True)
            part_ref[2:3, :] += jnp.sum(one, axis=0, keepdims=True)
            back = norm_back(one, normed, sone_ref[sl, 0:1], small_ref[0:1, :])
            low = back.astype(jnp.bfloat16)
            acc_ref[sl, :] = back
            dup_ref[sl, :] = low
            part_ref[6:7, :] += jnp.sum(low.astype(jnp.float32), axis=0, keepdims=True)
        run("norm")
        late()[2].wait()
        late()[5].wait()

        def put(start, value):
            for j in range(3):
                put_rows(outs.at[j], start, value[:, tile * j:tile * (j + 1)].reshape(96, 8, tile).astype(jnp.bfloat16))
        put(0, dotf(mixed_ref[...], dup_ref[...], TN))
        for k in range(4):
            put((width + 768 * k) // 8, dotf(act_ref[:, 768 * k:768 * (k + 1)], ddown_ref[...], TN))
        for j in range(3):
            sc.r1(O + j)
        run("out")
        wo.wait()
        do_ref[...] = dotf(dup_ref[...], w_ref[0], NT).astype(jnp.bfloat16)
        for d in late()[3:5]:
            d.wait()
        for d in last_w():
            d.start()

    for i in range(heads):
        if plan.get(("head", i)):
            @pl.when(g == i)
            def _():
                run(("head", i))

    pair, half = g // 2, lax.rem(g, 2)
    at = lambda off: pl.ds(pl.multiple_of(off * width + pair * 128, 128), 128)
    lane = lax.broadcasted_iota(jnp.int32, (rows, 128), 1)
    pick = lambda v: jnp.where(lane // 64 == half, v, jnp.zeros_like(v))
    q2, k2, v2, do2 = qkv_ref[:, at(0)], qkv_ref[:, at(1)], qkv_ref[:, at(2)], do_ref[:, at(0)]
    p = probs_ref[0].astype(jnp.float32)
    dp = dotf(pick(do2), v2, NT)
    ds = p * (dp - jnp.sum(p * dp, axis=1, keepdims=True))
    grad = (ds + dl_ref[0].astype(jnp.float32)).astype(jnp.bfloat16)
    dprev_ref[0] = grad
    dq = (dotf(grad, pick(k2), NN) * 0.125).astype(jnp.bfloat16)
    dk = (dotf(dprev_ref[0], pick(q2), TN) * 0.125).astype(jnp.bfloat16)
    dv = dotf(probs_ref[0], pick(do2), TN).astype(jnp.bfloat16)

    @pl.when(half == 0)
    def _():
        for i, v in enumerate((dq, dk, dv)):
            gp_ref[:, 128 * i:128 * (i + 1)] = v

    @pl.when(half == 1)
    def _():
        for i, v in enumerate((dq, dk, dv)):
            v = gp_ref[:, 128 * i:128 * (i + 1)] + v
            gp_ref[:, 128 * i:128 * (i + 1)] = v
            qkv_ref[:, at(i)] = v
            if i != 1:
                part_ref[4 + i // 2:5 + i // 2, at(0)] = jnp.sum(v.astype(jnp.float32), axis=0, keepdims=True)
        for p in range(0, heads // 2, 2):
            @pl.when(pair == p)
            def _():
                sc.finish(U + p // 2)
        to = pl.ds(pl.multiple_of(384 * lax.rem(pair, 2), 384), 384)
        ups[pair // 2, :, :, :, :, :, :, to] = dotf(x_ref[...], gp_ref[:, 0:384], TN).reshape(ups.shape[1:7] + (384,)).astype(jnp.bfloat16)
        for p in range(heads // 2):
            @pl.when(pair == p)
            def _():
                sc.r1(Q + p)

    @pl.when(g == heads - 1)
    def _():
        for d, tile_of in own_columns(part_ref[...], 32, columns):
            fvec_ref[d // 16, d // 8 % 2, d // 2 % 4, d % 2] = tile_of
        sc.r1(V)
        run("end")
        for d in last_w():
            d.wait()

        @pl.loop(0, 3)
        def _(i):
            acc_ref[...] += dotf(qkv_ref[:, pl.ds(pl.multiple_of(768 * i, 768), 768)], w_ref[i], NT)
            for j in range(3):
                @pl.when(i == j)
                def _():
                    run(("dx", j))
        dx_ref[...] = acc_ref[...].astype(jnp.bfloat16)
        run("last")
        squares = gvec_ref[0:8, :] * gvec_ref[0:8, :] + gvec_ref[8:16, :] * gvec_ref[8:16, :]
        for ref in (gin_ref, gout_ref):
            v = ref[...]
            v = jnp.sum(v * v, axis=0)
            for j in range(v.shape[1] // 128):
                squares = squares + v[:, 128 * j:128 * (j + 1)]
        nmine[0] = jnp.sum(squares, keepdims=True) + jnp.zeros((8, 128), jnp.float32)
        for i in range(7):
            share(i).start()
        for k in range(14):
            if k not in (0, 1, 2):
                sc.finish(k)
        for i in range(7):
            share(i).wait_recv()
        me = y * 4 + c * 2 + x

        def from_near(i):
            return me if i == 0 else lax.rem(y + i // 4, 2) * 4 + lax.rem(c + i // 2 % 2, 2) * 2 + lax.rem(x + i % 2, 2)
        plane = in_order([nmine[0]] + [ngot[i] for i in range(7)], from_near)
        nmine[1] = plane
        for i in range(7, 10):
            share(i).start()
        for i in range(7, 10):
            share(i).wait_recv()
        total = in_order([plane] + [ngot[i] for i in range(7, 10)], lambda i: lax.rem(z - i + 4, 4))
        norm_ref[...] = jnp.sqrt(total)
        for i in range(10):
            share(i).wait_send()


def backward_all(plan, routes, columns, grad_down, hidden_low, small, two_sums, scale_one, probs, grad_logits,
                 activated, slope, full_out, full_up, full_qkv, grad_second, normed_one, mixed, tokens, qkv):
    rows, width = tokens.shape
    heads = probs.shape[0]
    hidden = activated.shape[1]
    f32, bf16 = jnp.float32, jnp.bfloat16
    fixed = lambda shape: pl.BlockSpec(shape, lambda g: (0,) * len(shape), pipeline_mode=pl.Buffered(1))
    head = pl.BlockSpec((1, rows, rows), lambda g: (g, 0, 0))
    hbm = pl.BlockSpec(memory_space=pl.ANY)
    r_in, r_out = full_qkv.shape[3] // 2, full_out.shape[3] // 2
    landing = []
    kinds = [((r_in // 8, 8, 768), bf16)] * 4 + [((r_out // 8, 8, 256), bf16)] * 3 + [((r_in // 8, 8, 384), bf16)] * 6 + [((16, 128), f32)]
    for (shape, kind), route in zip(kinds, routes):
        rest = [(4,), (3,)] if route == "z" else [(3, 2), (1,)]
        landing += [pltpu.VMEM(first + shape, kind) for first in [(2, 4, 2), (2, 4)] + rest]
    lead = (2, 2, 4, 2)
    v = lambda *shape: pltpu.VMEM(shape, bf16)
    vf = lambda *shape: pltpu.VMEM(shape, f32)
    shapes = [((r_in // 8, 8, 3 * width + hidden), f32), ((r_out // 8, 8, width), f32), ((16, 128), f32), ((8, 128), f32)]
    dma = pltpu.SemaphoreType.DMA
    return pl.pallas_call(
        functools.partial(backward_kernel, heads, plan, routes, columns),
        grid=(heads,),
        in_specs=[fixed((rows, width)), fixed((rows, width)), fixed(small.shape), fixed(two_sums.shape),
                  fixed(scale_one.shape), head, head] + [hbm] * 10,
        out_specs=[head, fixed((rows, width))] + [fixed(s) for s, _ in shapes],
        out_shape=[jax.ShapeDtypeStruct(probs.shape, bf16), jax.ShapeDtypeStruct((rows, width), bf16)]
        + [jax.ShapeDtypeStruct(s, t) for s, t in shapes],
        scratch_shapes=[v(rows, 3 * width), v(rows, width), v(rows, width), v(rows, width), v(rows, hidden),
                        v(rows, 768), v(rows, 768), v(3, 768, width), vf(rows, width), vf(rows, width),
                        vf(16, width), vf(*lead, 16, 128)]
        + [v(4, *lead, r_in // 8, 8, 768), v(3, *lead, r_out // 8, 8, 256)] + landing
        + [vf(2, 8, 128), vf(10, 8, 128), dma((14, 10)), dma((14, 10)), dma((10,)), dma((10,)), dma((10,))],
        compiler_params=pltpu.CompilerParams(collective_id=2, has_side_effects=True, vmem_limit_bytes=64 * 2**20 - 65536),
        name="backward",
    )(grad_down, hidden_low, small, two_sums, scale_one, probs, grad_logits,
      activated, slope, full_out, full_up, full_qkv, grad_second, normed_one, mixed, tokens, qkv)


def update_kernel(norm_ref, step_ref, *refs):
    through, refs = refs[:4], refs[4:]
    trios, refs = [refs[4 * i:4 * i + 4] for i in range(3)], refs[12:]
    through_out, refs = refs[:4], refs[4:]
    outs, gn_ref = [refs[5 * i:5 * i + 5] for i in range(3)], refs[15]
    for a, b in zip(through, through_out):
        b[...] = a[...]
    norm = norm_ref[0:1, 0:1]
    gn_ref[...] = norm
    factor = jnp.minimum(1.0, clip_scale * math.sqrt(PARAMS) / (norm + 1e-06))
    step = jnp.full((1, 1), step_ref[0], jnp.int32).astype(jnp.float32)
    one = 1.0 - jnp.exp(step * math.log(beta_one))
    two = 1.0 - jnp.exp(step * math.log(beta_two))
    for i, ((g_ref, w_ref, m_ref, v_ref), out) in enumerate(zip(trios, outs)):
        rate, decay = (rate_vector, 0.0) if i == 2 else (rate_matrix, decay_matrix)
        grad = g_ref[...].reshape(w_ref.shape) if i < 2 else g_ref[0:w_ref.shape[0], 0:w_ref.shape[1]]
        clipped = grad * factor
        moment = beta_one * m_ref[...] + (1.0 - beta_one) * clipped
        square = beta_two * v_ref[...] + (1.0 - beta_two) * clipped * clipped
        weight = w_ref[...] - rate * ((moment / one) / (jnp.sqrt(square / two) + adam_eps) + decay * w_ref[...])
        for ref, val in zip(out, (clipped, moment, square, weight, weight.astype(jnp.bfloat16))):
            ref[...] = val


def update_all(norm, step_count, through, trios):
    steps = 2
    f32 = jnp.float32

    def spec(a):
        if a.shape[-1] < 128 * steps:
            return pl.BlockSpec(a.shape, lambda g: (0,) * a.ndim)
        return pl.BlockSpec(a.shape[:-1] + (a.shape[-1] // steps,), lambda g: (0,) * (a.ndim - 1) + (g,))
    slabs = [pl.BlockSpec((a.shape[0] // steps,) + a.shape[1:], lambda g: (g, 0, 0)) if a.ndim == 3 else spec(a) for a in through]
    shapes = []
    for g, w, m, v in trios:
        shapes += [jax.ShapeDtypeStruct(w.shape, t) for t in (f32, f32, f32, f32, jnp.bfloat16)]
    flat = [a for trio in trios for a in trio]
    return pl.pallas_call(
        update_kernel,
        grid=(steps,),
        in_specs=[pl.BlockSpec((8, 128), lambda g: (0, 0)), pl.BlockSpec(memory_space=pltpu.SMEM)] + slabs + [spec(a) for a in flat],
        out_specs=slabs + [spec(s) for s in shapes] + [pl.BlockSpec((1, 1), lambda g: (0, 0))],
        out_shape=[jax.ShapeDtypeStruct(a.shape, a.dtype) for a in through] + shapes + [jax.ShapeDtypeStruct((1, 1), f32)],
        compiler_params=pltpu.CompilerParams(vmem_limit_bytes=64 * 2**20 - 65536),
        name="update",
    )(norm, step_count, *through, *flat)


def adam_update(master, moment, square, gradient, factor, step_value, step_rate, decay_rate):
    clipped = gradient * factor
    new_moment = beta_one * moment + (1.0 - beta_one) * clipped
    new_square = beta_two * square + (1.0 - beta_two) * clipped * clipped
    fixed_moment = new_moment / (1.0 - jnp.power(beta_one, step_value))
    fixed_square = new_square / (1.0 - jnp.power(beta_two, step_value))
    updated = master - step_rate * (
        fixed_moment / (jnp.sqrt(fixed_square) + adam_eps) + decay_rate * master
    )
    return (clipped, new_moment, new_square, updated)


def rounded(v):
    return lax.reduce_precision(v, 8, 7)


def gather_all(weight_in, weight_out, vectors, width):
    whole = lambda v: lax.all_gather(v, AXES, axis=0, tiled=True)
    low_in = weight_in.astype(jnp.bfloat16)
    small = lax.all_gather(rounded(vectors), AXES, axis=1, tiled=True)
    return whole(low_in[:, : 3 * width]), whole(low_in[:, 3 * width :]), whole(weight_out.astype(jnp.bfloat16)), small


def forward_plain(tokens, grad_out, full_qkv, full_up, full_out, small, prev, segments):
    width = tokens.shape[1]
    dot = lambda a, b: jnp.dot(a, b, preferred_element_type=jnp.float32)
    sums = lambda v: jnp.sum(v, axis=0, dtype=jnp.float32)
    offsets = jnp.concatenate([small[4], jnp.zeros_like(small[4]), small[5]])
    qkv = (dot(tokens, full_qkv) + offsets).astype(jnp.bfloat16)
    logits, mixed, log_sums = attn_fwd(qkv, prev, segments, 640)
    first = tokens.astype(jnp.float32) + (dot(mixed, full_out[:width]) + small[6])
    hidden_one, normed_one, scale_one = norm_rows(first, small[0], small[2])
    hidden_low = hidden_one.astype(jnp.bfloat16)
    upward = dot(hidden_low, full_up) + small[8:].reshape(-1)
    activated, gelu_pull = jax.vjp(gelu_exact, upward)
    activated, slope = activated.astype(jnp.bfloat16), gelu_pull(jnp.ones_like(upward))[0]
    second = hidden_one + (dot(activated, full_out[width:]) + small[7])
    output, normed_two, scale_two = norm_rows(second, small[1], small[3])
    grad_output = grad_out.astype(jnp.float32)
    grad_second = norm_back(grad_output, normed_two, scale_two, small[1])
    grad_down = grad_second.astype(jnp.bfloat16)
    two_sums = jnp.stack([sums(grad_output * normed_two), sums(grad_output), sums(grad_down)])
    return (logits, qkv, mixed, log_sums, hidden_low, normed_one, scale_one, activated, slope, output.astype(jnp.bfloat16),
            grad_second, grad_down, two_sums)


def reduce_all(grad_qkv, grad_up, grad_out, small, shards):
    part = lambda v: lax.psum_scatter(v, AXES, scatter_dimension=0, tiled=True).astype(jnp.float32)
    owned_in = jnp.concatenate([part(grad_qkv), part(grad_up)], axis=1)
    owned_out = part(grad_out)
    owned_small = lax.psum_scatter(small, AXES, scatter_dimension=1, tiled=True)
    total = lax.psum(jnp.sum(owned_in**2) + jnp.sum(owned_out**2) + jnp.sum(owned_small**2), AXES)
    return owned_in, owned_out, owned_small, jnp.sqrt(total)


def body(remote, hidden_in, prev_logits, segment_ids, d_hidden, d_logits, weight_in, weight_out, vectors,
         moment_in, moment_out, moment_vectors, square_in, square_out, square_vectors, step_count):
    width = weight_out.shape[1]
    shards = lax.axis_size("dp") * lax.axis_size("fsdp")
    dot = lambda spec, a, b: jnp.einsum(spec, a, b, preferred_element_type=jnp.float32)
    sums = lambda v: jnp.sum(v, axis=0, dtype=jnp.float32)
    segments = segment_ids[0]
    if remote:
        (logits, probs, full_qkv, full_up, full_out, qkv, mixed, hidden_low, normed_one, activated, slope, output, grad_second, grad_down,
         small, scale_one, two_sums) = forward_all(
             FORWARD_PLAN, ROUTES, hidden_in, d_hidden, weight_in, weight_out, vectors, prev_logits[0], segments)
        grad_prev, grad_tokens, grad_in, grad_out, grad_vec, norm = backward_all(
            BACKWARD_PLAN, BACKWARD_ROUTES, vectors.shape[1], grad_down, hidden_low, small, two_sums, scale_one, probs, d_logits[0],
            activated, slope, full_out, full_up, full_qkv, grad_second, normed_one, mixed, hidden_in, qkv)
        (logits, grad_prev, output, grad_tokens, *states, grad_norm) = update_all(
            norm, step_count, [logits, grad_prev, output, grad_tokens],
            [(grad_in, weight_in, moment_in, square_in), (grad_out, weight_out, moment_out, square_out),
             (grad_vec, vectors, moment_vectors, square_vectors)])
        clipped, moments, squares, updated, copies = [states[i::5] for i in range(5)]
        return (output, logits[None], grad_tokens, grad_prev[None], *clipped, *moments, *squares, *updated, *copies, grad_norm[0, 0])
    (full_qkv, full_up, full_out, small) = gather_all(weight_in, weight_out, vectors, width)
    (logits, qkv, mixed, log_sums, hidden_low, normed_one, scale_one, activated, slope, output,
     grad_second, grad_down, two_sums) = forward_plain(hidden_in, d_hidden, full_qkv, full_up, full_out, small, prev_logits[0], segments)
    w_attn, w_down = full_out[:width], full_out[width:]
    down_grad = dot("tf,td->fd", activated, grad_down).astype(jnp.bfloat16)
    grad_up = (dot("td,fd->tf", grad_down, w_down) * slope).astype(jnp.bfloat16)
    up_grad = dot("td,tf->df", hidden_low, grad_up).astype(jnp.bfloat16)
    grad_one = grad_second + dot("tf,df->td", grad_up, full_up)
    grad_first = norm_back(grad_one, normed_one, scale_one, small[0])
    grad_attn = grad_first.astype(jnp.bfloat16)
    attn_grad = dot("tc,td->cd", mixed, grad_attn).astype(jnp.bfloat16)
    grad_mixed = dot("td,cd->tc", grad_attn, w_attn).astype(jnp.bfloat16)
    grad_prev, grad_q, grad_k, grad_v = attn_bwd(qkv, grad_mixed, prev_logits[0], d_logits[0], log_sums, segments, 640)
    grad_qkv = jnp.concatenate([grad_q, grad_k, grad_v], axis=1)
    qkv_grad = dot("td,tc->dc", hidden_in, grad_qkv).astype(jnp.bfloat16)
    grad_tokens = (grad_first + dot("tc,dc->td", grad_qkv, full_qkv)).astype(jnp.bfloat16)
    small_grad = jnp.concatenate([
        jnp.stack([sums(grad_one * normed_one), two_sums[0], sums(grad_one), two_sums[1],
                   sums(grad_q), sums(grad_v), sums(grad_attn), two_sums[2]]),
        sums(grad_up).reshape(-1, width)], axis=0)

    owned_in, owned_out, owned_small, grad_norm = reduce_all(
        qkv_grad, up_grad, jnp.concatenate([attn_grad, down_grad], axis=0), small_grad, shards)
    factor = jnp.minimum(1.0, clip_scale * math.sqrt(PARAMS) / (grad_norm + 1e-06))
    step_value = step_count[0].astype(jnp.float32)
    new = [
        adam_update(weight_in, moment_in, square_in, owned_in, factor, step_value, rate_matrix, decay_matrix),
        adam_update(weight_out, moment_out, square_out, owned_out, factor, step_value, rate_matrix, decay_matrix),
        adam_update(vectors, moment_vectors, square_vectors, owned_small, factor, step_value, rate_vector, 0.0),
    ]
    clipped, moments, squares, updated = zip(*new)
    return (output.astype(jnp.bfloat16), logits[None], grad_tokens, grad_prev[None],
            *clipped, *moments, *squares, *updated, *[u.astype(jnp.bfloat16) for u in updated], grad_norm)


def solution(mesh):
    remote = (mesh.shape["dp"], mesh.shape["fsdp"]) == (4, 8)
    rows = P(AXES, None)
    heads = P(AXES, None, None, None)
    cols = P(None, AXES)
    trio = (rows, rows, cols)
    return jax.shard_map(
        functools.partial(body, remote),
        mesh=mesh,
        in_specs=(rows, heads, rows, rows, heads, *trio, *trio, *trio, P()),
        out_specs=(rows, heads, rows, heads, *trio, *trio, *trio, *trio, *trio, P()),
        check_vma=False,
    )
```
